256 devices in a mesh: row: 16 (over z_lo, y), col: 16 (over z_hi, x, core).
Axes of the slice: x: 4, y: 4, z: 8 (z_hi: 2, z_lo: 4; z = z_hi * 4 + z_lo), core: 2. Of those that a mesh axis runs over, the one named last changes fastest.
Arguments:
- object_field: float32 [2, 2048, 2048], P(None, 'row', 'col'), may hold values from -5 to 5
- probe: float32 [2, 2, 256, 256], replicated, may hold values from -5 to 5
- amplitudes: float32 [16, 16, 2, 256, 256], P('row', 'col'), may hold values from 0.2 to 2.5
- offsets: int32 [16, 16, 2, 2], P('row', 'col'), may hold values from -128 to 0
Outputs:
- object_out: float32 [2, 2048, 2048], P(None, 'row', 'col')
- probe_out: float32 [2, 2, 256, 256], replicated
The draws below stay inside these ranges and needn't reach their ends.
Inputs may be any that keep to these rules, and one draw needn't show every extreme that they name: `offsets`: each scan's 256 x 256 window starts at this offset from its own tile's anchor, so it reaches at most 128 pixels into neighbouring tiles.
All inputs are finite; a program needn't handle non-finite values.
Results may differ from the reference program's by a relative error of at most 0.0003.
Values sent between devices are 32-bit elements; how exact they have to be, the bound alone decides.
No kernel may reach another device: no remote copies, remote signals or barrier semaphores. Data moves between devices by JAX's collectives and lax.ppermute only.
A program may use at most 128 MiB of HBM per device.

```python
import jax
import jax.numpy as jnp
from jax import lax

PROBE = 256
HALF = 128
MODES = 2
SCANS = 2
TILE = 128
ITERS = 2
GRID_ROWS = 16
GRID_COLS = 16
NY = 2048
NX = 2048


def set_ends(values, stream_key, least, largest):
    longest = values.shape.index(max(values.shape))
    spots = []
    for shift in (0, 1):
        where = [jax.random.randint(jax.random.fold_in(stream_key, axis), (), 0, length) for axis, length in enumerate(values.shape)]
        where[longest] = (where[longest] + shift) % values.shape[longest]
        spots.append(tuple(where))
    return values.at[spots[0]].set(least).at[spots[1]].set(largest)


def levels(rng, extent, shards, least, top_value):
    def one(position, blocks):
        draws = jax.random.uniform(jax.random.fold_in(jax.random.fold_in(rng, 6), position), (blocks,), jnp.float32, least / len(shards), top_value / len(shards))
        return jnp.repeat(jnp.exp(draws), extent[position] // blocks).reshape((-1,) + (1,) * (len(extent) - position - 1))

    factor_of = one(*shards[0])
    for cut in shards[1:]:
        factor_of = factor_of * one(*cut)
    return factor_of


def centred(stream_key, shape, scale, most, shards=(), held_as=jnp.bfloat16):
    entries = scale * jax.random.normal(stream_key, shape, jnp.float32)
    if shards:
        entries = entries * levels(stream_key, shape, shards, -0.22, 0.18)
    return jnp.clip(entries, -most, most).astype(held_as)


def setup_inputs(seed: int = 0) -> dict:
    arg_keys = jax.random.split(jax.random.key(seed), 5)
    return {
        "object_field": centred(arg_keys[0], (2, NY, NX), 0.7, 5.0, ((1, 16), (2, 16)), jnp.float32),
        "probe": centred(arg_keys[1], (2, MODES, PROBE, PROBE), 0.7, 5.0, (), jnp.float32),
        "amplitudes": jnp.clip(0.2 + 2.3 * jax.random.uniform(arg_keys[2], (GRID_ROWS, GRID_COLS, SCANS, PROBE, PROBE), jnp.float32) ** levels(arg_keys[2], (GRID_ROWS, GRID_COLS, SCANS, PROBE, PROBE), ((0, 16), (1, 16)), -0.2, 0.2), 0.2, 2.5),
        "offsets": set_ends(jax.random.randint(arg_keys[3], (GRID_ROWS, GRID_COLS, SCANS, 2), -HALF, TILE - HALF + 1), jax.random.fold_in(arg_keys[3], 1), -HALF, TILE - HALF).astype(jnp.int32),
    }


FLOOR = 0.5
OBJECT_STEP = 0.5
OBJECT_REG = 0.5
PROBE_STEP = 1.0
PROBE_REG = 1.0

def reference(object_field, probe, amplitudes, offsets):
    rows_idx = lax.broadcasted_iota(jnp.int32, (GRID_ROWS, GRID_COLS, SCANS), 0)
    cols_idx = lax.broadcasted_iota(jnp.int32, (GRID_ROWS, GRID_COLS, SCANS), 1)
    row_starts = (rows_idx * TILE + offsets[..., 0] + HALF).reshape(-1).astype(jnp.int32)
    col_starts = (cols_idx * TILE + offsets[..., 1] + HALF).reshape(-1).astype(jnp.int32)
    measured = amplitudes.reshape(-1, PROBE, PROBE)
    zero_index = jnp.zeros((), jnp.int32)
    for iteration in range(ITERS):
        padded = jnp.pad(object_field, ((0, 0), (HALF, HALF), (HALF, HALF)))
        probe_wave = probe[0] + 1j * probe[1]
        probe_power = lax.optimization_barrier(jnp.sum(probe[0] * probe[0] + probe[1] * probe[1], axis=0))

        def visit_scan(state_in, record):
            grad_object, grad_probe, probe_weight = state_in
            row_start, col_start, amplitude = record
            corner = (zero_index, row_start.astype(jnp.int32), col_start.astype(jnp.int32))
            window = lax.dynamic_slice(padded, corner, (2, PROBE, PROBE))
            object_wave = window[0] + 1j * window[1]
            far_field = jnp.fft.fft2(probe_wave * object_wave[None], norm='ortho')
            intensity = lax.optimization_barrier(jnp.sum(far_field.real ** 2 + far_field.imag ** 2, axis=0))
            factor = amplitude / jnp.maximum(jnp.sqrt(intensity), FLOOR) - 1.0
            back_wave = jnp.fft.ifft2(far_field * factor[None], norm='ortho')
            obj_term = lax.optimization_barrier(jnp.sum(jnp.conj(probe_wave) * back_wave, axis=0))
            contrib = jnp.stack([obj_term.real, obj_term.imag, probe_power])
            current = lax.dynamic_slice(grad_object, corner, (3, PROBE, PROBE))
            grad_object = lax.dynamic_update_slice(grad_object, current + contrib, corner)
            probe_term = jnp.conj(object_wave)[None] * back_wave
            grad_probe = grad_probe + jnp.stack([probe_term.real, probe_term.imag])
            probe_weight = probe_weight + window[0] * window[0] + window[1] * window[1]
            return ((grad_object, grad_probe, probe_weight), None)
        start_state = (jnp.zeros((3, NY + 2 * HALF, NX + 2 * HALF), jnp.float32), jnp.zeros((2, MODES, PROBE, PROBE), jnp.float32), jnp.zeros((PROBE, PROBE), jnp.float32))
        (grad_object, grad_probe, probe_weight), _ = lax.scan(visit_scan, start_state, (row_starts, col_starts, measured))
        totals = grad_object[:, HALF:HALF + NY, HALF:HALF + NX]
        object_field = object_field + OBJECT_STEP * totals[0:2] / (totals[2:3] + OBJECT_REG)
        probe = probe + PROBE_STEP * grad_probe / (probe_weight + PROBE_REG)
    return (object_field, probe)
```

```python
import functools
import math

import jax
import jax.numpy as jnp
import ml_dtypes
import numpy as np
from jax import lax
from jax.experimental import pallas as pl
from jax.experimental.pallas import tpu as pltpu
from jax.sharding import PartitionSpec as P

ITERS = 2
FLOOR = 0.5
OBJECT_STEP = 0.5
OBJECT_REG = 0.5
PROBE_STEP = 1.0
PROBE_REG = 1.0
TILE = 128
SIDE = 256
HALF = SIDE // 2
WIDE = 3 * TILE
CHUNK = 64
F32 = jnp.float32
BF16 = jnp.bfloat16


def split_np(table):
    high = table.astype(np.float32).astype(ml_dtypes.bfloat16)
    low = (table - high.astype(np.float64)).astype(np.float32).astype(ml_dtypes.bfloat16)
    return np.stack([high, low])


def tables():
    out = []
    for parity in range(2):
        u = 2 * np.arange(HALF)[:, None] + parity
        angle = 2.0 * math.pi * ((u * np.arange(HALF)[None, :]) % SIDE) / SIDE
        cos, sin = np.cos(angle) / 16.0, np.sin(angle) / 16.0
        forward = np.block([[cos, sin], [-sin, cos]])
        out.append(np.stack([split_np(forward), split_np(forward.T)]))
    return np.stack(out)


def split(x):
    high = x.astype(BF16)
    return high, (x - high.astype(F32)).astype(BF16)


def split_whole(x):
    high = x.astype(BF16)
    rest = x - high.astype(F32)
    middle = rest.astype(BF16)
    return high, middle, (rest - middle.astype(F32)).astype(BF16)


def dot(a, b):
    return jnp.dot(a, b, preferred_element_type=F32)


def sort_kernel(measured_ref, out_ref):
    source = lax.broadcasted_iota(jnp.int32, (SIDE, SIDE), 0)
    place = lax.broadcasted_iota(jnp.int32, (SIDE, SIDE), 1)
    wanted = jnp.where(place < HALF, 2 * place, 2 * place - (SIDE - 1))
    select = jnp.where(source == wanted, 1.0, 0.0).astype(BF16)
    wanted = jnp.where(source < HALF, 2 * source, 2 * source - (SIDE - 1))
    select_rows = jnp.where(place == wanted, 1.0, 0.0).astype(BF16)
    for scan in range(2):
        high, middle, low = split_whole(measured_ref[scan])
        turned = (dot(low, select) + dot(middle, select)) + dot(high, select)
        high, middle, low = split_whole(turned)
        turned = (dot(select_rows, low) + dot(select_rows, middle)) + dot(select_rows, high)
        out_ref[scan, 0] = turned[:HALF]
        out_ref[scan, 1] = turned[HALF:]


def step_kernel(
    starts_ref,
    table_ref,
    probe_ref,
    measured_ref,
    left_ref,
    middle_ref,
    right_ref,
    probe_out,
    grad_left,
    grad_middle,
    grad_right,
    padded,
    windows,
    folded,
    stacked,
    far,
    back,
    contrib,
    total,
):
    lane = lax.broadcasted_iota(jnp.int32, (CHUNK // 8, 8, TILE), 2)
    sublane = lax.broadcasted_iota(jnp.int32, (CHUNK // 8, 8, TILE), 1)
    for channel in range(2):
        for block in range(3):
            rows = pl.ds(block * TILE, TILE)
            padded[channel, rows, 0:TILE] = left_ref[block, channel]
            padded[channel, rows, TILE : 2 * TILE] = middle_ref[block, channel]
            padded[channel, rows, 2 * TILE :] = right_ref[block, channel]
    for channel in range(3):
        total[channel] = jnp.zeros((WIDE + 8, WIDE), F32)

    def cut(scan, carry):
        row, column = starts_ref[scan, 0], starts_ref[scan, 1]
        inner = lax.rem(row, 8)
        base = pl.multiple_of(row - inner, 8)
        turn, keep = lax.rem(TILE - column, TILE), lane < TILE - column
        lift, stay = lax.rem(8 - inner, 8), sublane < 8 - inner
        for channel in range(2):
            for piece in range(SIDE // CHUNK):
                turned = []
                for b in range(3):
                    rows = padded[channel, pl.ds(base + piece * CHUNK, CHUNK + 8), pl.ds(b * TILE, TILE)]
                    rows = pltpu.roll(rows.reshape(CHUNK // 8 + 1, 8, TILE), lift, 1)
                    rows = jnp.where(stay, rows[:-1], rows[1:])
                    turned.append(pltpu.roll(rows, turn, 2))
                for b in range(2):
                    windows[scan, channel, pl.ds(piece * CHUNK, CHUNK), pl.ds(b * TILE, TILE)] = (
                        jnp.where(keep, turned[b], turned[b + 1]).reshape(CHUNK, TILE)
                    )
        return carry

    lax.fori_loop(0, 2, cut, 0)

    def forward(image, carry):
        scan, mode = image // 2, image % 2
        for piece in range(SIDE // CHUNK):
            rows = pl.ds(piece * CHUNK, CHUNK)
            p_re, p_im = probe_ref[0, mode, rows, :], probe_ref[1, mode, rows, :]
            w_re, w_im = windows[scan, 0, rows, :], windows[scan, 1, rows, :]
            e_re = p_re * w_re - p_im * w_im
            e_im = p_re * w_im + p_im * w_re
            for parity in range(2):
                sign = 1.0 if parity == 0 else -1.0
                for part, value in enumerate((e_re, e_im)):
                    half = value[:, :HALF] + sign * value[:, HALF:]
                    high, low = split(half)
                    folded[parity, 0, rows, part * HALF : (part + 1) * HALF] = high
                    folded[parity, 1, rows, part * HALF : (part + 1) * HALF] = low
        for parity in range(2):
            out = (
                dot(folded[parity, 1], table_ref[parity, 1, 0])
                + dot(folded[parity, 0], table_ref[parity, 1, 1])
                + dot(folded[parity, 0], table_ref[parity, 1, 0])
            )
            for other in range(2):
                sign = 1.0 if other == 0 else -1.0
                half = out[:HALF] + sign * out[HALF:]
                high, low = split(half)
                place = pl.ds(parity * HALF, HALF)
                stacked[other, 0, 0:HALF, place] = high[:, :HALF]
                stacked[other, 0, HALF:, place] = high[:, HALF:]
                stacked[other, 1, 0:HALF, place] = low[:, :HALF]
                stacked[other, 1, HALF:, place] = low[:, HALF:]
        for other in range(2):
            far[image, other] = (
                dot(table_ref[other, 0, 0], stacked[other, 1])
                + dot(table_ref[other, 0, 1], stacked[other, 0])
                + dot(table_ref[other, 0, 0], stacked[other, 0])
            )
        return carry

    lax.fori_loop(0, 4, forward, 0)

    def scale(index, carry):
        scan, other = index // 2, index % 2
        for piece in range(HALF // 32):
            upper, lower = pl.ds(piece * 32, 32), pl.ds(HALF + piece * 32, 32)
            parts = [
                far[2 * scan + mode, other, rows, :] for mode in range(2) for rows in (upper, lower)
            ]
            intensity = (parts[0] * parts[0] + parts[1] * parts[1]) + (
                parts[2] * parts[2] + parts[3] * parts[3]
            )
            measured = measured_ref[scan, other, upper, :]
            factor = measured / jnp.maximum(jnp.sqrt(intensity), FLOOR) - 1.0
            for mode in range(2):
                far[2 * scan + mode, other, upper, :] = parts[2 * mode] * factor
                far[2 * scan + mode, other, lower, :] = parts[2 * mode + 1] * factor
        return carry

    lax.fori_loop(0, 4, scale, 0)

    def backward(image, carry):
        scan, mode = image // 2, image % 2
        halves = []
        for other in range(2):
            high, low = split(far[image, other])
            halves.append(
                dot(table_ref[other, 1, 0], low)
                + dot(table_ref[other, 1, 1], high)
                + dot(table_ref[other, 1, 0], high)
            )
        for place, value in ((0, halves[0] + halves[1]), (HALF, halves[0] - halves[1])):
            high, low = split(value)
            for parity in range(2):
                columns = slice(parity * HALF, (parity + 1) * HALF)
                for part in range(2):
                    rows = slice(part * HALF, (part + 1) * HALF)
                    target = pl.ds(part * HALF, HALF)
                    folded[parity, 0, pl.ds(place, HALF), target] = high[rows, columns]
                    folded[parity, 1, pl.ds(place, HALF), target] = low[rows, columns]
        for parity in range(2):
            back[parity] = (
                dot(folded[parity, 1], table_ref[parity, 0, 0])
                + dot(folded[parity, 0], table_ref[parity, 0, 1])
                + dot(folded[parity, 0], table_ref[parity, 0, 0])
            )
        first_scan, first_mode = scan == 0, mode == 0
        for piece in range(SIDE // CHUNK):
            rows = pl.ds(piece * CHUNK, CHUNK)
            even, odd = back[0, rows, :], back[1, rows, :]
            for b in range(2):
                columns = pl.ds(b * HALF, HALF)
                sign = 1.0 if b == 0 else -1.0
                b_re = even[:, :HALF] + sign * odd[:, :HALF]
                b_im = even[:, HALF:] + sign * odd[:, HALF:]
                p_re, p_im = probe_ref[0, mode, rows, columns], probe_ref[1, mode, rows, columns]
                w_re, w_im = windows[scan, 0, rows, columns], windows[scan, 1, rows, columns]
                o_re = p_re * b_re + p_im * b_im
                o_im = p_re * b_im - p_im * b_re
                zero = jnp.zeros_like(o_re)
                contrib[0, rows, columns] = o_re + jnp.where(
                    first_mode, zero, contrib[0, rows, columns]
                )
                contrib[1, rows, columns] = o_im + jnp.where(
                    first_mode, zero, contrib[1, rows, columns]
                )
                g_re = w_re * b_re + w_im * b_im
                g_im = w_re * b_im - w_im * b_re
                for slot in range(CHUNK // 8):
                    group = piece * (CHUNK // 8) + slot
                    inner = slice(slot * 8, slot * 8 + 8)
                    for part, value in enumerate((g_re, g_im)):
                        place = 2 * part + mode
                        old = probe_out[group, place, :, columns]
                        probe_out[group, place, :, columns] = value[inner] + jnp.where(
                            first_scan, jnp.zeros_like(old), old
                        )

        @pl.when(mode == 1)
        def _():
            row, column = starts_ref[scan, 0], starts_ref[scan, 1]
            inner = lax.rem(row, 8)
            base = pl.multiple_of(row - inner, 8)
            turn, keep = lax.rem(column, TILE), lane >= column
            zero = jnp.zeros((CHUNK // 8, 8, TILE), F32)
            edge = jnp.zeros((1, 8, TILE), F32)
            stay = lax.broadcasted_iota(jnp.int32, (CHUNK // 8 + 1, 8, TILE), 1) >= inner
            for channel in range(3):
                for piece in range(SIDE // CHUNK):
                    halves = []
                    for b in range(2):
                        value = contrib[channel, pl.ds(piece * CHUNK, CHUNK), pl.ds(b * TILE, TILE)]
                        halves.append(pltpu.roll(value.reshape(CHUNK // 8, 8, TILE), turn, 2))
                    thirds = (
                        jnp.where(keep, halves[0], zero),
                        jnp.where(keep, halves[1], halves[0]),
                        jnp.where(keep, zero, halves[1]),
                    )
                    place = pl.ds(base + piece * CHUNK, CHUNK + 8)
                    for b in range(3):
                        value = pltpu.roll(thirds[b], inner, 1)
                        value = jnp.where(
                            stay,
                            jnp.concatenate([value, edge]),
                            jnp.concatenate([edge, value]),
                        )
                        total[channel, place, pl.ds(b * TILE, TILE)] += value.reshape(CHUNK + 8, TILE)

        return carry

    for piece in range(SIDE // CHUNK):
        rows = pl.ds(piece * CHUNK, CHUNK)
        power = None
        for mode in range(2):
            for part in range(2):
                value = probe_ref[part, mode, rows, :]
                power = value * value if power is None else power + value * value
        contrib[2, rows, :] = power
        weight = None
        for scan in range(2):
            for part in range(2):
                value = windows[scan, part, rows, :]
                weight = value * value if weight is None else weight + value * value
        for slot in range(CHUNK // 8):
            probe_out[piece * (CHUNK // 8) + slot, 4] = weight[slot * 8 : slot * 8 + 8]

    lax.fori_loop(0, 4, backward, 0)

    for channel in range(3):
        for block in range(3):
            rows = pl.ds(block * TILE, TILE)
            grad_left[block, channel] = total[channel, rows, 0:TILE]
            grad_middle[block, channel] = total[channel, rows, TILE : 2 * TILE]
            grad_right[block, channel] = total[channel, rows, 2 * TILE :]


VMEM_SPEC = pl.BlockSpec(memory_space=pltpu.VMEM)


def sort_measured(measured):
    return pl.pallas_call(
        sort_kernel,
        out_shape=jax.ShapeDtypeStruct((2, 2, HALF, SIDE), F32),
        in_specs=[VMEM_SPEC],
        out_specs=VMEM_SPEC,
        compiler_params=pltpu.CompilerParams(vmem_limit_bytes=40 * 2**20),
        name="sort_measured",
    )(measured)


def step(starts, table, probe, measured, left, middle, right):
    column = jax.ShapeDtypeStruct((3, 3, TILE, TILE), F32)
    return pl.pallas_call(
        step_kernel,
        out_shape=[jax.ShapeDtypeStruct((SIDE // 8, 5, 8, SIDE), F32), column, column, column],
        in_specs=[pl.BlockSpec(memory_space=pltpu.SMEM)] + [VMEM_SPEC] * 6,
        out_specs=[VMEM_SPEC] * 4,
        scratch_shapes=[
            pltpu.VMEM((2, WIDE + 8, WIDE), F32),
            pltpu.VMEM((2, 2, SIDE, SIDE), F32),
            pltpu.VMEM((2, 2, SIDE, SIDE), BF16),
            pltpu.VMEM((2, 2, SIDE, SIDE), BF16),
            pltpu.VMEM((4, 2, SIDE, SIDE), F32),
            pltpu.VMEM((2, SIDE, SIDE), F32),
            pltpu.VMEM((3, SIDE, SIDE), F32),
            pltpu.VMEM((3, WIDE + 8, WIDE), F32),
        ],
        compiler_params=pltpu.CompilerParams(vmem_limit_bytes=40 * 2**20),
        name="step",
    )(starts, table, probe, measured, left, middle, right)


def up(axis):
    return [(i, i + 1) for i in range(lax.axis_size(axis) - 1)]


def down(axis):
    return [(i + 1, i) for i in range(lax.axis_size(axis) - 1)]


def neighbourhood(tile):
    above = lax.ppermute(tile, "row", up("row"))
    below = lax.ppermute(tile, "row", down("row"))
    middle = jnp.stack([above, tile, below])
    left = lax.ppermute(middle, "col", up("col"))
    right = lax.ppermute(middle, "col", down("col"))
    return left, middle, right


def fold(left, middle, right):
    column = middle + lax.ppermute(left, "col", down("col")) + lax.ppermute(right, "col", up("col"))
    return (
        column[1]
        + lax.ppermute(column[0], "row", down("row"))
        + lax.ppermute(column[2], "row", up("row"))
    )


def scatter_sum(value, axis, count, groups=None):
    pieces = lax.all_to_all(value, axis, 0, 0, axis_index_groups=groups, tiled=True)
    return pieces.reshape((count, value.shape[0] // count) + value.shape[1:]).sum(0)


def gather(value, axis, count, groups=None):
    copies = jnp.broadcast_to(value[None], (count,) + value.shape)
    copies = copies.reshape((count * value.shape[0],) + value.shape[1:])
    return lax.all_to_all(copies, axis, 0, 0, axis_index_groups=groups, tiled=True)


def new_probe(sums, probe_rows):
    core = lax.axis_index("col") % 2
    swap = [(i, i ^ 1) for i in range(16)]
    groups = [[2 * i + c for i in range(8)] for c in range(2)]
    halves = sums.reshape((2, 16) + sums.shape[1:])
    mine = lax.dynamic_index_in_dim(halves, core, 0, False)
    other = lax.dynamic_index_in_dim(halves, 1 - core, 0, False)
    mine = mine + lax.ppermute(other, "col", swap)
    mine = scatter_sum(mine, "row", 16)
    mine = gather(mine, "col", 8, groups).sum(0, keepdims=True)
    place = core * 16 + lax.axis_index("row")
    old = lax.dynamic_slice_in_dim(probe_rows, place, 1, 0)
    mine = old + PROBE_STEP * mine[:, :4] / (mine[:, 4:] + PROBE_REG)
    mine = gather(mine, "row", 16)
    other = lax.ppermute(mine, "col", swap)
    return jnp.where(
        core == 0, jnp.concatenate([mine, other]), jnp.concatenate([other, mine])
    )


def local(object_field, probe, amplitudes, offsets):
    table = jnp.asarray(tables())
    starts = offsets[0, 0] + HALF
    measured = sort_measured(amplitudes[0, 0])
    for iteration in range(ITERS):
        left, middle, right = neighbourhood(object_field)
        sums, grad_left, grad_middle, grad_right = step(
            starts, table, probe, measured, left, middle, right
        )
        rows = probe.reshape(4, SIDE // 8, 8, SIDE).transpose(1, 0, 2, 3)
        rows = new_probe(sums, rows)
        totals = fold(grad_left, grad_middle, grad_right)
        object_field = object_field + OBJECT_STEP * totals[0:2] / (totals[2:3] + OBJECT_REG)
        probe = rows.transpose(1, 0, 2, 3).reshape(2, 2, SIDE, SIDE)
    return (object_field, probe)


def solution(mesh):
    return jax.shard_map(
        local,
        mesh=mesh,
        in_specs=(
            P(None, "row", "col"),
            P(),
            P("row", "col", None, None, None),
            P("row", "col", None, None),
        ),
        out_specs=(P(None, "row", "col"), P()),
        check_vma=False,
    )
```

```python
import functools
import math

import jax
import jax.numpy as jnp
import ml_dtypes
import numpy as np
from jax import lax
from jax.experimental import pallas as pl
from jax.experimental.pallas import tpu as pltpu
from jax.sharding import PartitionSpec as P

ITERS = 2
FLOOR = 0.5
OBJECT_STEP = 0.5
OBJECT_REG = 0.5
PROBE_STEP = 1.0
PROBE_REG = 1.0
TILE = 128
SIDE = 256
HALF = SIDE // 2
WIDE = 3 * TILE
CHUNK = 64
GROUPS = 16
DEPTH = 8
F32 = jnp.float32
BF16 = jnp.bfloat16


def split_np(table):
    high = table.astype(np.float32).astype(ml_dtypes.bfloat16)
    low = (table - high.astype(np.float64)).astype(np.float32).astype(ml_dtypes.bfloat16)
    return np.stack([high, low])


def tables():
    out = []
    for parity in range(2):
        u = 2 * np.arange(HALF)[:, None] + parity
        angle = 2.0 * math.pi * ((u * np.arange(HALF)[None, :]) % SIDE) / SIDE
        cos, sin = np.cos(angle) / 16.0, np.sin(angle) / 16.0
        forward = np.block([[cos, sin], [-sin, cos]])
        out.append(np.stack([split_np(forward), split_np(forward.T)]))
    return np.stack(out)


def split(x):
    high = x.astype(BF16)
    return high, (x - high.astype(F32)).astype(BF16)


def split_whole(x):
    high = x.astype(BF16)
    rest = x - high.astype(F32)
    middle = rest.astype(BF16)
    return high, middle, (rest - middle.astype(F32)).astype(BF16)


def dot(a, b):
    return jnp.dot(a, b, preferred_element_type=F32)


def sort_kernel(measured_ref, out_ref):
    source = lax.broadcasted_iota(jnp.int32, (SIDE, SIDE), 0)
    place = lax.broadcasted_iota(jnp.int32, (SIDE, SIDE), 1)
    wanted = jnp.where(place < HALF, 2 * place, 2 * place - (SIDE - 1))
    select = jnp.where(source == wanted, 1.0, 0.0).astype(BF16)
    wanted = jnp.where(source < HALF, 2 * source, 2 * source - (SIDE - 1))
    select_rows = jnp.where(place == wanted, 1.0, 0.0).astype(BF16)
    for scan in range(2):
        high, middle, low = split_whole(measured_ref[scan])
        turned = (dot(low, select) + dot(middle, select)) + dot(high, select)
        high, middle, low = split_whole(turned)
        turned = (dot(select_rows, low) + dot(select_rows, middle)) + dot(select_rows, high)
        out_ref[scan, 0] = turned[:HALF]
        out_ref[scan, 1] = turned[HALF:]


def lay_out_kernel(core_ref, mine_ref, other_ref, out_ref):
    for half, ref in enumerate((mine_ref, other_ref)):
        place = core_ref[0] if half == 0 else 1 - core_ref[0]
        for part in range(4):
            out_ref[part, pl.ds(place * GROUPS, GROUPS)] = ref[:, part]


def step_kernel(halves, offsets_ref, core_ref, table_in, *refs):
    probe_in, refs = refs[: 1 + halves], refs[1 + halves :]
    (
        measured_in,
        left_in,
        tile_in,
        right_in,
        above_in,
        below_in,
        mine_out,
        other_out,
        grad_above,
        grad_middle,
        grad_below,
        table_ref,
        probe,
        measured_ref,
        padded,
        windows,
        folded,
        stacked,
        far,
        back,
        contrib,
        total,
        sums,
        semaphores,
    ) = refs
    core = core_ref[0]
    copies = []

    def start(source, target):
        copy = pltpu.make_async_copy(source, target, semaphores.at[len(copies)])
        copy.start()
        copies.append(copy)

    def third(block):
        return pl.ds(block * TILE, TILE)

    for block, piece in enumerate((left_in, tile_in, right_in)):
        start(piece, padded.at[:, third(1), third(block)])
        start(above_in.at[block], padded.at[:, third(0), third(block)])
        start(below_in.at[block], padded.at[:, third(2), third(block)])
    near = len(copies)
    if halves:
        for half, ref in enumerate(probe_in):
            place = core if half == 0 else 1 - core
            for part in range(4):
                start(ref.at[:, part], probe.at[part, pl.ds(place * GROUPS, GROUPS)])
    else:
        start(probe_in[0], probe)
    start(table_in, table_ref)
    operands = len(copies)
    start(measured_in, measured_ref)

    def probe_rows(part, mode, piece, columns=slice(None)):
        groups = pl.ds(piece * (CHUNK // 8), CHUNK // 8)
        value = probe[2 * part + mode, groups, :, columns]
        return value.reshape(CHUNK, value.shape[-1])

    lane = lax.broadcasted_iota(jnp.int32, (CHUNK // 8, 8, TILE), 2)
    sublane = lax.broadcasted_iota(jnp.int32, (CHUNK // 8, 8, TILE), 1)
    for channel in range(3):
        total[channel] = jnp.zeros((WIDE + 8, WIDE), F32)
    for copy in copies[:near]:
        copy.wait()

    def cut(scan, carry):
        row, column = offsets_ref[0, 0, scan, 0] + HALF, offsets_ref[0, 0, scan, 1] + HALF
        inner = lax.rem(row, 8)
        base = pl.multiple_of(row - inner, 8)
        turn, keep = lax.rem(TILE - column, TILE), lane < TILE - column
        lift, stay = lax.rem(8 - inner, 8), sublane < 8 - inner
        for channel in range(2):
            for piece in range(SIDE // CHUNK):
                turned = []
                for b in range(3):
                    rows = padded[channel, pl.ds(base + piece * CHUNK, CHUNK + 8), pl.ds(b * TILE, TILE)]
                    rows = pltpu.roll(rows.reshape(CHUNK // 8 + 1, 8, TILE), lift, 1)
                    rows = jnp.where(stay, rows[:-1], rows[1:])
                    turned.append(pltpu.roll(rows, turn, 2))
                for b in range(2):
                    windows[scan, channel, pl.ds(piece * CHUNK, CHUNK), pl.ds(b * TILE, TILE)] = (
                        jnp.where(keep, turned[b], turned[b + 1]).reshape(CHUNK, TILE)
                    )
        return carry

    lax.fori_loop(0, 2, cut, 0)
    for copy in copies[near:operands]:
        copy.wait()

    def forward(image, carry):
        scan, mode = image // 2, image % 2
        for piece in range(SIDE // CHUNK):
            rows = pl.ds(piece * CHUNK, CHUNK)
            p_re, p_im = probe_rows(0, mode, piece), probe_rows(1, mode, piece)
            w_re, w_im = windows[scan, 0, rows, :], windows[scan, 1, rows, :]
            e_re = p_re * w_re - p_im * w_im
            e_im = p_re * w_im + p_im * w_re
            for parity in range(2):
                sign = 1.0 if parity == 0 else -1.0
                for part, value in enumerate((e_re, e_im)):
                    half = value[:, :HALF] + sign * value[:, HALF:]
                    high, low = split(half)
                    folded[parity, 0, rows, part * HALF : (part + 1) * HALF] = high
                    folded[parity, 1, rows, part * HALF : (part + 1) * HALF] = low
        for parity in range(2):
            out = (
                dot(folded[parity, 1], table_ref[parity, 1, 0])
                + dot(folded[parity, 0], table_ref[parity, 1, 1])
                + dot(folded[parity, 0], table_ref[parity, 1, 0])
            )
            for other in range(2):
                sign = 1.0 if other == 0 else -1.0
                half = out[:HALF] + sign * out[HALF:]
                high, low = split(half)
                place = pl.ds(parity * HALF, HALF)
                stacked[other, 0, 0:HALF, place] = high[:, :HALF]
                stacked[other, 0, HALF:, place] = high[:, HALF:]
                stacked[other, 1, 0:HALF, place] = low[:, :HALF]
                stacked[other, 1, HALF:, place] = low[:, HALF:]
        for other in range(2):
            far[image, other] = (
                dot(table_ref[other, 0, 0], stacked[other, 1])
                + dot(table_ref[other, 0, 1], stacked[other, 0])
                + dot(table_ref[other, 0, 0], stacked[other, 0])
            )
        return carry

    lax.fori_loop(0, 4, forward, 0)

    def scale(index, carry):
        scan, other = index // 2, index % 2
        for piece in range(HALF // 32):
            upper, lower = pl.ds(piece * 32, 32), pl.ds(HALF + piece * 32, 32)
            parts = [
                far[2 * scan + mode, other, rows, :] for mode in range(2) for rows in (upper, lower)
            ]
            intensity = (parts[0] * parts[0] + parts[1] * parts[1]) + (
                parts[2] * parts[2] + parts[3] * parts[3]
            )
            measured = measured_ref[scan, other, upper, :]
            factor = measured / jnp.maximum(jnp.sqrt(intensity), FLOOR) - 1.0
            for mode in range(2):
                far[2 * scan + mode, other, upper, :] = parts[2 * mode] * factor
                far[2 * scan + mode, other, lower, :] = parts[2 * mode + 1] * factor
        return carry

    copies[operands].wait()
    lax.fori_loop(0, 4, scale, 0)

    def backward(image, carry):
        scan, mode = image // 2, image % 2
        halves = []
        for other in range(2):
            high, low = split(far[image, other])
            halves.append(
                dot(table_ref[other, 1, 0], low)
                + dot(table_ref[other, 1, 1], high)
                + dot(table_ref[other, 1, 0], high)
            )
        for place, value in ((0, halves[0] + halves[1]), (HALF, halves[0] - halves[1])):
            high, low = split(value)
            for parity in range(2):
                columns = slice(parity * HALF, (parity + 1) * HALF)
                for part in range(2):
                    rows = slice(part * HALF, (part + 1) * HALF)
                    target = pl.ds(part * HALF, HALF)
                    folded[parity, 0, pl.ds(place, HALF), target] = high[rows, columns]
                    folded[parity, 1, pl.ds(place, HALF), target] = low[rows, columns]
        for parity in range(2):
            back[parity] = (
                dot(folded[parity, 1], table_ref[parity, 0, 0])
                + dot(folded[parity, 0], table_ref[parity, 0, 1])
                + dot(folded[parity, 0], table_ref[parity, 0, 0])
            )
        first_scan, first_mode = scan == 0, mode == 0
        for piece in range(SIDE // CHUNK):
            rows = pl.ds(piece * CHUNK, CHUNK)
            even, odd = back[0, rows, :], back[1, rows, :]
            for b in range(2):
                columns = pl.ds(b * HALF, HALF)
                sign = 1.0 if b == 0 else -1.0
                b_re = even[:, :HALF] + sign * odd[:, :HALF]
                b_im = even[:, HALF:] + sign * odd[:, HALF:]
                p_re = probe_rows(0, mode, piece, columns)
                p_im = probe_rows(1, mode, piece, columns)
                w_re, w_im = windows[scan, 0, rows, columns], windows[scan, 1, rows, columns]
                o_re = p_re * b_re + p_im * b_im
                o_im = p_re * b_im - p_im * b_re
                zero = jnp.zeros_like(o_re)
                contrib[0, rows, columns] = o_re + jnp.where(
                    first_mode, zero, contrib[0, rows, columns]
                )
                contrib[1, rows, columns] = o_im + jnp.where(
                    first_mode, zero, contrib[1, rows, columns]
                )
                g_re = w_re * b_re + w_im * b_im
                g_im = w_re * b_im - w_im * b_re
                for slot in range(CHUNK // 8):
                    group = piece * (CHUNK // 8) + slot
                    inner = slice(slot * 8, slot * 8 + 8)
                    for part, value in enumerate((g_re, g_im)):
                        place = 2 * part + mode
                        old = sums[group, place, :, columns]
                        sums[group, place, :, columns] = value[inner] + jnp.where(
                            first_scan, jnp.zeros_like(old), old
                        )

        @pl.when(mode == 1)
        def _():
            row, column = offsets_ref[0, 0, scan, 0] + HALF, offsets_ref[0, 0, scan, 1] + HALF
            inner = lax.rem(row, 8)
            base = pl.multiple_of(row - inner, 8)
            turn, keep = lax.rem(column, TILE), lane >= column
            zero = jnp.zeros((CHUNK // 8, 8, TILE), F32)
            edge = jnp.zeros((1, 8, TILE), F32)
            stay = lax.broadcasted_iota(jnp.int32, (CHUNK // 8 + 1, 8, TILE), 1) >= inner
            for channel in range(3):
                for piece in range(SIDE // CHUNK):
                    halves = []
                    for b in range(2):
                        value = contrib[channel, pl.ds(piece * CHUNK, CHUNK), pl.ds(b * TILE, TILE)]
                        halves.append(pltpu.roll(value.reshape(CHUNK // 8, 8, TILE), turn, 2))
                    thirds = (
                        jnp.where(keep, halves[0], zero),
                        jnp.where(keep, halves[1], halves[0]),
                        jnp.where(keep, zero, halves[1]),
                    )
                    place = pl.ds(base + piece * CHUNK, CHUNK + 8)
                    for b in range(3):
                        value = pltpu.roll(thirds[b], inner, 1)
                        value = jnp.where(
                            stay,
                            jnp.concatenate([value, edge]),
                            jnp.concatenate([edge, value]),
                        )
                        total[channel, place, pl.ds(b * TILE, TILE)] += value.reshape(CHUNK + 8, TILE)

        return carry

    for piece in range(SIDE // CHUNK):
        rows = pl.ds(piece * CHUNK, CHUNK)
        power = None
        for mode in range(2):
            for part in range(2):
                value = probe_rows(part, mode, piece)
                power = value * value if power is None else power + value * value
        contrib[2, rows, :] = power
        weight = None
        for scan in range(2):
            for part in range(2):
                value = windows[scan, part, rows, :]
                weight = value * value if weight is None else weight + value * value
        for slot in range(CHUNK // 8):
            sums[piece * (CHUNK // 8) + slot, 4] = weight[slot * 8 : slot * 8 + 8]

    lax.fori_loop(0, 4, backward, 0)

    done = len(copies)
    for block, ref in enumerate((grad_above, grad_middle, grad_below)):
        for column in range(3):
            start(total.at[:, third(block), third(column)], ref.at[column])
    start(sums.at[pl.ds(core * GROUPS, GROUPS)], mine_out)
    start(sums.at[pl.ds((1 - core) * GROUPS, GROUPS)], other_out)
    for copy in copies[done:]:
        copy.wait()


def spread_kernel(pieces_ref, out_ref):
    total = pieces_ref[0]
    for piece in range(1, GROUPS):
        total = total + pieces_ref[piece]
    for copy in range(DEPTH):
        out_ref[copy] = total


def update_kernel(pieces_ref, old_ref, out_ref, new_ref):
    total = pieces_ref[0]
    for piece in range(1, DEPTH):
        total = total + pieces_ref[piece]
    new = old_ref[...] + PROBE_STEP * total[:4] / (total[4:] + PROBE_REG)
    new_ref[...] = new
    for copy in range(GROUPS):
        out_ref[copy] = new


VMEM_SPEC = pl.BlockSpec(memory_space=pltpu.VMEM)
SMEM_SPEC = pl.BlockSpec(memory_space=pltpu.SMEM)
ANY_SPEC = pl.BlockSpec(memory_space=pl.ANY)


def in_hbm(value):
    return pltpu.with_memory_space_constraint(value, pltpu.HBM)


def params(mebibytes):
    return pltpu.CompilerParams(vmem_limit_bytes=mebibytes * 2**20)


def sort_measured(measured):
    return pl.pallas_call(
        sort_kernel,
        out_shape=jax.ShapeDtypeStruct((2, 2, HALF, SIDE), F32),
        in_specs=[VMEM_SPEC],
        out_specs=VMEM_SPEC,
        compiler_params=params(8),
        name="sort_measured",
    )(measured)


def step(offsets, core, table, probe, measured, around):
    halves = len(probe) - 1
    band = jax.ShapeDtypeStruct((3, 3, TILE, TILE), F32)
    half = jax.ShapeDtypeStruct((GROUPS, 5, 8, SIDE), F32)
    return pl.pallas_call(
        functools.partial(step_kernel, halves),
        out_shape=[half, half, band, band, band],
        in_specs=[SMEM_SPEC, SMEM_SPEC] + [ANY_SPEC] * (8 + halves),
        out_specs=[ANY_SPEC] * 5,
        scratch_shapes=[
            pltpu.VMEM(table.shape, BF16),
            pltpu.VMEM((4, 2 * GROUPS, 8, SIDE), F32),
            pltpu.VMEM(measured.shape, F32),
            pltpu.VMEM((2, WIDE + 8, WIDE), F32),
            pltpu.VMEM((2, 2, SIDE, SIDE), F32),
            pltpu.VMEM((2, 2, SIDE, SIDE), BF16),
            pltpu.VMEM((2, 2, SIDE, SIDE), BF16),
            pltpu.VMEM((4, 2, SIDE, SIDE), F32),
            pltpu.VMEM((2, SIDE, SIDE), F32),
            pltpu.VMEM((3, SIDE, SIDE), F32),
            pltpu.VMEM((3, WIDE + 8, WIDE), F32),
            pltpu.VMEM((2 * GROUPS, 5, 8, SIDE), F32),
            pltpu.SemaphoreType.DMA((32,)),
        ],
        compiler_params=params(20),
        name="step",
    )(offsets, core, table, *probe, measured, *around)


def up(axis):
    return [(i, i + 1) for i in range(lax.axis_size(axis) - 1)]


def down(axis):
    return [(i + 1, i) for i in range(lax.axis_size(axis) - 1)]


def neighbourhood(tile):
    left = lax.ppermute(tile, "col", up("col"))
    right = lax.ppermute(tile, "col", down("col"))
    band = jnp.stack([left, tile, right])
    above = lax.ppermute(band, "row", up("row"))
    below = lax.ppermute(band, "row", down("row"))
    return left, tile, right, above, below


def fold(above, middle, below):
    above = lax.ppermute(above, "row", down("row"))
    below = lax.ppermute(below, "row", up("row"))
    first, own, last = (middle[i] + above[i] + below[i] for i in range(3))
    first = lax.ppermute(first, "col", down("col"))
    last = lax.ppermute(last, "col", up("col"))
    return own + first + last


def places(device):
    row, column = divmod(device, 16)
    return (column // 8) * 4 + row // 4, row % 4, column // 2 % 4, column % 2


def grouped(key):
    groups = {}
    for device in range(256):
        groups.setdefault(key(*places(device)), []).append(device)
    return list(groups.values())


PLANES = grouped(lambda z, y, x, core: (z, core))
LINES = grouped(lambda z, y, x, core: (y, x, core))
BOTH = ("row", "col")
SWAP = [(i, i ^ 1) for i in range(16)]


def exchange(value, groups):
    return lax.all_to_all(value, BOTH, 0, 0, axis_index_groups=groups, tiled=True)


def new_probe(mine, other, old):
    mine = mine + lax.ppermute(other, "col", SWAP)
    pieces = exchange(mine, PLANES)
    pieces = pl.pallas_call(
        spread_kernel,
        out_shape=jax.ShapeDtypeStruct((DEPTH, 5, 8, SIDE), F32),
        compiler_params=params(8),
        name="spread",
    )(pieces)
    pieces = exchange(pieces, LINES)
    pieces, new = pl.pallas_call(
        update_kernel,
        out_shape=[
            jax.ShapeDtypeStruct((GROUPS, 4, 8, SIDE), F32),
            jax.ShapeDtypeStruct((4, 8, SIDE), F32),
        ],
        compiler_params=params(8),
        name="update",
    )(pieces, old)
    mine = exchange(pieces, PLANES)
    other = lax.ppermute(mine, "col", SWAP)
    return mine, other, new


def local(object_field, probe, amplitudes, offsets):
    table = in_hbm(jnp.asarray(tables()))
    row, column = lax.axis_index("row"), lax.axis_index("col")
    core = column & 1
    group = core * GROUPS + (row & 3) * 4 + (lax.shift_right_logical(column, 1) & 3)
    probe = probe.reshape(4, 2 * GROUPS, 8, SIDE)
    old = lax.dynamic_index_in_dim(probe, group, 1, False)
    core = core.reshape(1)
    measured = sort_measured(amplitudes[0, 0])
    parts = (in_hbm(probe),)
    for iteration in range(ITERS):
        mine, other, above, middle, below = step(
            offsets, core, table, parts, measured, neighbourhood(object_field)
        )
        mine, other, old = new_probe(mine, other, old)
        parts = (mine, other)
        totals = fold(above, middle, below)
        object_field = object_field + OBJECT_STEP * totals[0:2] / (totals[2:3] + OBJECT_REG)
    probe = pl.pallas_call(
        lay_out_kernel,
        out_shape=jax.ShapeDtypeStruct((4, 2 * GROUPS, 8, SIDE), F32),
        in_specs=[SMEM_SPEC, VMEM_SPEC, VMEM_SPEC],
        out_specs=VMEM_SPEC,
        compiler_params=params(8),
        name="lay_out",
    )(core, *parts)
    return (object_field, probe.reshape(2, 2, SIDE, SIDE))


def solution(mesh):
    return jax.shard_map(
        local,
        mesh=mesh,
        in_specs=(
            P(None, "row", "col"),
            P(),
            P("row", "col", None, None, None),
            P("row", "col", None, None),
        ),
        out_specs=(P(None, "row", "col"), P()),
        check_vma=False,
    )
```

```python
import functools
import math

import jax
import jax.numpy as jnp
import ml_dtypes
import numpy as np
from jax import lax
from jax.experimental import pallas as pl
from jax.experimental.pallas import tpu as pltpu
from jax.sharding import PartitionSpec as P

ITERS = 2
FLOOR = 0.5
OBJECT_STEP = 0.5
OBJECT_REG = 0.5
PROBE_STEP = 1.0
PROBE_REG = 1.0
TILE = 128
SIDE = 256
HALF = SIDE // 2
WIDE = 3 * TILE
CHUNK = 64
GROUPS = 16
DEPTH = 8
F32 = jnp.float32
BF16 = jnp.bfloat16


def split_np(table):
    high = table.astype(np.float32).astype(ml_dtypes.bfloat16)
    low = (table - high.astype(np.float64)).astype(np.float32).astype(ml_dtypes.bfloat16)
    return np.stack([high, low])


def tables():
    out = []
    for parity in range(2):
        u = 2 * np.arange(HALF)[:, None] + parity
        angle = 2.0 * math.pi * ((u * np.arange(HALF)[None, :]) % SIDE) / SIDE
        cos, sin = np.cos(angle) / 16.0, np.sin(angle) / 16.0
        forward = np.block([[cos, sin], [-sin, cos]])
        out.append(np.stack([split_np(forward), split_np(forward.T)]))
    return np.stack(out)


def split(x):
    high = x.astype(BF16)
    return high, (x - high.astype(F32)).astype(BF16)


def split_whole(x):
    high = x.astype(BF16)
    rest = x - high.astype(F32)
    middle = rest.astype(BF16)
    return high, middle, (rest - middle.astype(F32)).astype(BF16)


def dot(a, b):
    return jnp.dot(a, b, preferred_element_type=F32)


def sort_kernel(measured_ref, out_ref):
    source = lax.broadcasted_iota(jnp.int32, (SIDE, SIDE), 0)
    place = lax.broadcasted_iota(jnp.int32, (SIDE, SIDE), 1)
    wanted = jnp.where(place < HALF, 2 * place, 2 * place - (SIDE - 1))
    select = jnp.where(source == wanted, 1.0, 0.0).astype(BF16)
    wanted = jnp.where(source < HALF, 2 * source, 2 * source - (SIDE - 1))
    select_rows = jnp.where(place == wanted, 1.0, 0.0).astype(BF16)
    for scan in range(2):
        high, middle, low = split_whole(measured_ref[scan])
        turned = (dot(low, select) + dot(middle, select)) + dot(high, select)
        high, middle, low = split_whole(turned)
        turned = (dot(select_rows, low) + dot(select_rows, middle)) + dot(select_rows, high)
        out_ref[scan, 0] = turned[:HALF]
        out_ref[scan, 1] = turned[HALF:]


def lay_out_kernel(core_ref, mine_ref, other_ref, out_ref):
    for half, ref in enumerate((mine_ref, other_ref)):
        place = core_ref[0] if half == 0 else 1 - core_ref[0]
        for part in range(4):
            out_ref[part, pl.ds(place * GROUPS, GROUPS)] = ref[:, part]


def step_kernel(halves, offsets_ref, core_ref, table_in, *refs):
    probe_in, refs = refs[: 1 + halves], refs[1 + halves :]
    (
        measured_in,
        left_in,
        tile_in,
        right_in,
        above_in,
        below_in,
        mine_out,
        other_out,
        grad_above,
        grad_middle,
        grad_below,
        table_ref,
        probe,
        measured_ref,
        padded,
        windows,
        folded,
        stacked,
        far,
        back,
        contrib,
        total,
        sums,
        semaphores,
    ) = refs
    core = core_ref[0]
    copies = []

    def start(source, target):
        copy = pltpu.make_async_copy(source, target, semaphores.at[len(copies)])
        copy.start()
        copies.append(copy)

    def third(block):
        return pl.ds(block * TILE, TILE)

    for block, piece in enumerate((left_in, tile_in, right_in)):
        start(piece, padded.at[:, third(1), third(block)])
        start(above_in.at[block], padded.at[:, third(0), third(block)])
        start(below_in.at[block], padded.at[:, third(2), third(block)])
    near = len(copies)
    if halves:
        for half, ref in enumerate(probe_in):
            place = core if half == 0 else 1 - core
            for part in range(4):
                start(ref.at[:, part], probe.at[part, pl.ds(place * GROUPS, GROUPS)])
    else:
        start(probe_in[0], probe)
    start(table_in, table_ref)
    operands = len(copies)
    start(measured_in, measured_ref)

    def probe_rows(part, mode, piece, columns=slice(None)):
        groups = pl.ds(piece * (CHUNK // 8), CHUNK // 8)
        value = probe[2 * part + mode, groups, :, columns]
        return value.reshape(CHUNK, value.shape[-1])

    lane = lax.broadcasted_iota(jnp.int32, (CHUNK // 8, 8, TILE), 2)
    sublane = lax.broadcasted_iota(jnp.int32, (CHUNK // 8, 8, TILE), 1)
    for channel in range(3):
        total[channel] = jnp.zeros((WIDE + 8, WIDE), F32)
    for copy in copies[:near]:
        copy.wait()

    def cut(scan, carry):
        row, column = offsets_ref[0, 0, scan, 0] + HALF, offsets_ref[0, 0, scan, 1] + HALF
        inner = lax.rem(row, 8)
        base = pl.multiple_of(row - inner, 8)
        turn, keep = lax.rem(TILE - column, TILE), lane < TILE - column
        lift, stay = lax.rem(8 - inner, 8), sublane < 8 - inner
        for channel in range(2):
            for piece in range(SIDE // CHUNK):
                turned = []
                for b in range(3):
                    rows = padded[channel, pl.ds(base + piece * CHUNK, CHUNK + 8), pl.ds(b * TILE, TILE)]
                    rows = pltpu.roll(rows.reshape(CHUNK // 8 + 1, 8, TILE), lift, 1)
                    rows = jnp.where(stay, rows[:-1], rows[1:])
                    turned.append(pltpu.roll(rows, turn, 2))
                for b in range(2):
                    windows[scan, channel, pl.ds(piece * CHUNK, CHUNK), pl.ds(b * TILE, TILE)] = (
                        jnp.where(keep, turned[b], turned[b + 1]).reshape(CHUNK, TILE)
                    )
        return carry

    lax.fori_loop(0, 2, cut, 0)
    for copy in copies[near:operands]:
        copy.wait()

    def forward(image, carry):
        scan, mode = image // 2, image % 2
        for piece in range(SIDE // CHUNK):
            rows = pl.ds(piece * CHUNK, CHUNK)
            p_re, p_im = probe_rows(0, mode, piece), probe_rows(1, mode, piece)
            w_re, w_im = windows[scan, 0, rows, :], windows[scan, 1, rows, :]
            e_re = p_re * w_re - p_im * w_im
            e_im = p_re * w_im + p_im * w_re
            for parity in range(2):
                sign = 1.0 if parity == 0 else -1.0
                for part, value in enumerate((e_re, e_im)):
                    half = value[:, :HALF] + sign * value[:, HALF:]
                    high, low = split(half)
                    folded[parity, 0, rows, part * HALF : (part + 1) * HALF] = high
                    folded[parity, 1, rows, part * HALF : (part + 1) * HALF] = low
        for parity in range(2):
            out = (
                dot(folded[parity, 1], table_ref[parity, 1, 0])
                + dot(folded[parity, 0], table_ref[parity, 1, 1])
                + dot(folded[parity, 0], table_ref[parity, 1, 0])
            )
            for other in range(2):
                sign = 1.0 if other == 0 else -1.0
                half = out[:HALF] + sign * out[HALF:]
                high, low = split(half)
                place = pl.ds(parity * HALF, HALF)
                stacked[other, 0, 0:HALF, place] = high[:, :HALF]
                stacked[other, 0, HALF:, place] = high[:, HALF:]
                stacked[other, 1, 0:HALF, place] = low[:, :HALF]
                stacked[other, 1, HALF:, place] = low[:, HALF:]
        for other in range(2):
            far[image, other] = (
                dot(table_ref[other, 0, 0], stacked[other, 1])
                + dot(table_ref[other, 0, 1], stacked[other, 0])
                + dot(table_ref[other, 0, 0], stacked[other, 0])
            )
        return carry

    lax.fori_loop(0, 4, forward, 0)

    def scale(index, carry):
        scan, other = index // 2, index % 2
        for piece in range(HALF // 32):
            upper, lower = pl.ds(piece * 32, 32), pl.ds(HALF + piece * 32, 32)
            parts = [
                far[2 * scan + mode, other, rows, :] for mode in range(2) for rows in (upper, lower)
            ]
            intensity = (parts[0] * parts[0] + parts[1] * parts[1]) + (
                parts[2] * parts[2] + parts[3] * parts[3]
            )
            measured = measured_ref[scan, other, upper, :]
            factor = measured / jnp.maximum(jnp.sqrt(intensity), FLOOR) - 1.0
            for mode in range(2):
                far[2 * scan + mode, other, upper, :] = parts[2 * mode] * factor
                far[2 * scan + mode, other, lower, :] = parts[2 * mode + 1] * factor
        return carry

    copies[operands].wait()
    lax.fori_loop(0, 4, scale, 0)

    def backward(image, carry):
        scan, mode = image // 2, image % 2
        halves = []
        for other in range(2):
            high, low = split(far[image, other])
            halves.append(
                dot(table_ref[other, 1, 0], low)
                + dot(table_ref[other, 1, 1], high)
                + dot(table_ref[other, 1, 0], high)
            )
        for place, value in ((0, halves[0] + halves[1]), (HALF, halves[0] - halves[1])):
            high, low = split(value)
            for parity in range(2):
                columns = slice(parity * HALF, (parity + 1) * HALF)
                for part in range(2):
                    rows = slice(part * HALF, (part + 1) * HALF)
                    target = pl.ds(part * HALF, HALF)
                    folded[parity, 0, pl.ds(place, HALF), target] = high[rows, columns]
                    folded[parity, 1, pl.ds(place, HALF), target] = low[rows, columns]
        for parity in range(2):
            back[parity] = (
                dot(folded[parity, 1], table_ref[parity, 0, 0])
                + dot(folded[parity, 0], table_ref[parity, 0, 1])
                + dot(folded[parity, 0], table_ref[parity, 0, 0])
            )
        first_scan, first_mode = scan == 0, mode == 0
        for piece in range(SIDE // CHUNK):
            rows = pl.ds(piece * CHUNK, CHUNK)
            even, odd = back[0, rows, :], back[1, rows, :]
            for b in range(2):
                columns = pl.ds(b * HALF, HALF)
                sign = 1.0 if b == 0 else -1.0
                b_re = even[:, :HALF] + sign * odd[:, :HALF]
                b_im = even[:, HALF:] + sign * odd[:, HALF:]
                p_re = probe_rows(0, mode, piece, columns)
                p_im = probe_rows(1, mode, piece, columns)
                w_re, w_im = windows[scan, 0, rows, columns], windows[scan, 1, rows, columns]
                o_re = p_re * b_re + p_im * b_im
                o_im = p_re * b_im - p_im * b_re
                zero = jnp.zeros_like(o_re)
                contrib[0, rows, columns] = o_re + jnp.where(
                    first_mode, zero, contrib[0, rows, columns]
                )
                contrib[1, rows, columns] = o_im + jnp.where(
                    first_mode, zero, contrib[1, rows, columns]
                )
                g_re = w_re * b_re + w_im * b_im
                g_im = w_re * b_im - w_im * b_re
                for slot in range(CHUNK // 8):
                    group = piece * (CHUNK // 8) + slot
                    inner = slice(slot * 8, slot * 8 + 8)
                    for part, value in enumerate((g_re, g_im)):
                        place = 2 * part + mode
                        old = sums[group, place, :, columns]
                        sums[group, place, :, columns] = value[inner] + jnp.where(
                            first_scan, jnp.zeros_like(old), old
                        )

        @pl.when(mode == 1)
        def _():
            row, column = offsets_ref[0, 0, scan, 0] + HALF, offsets_ref[0, 0, scan, 1] + HALF
            inner = lax.rem(row, 8)
            base = pl.multiple_of(row - inner, 8)
            turn, keep = lax.rem(column, TILE), lane >= column
            zero = jnp.zeros((CHUNK // 8, 8, TILE), F32)
            edge = jnp.zeros((1, 8, TILE), F32)
            stay = lax.broadcasted_iota(jnp.int32, (CHUNK // 8 + 1, 8, TILE), 1) >= inner
            for channel in range(3):
                for piece in range(SIDE // CHUNK):
                    halves = []
                    for b in range(2):
                        value = contrib[channel, pl.ds(piece * CHUNK, CHUNK), pl.ds(b * TILE, TILE)]
                        halves.append(pltpu.roll(value.reshape(CHUNK // 8, 8, TILE), turn, 2))
                    thirds = (
                        jnp.where(keep, halves[0], zero),
                        jnp.where(keep, halves[1], halves[0]),
                        jnp.where(keep, zero, halves[1]),
                    )
                    place = pl.ds(base + piece * CHUNK, CHUNK + 8)
                    for b in range(3):
                        value = pltpu.roll(thirds[b], inner, 1)
                        value = jnp.where(
                            stay,
                            jnp.concatenate([value, edge]),
                            jnp.concatenate([edge, value]),
                        )
                        total[channel, place, pl.ds(b * TILE, TILE)] += value.reshape(CHUNK + 8, TILE)

        return carry

    for piece in range(SIDE // CHUNK):
        rows = pl.ds(piece * CHUNK, CHUNK)
        power = None
        for mode in range(2):
            for part in range(2):
                value = probe_rows(part, mode, piece)
                power = value * value if power is None else power + value * value
        contrib[2, rows, :] = power
        weight = None
        for scan in range(2):
            for part in range(2):
                value = windows[scan, part, rows, :]
                weight = value * value if weight is None else weight + value * value
        for slot in range(CHUNK // 8):
            sums[piece * (CHUNK // 8) + slot, 4] = weight[slot * 8 : slot * 8 + 8]

    lax.fori_loop(0, 4, backward, 0)

    done = len(copies)
    for block, ref in enumerate((grad_above, grad_middle, grad_below)):
        for column in range(3):
            start(total.at[:, third(block), third(column)], ref.at[column])
    start(sums.at[pl.ds(core * GROUPS, GROUPS)], mine_out)
    start(sums.at[pl.ds((1 - core) * GROUPS, GROUPS)], other_out)
    for copy in copies[done:]:
        copy.wait()


def spread_kernel(pieces_ref, out_ref):
    total = pieces_ref[0]
    for piece in range(1, GROUPS):
        total = total + pieces_ref[piece]
    for copy in range(DEPTH):
        out_ref[copy] = total


def update_kernel(pieces_ref, old_ref, out_ref, new_ref):
    total = pieces_ref[0]
    for piece in range(1, DEPTH):
        total = total + pieces_ref[piece]
    new = old_ref[...] + PROBE_STEP * total[:4] / (total[4:] + PROBE_REG)
    new_ref[...] = new
    for copy in range(GROUPS):
        out_ref[copy] = new


VMEM_SPEC = pl.BlockSpec(memory_space=pltpu.VMEM)
SMEM_SPEC = pl.BlockSpec(memory_space=pltpu.SMEM)
ANY_SPEC = pl.BlockSpec(memory_space=pl.ANY)


def in_hbm(value):
    return pltpu.with_memory_space_constraint(value, pltpu.HBM)


def params(mebibytes):
    return pltpu.CompilerParams(vmem_limit_bytes=mebibytes * 2**20)


def sort_measured(measured):
    return pl.pallas_call(
        sort_kernel,
        out_shape=jax.ShapeDtypeStruct((2, 2, HALF, SIDE), F32),
        in_specs=[VMEM_SPEC],
        out_specs=VMEM_SPEC,
        compiler_params=params(8),
        name="sort_measured",
    )(measured)


def step(offsets, core, table, probe, measured, around):
    halves = len(probe) - 1
    band = jax.ShapeDtypeStruct((3, 3, TILE, TILE), F32)
    half = jax.ShapeDtypeStruct((GROUPS, 5, 8, SIDE), F32)
    return pl.pallas_call(
        functools.partial(step_kernel, halves),
        out_shape=[half, half, band, band, band],
        in_specs=[SMEM_SPEC, SMEM_SPEC] + [ANY_SPEC] * (8 + halves),
        out_specs=[ANY_SPEC] * 5,
        scratch_shapes=[
            pltpu.VMEM(table.shape, BF16),
            pltpu.VMEM((4, 2 * GROUPS, 8, SIDE), F32),
            pltpu.VMEM(measured.shape, F32),
            pltpu.VMEM((2, WIDE + 8, WIDE), F32),
            pltpu.VMEM((2, 2, SIDE, SIDE), F32),
            pltpu.VMEM((2, 2, SIDE, SIDE), BF16),
            pltpu.VMEM((2, 2, SIDE, SIDE), BF16),
            pltpu.VMEM((4, 2, SIDE, SIDE), F32),
            pltpu.VMEM((2, SIDE, SIDE), F32),
            pltpu.VMEM((3, SIDE, SIDE), F32),
            pltpu.VMEM((3, WIDE + 8, WIDE), F32),
            pltpu.VMEM((2 * GROUPS, 5, 8, SIDE), F32),
            pltpu.SemaphoreType.DMA((32,)),
        ],
        compiler_params=params(20),
        name="step",
    )(offsets, core, table, *probe, measured, *around)


def up(axis):
    return [(i, i + 1) for i in range(lax.axis_size(axis) - 1)]


def down(axis):
    return [(i + 1, i) for i in range(lax.axis_size(axis) - 1)]


def beside(tile):
    left = lax.ppermute(tile, "col", up("col"))
    right = lax.ppermute(tile, "col", down("col"))
    return left, right, jnp.stack([left, tile, right])


def beyond(band):
    return lax.ppermute(band, "row", up("row")), lax.ppermute(band, "row", down("row"))


def after(value, *others):
    return lax.optimization_barrier((value,) + others)[0]


def places(device):
    row, column = divmod(device, 16)
    return (column // 8) * 4 + row // 4, row % 4, column // 2 % 4, column % 2


def grouped(key):
    groups = {}
    for device in range(256):
        groups.setdefault(key(*places(device)), []).append(device)
    return list(groups.values())


PLANES = grouped(lambda z, y, x, core: (z, core))
LINES = grouped(lambda z, y, x, core: (y, x, core))
BOTH = ("row", "col")
SWAP = [(i, i ^ 1) for i in range(16)]


def exchange(value, groups):
    return lax.all_to_all(value, BOTH, 0, 0, axis_index_groups=groups, tiled=True)


def spread(pieces):
    return pl.pallas_call(
        spread_kernel,
        out_shape=jax.ShapeDtypeStruct((DEPTH, 5, 8, SIDE), F32),
        compiler_params=params(8),
        name="spread",
    )(pieces)


def update(pieces, old):
    return pl.pallas_call(
        update_kernel,
        out_shape=[
            jax.ShapeDtypeStruct((GROUPS, 4, 8, SIDE), F32),
            jax.ShapeDtypeStruct((4, 8, SIDE), F32),
        ],
        compiler_params=params(8),
        name="update",
    )(pieces, old)


def local(object_field, probe, amplitudes, offsets):
    table = in_hbm(jnp.asarray(tables()))
    row, column = lax.axis_index("row"), lax.axis_index("col")
    core = column & 1
    group = core * GROUPS + (row & 3) * 4 + (lax.shift_right_logical(column, 1) & 3)
    probe = probe.reshape(4, 2 * GROUPS, 8, SIDE)
    old = lax.dynamic_index_in_dim(probe, group, 1, False)
    core = core.reshape(1)
    measured = sort_measured(amplitudes[0, 0])
    parts = (in_hbm(probe),)
    tile = object_field
    left, right, band = beside(tile)
    above, below = beyond(band)
    for iteration in range(ITERS):
        mine, other, above, middle, below = step(
            offsets, core, table, parts, measured, (left, tile, right, above, below)
        )
        above = lax.ppermute(above, "row", down("row"))
        below = lax.ppermute(below, "row", up("row"))
        mine = mine + lax.ppermute(other, "col", SWAP)
        pieces = exchange(mine, PLANES)
        first, own, last = (middle[i] + above[i] + below[i] for i in range(3))
        pieces = spread(after(pieces, first, own, last))
        first = lax.ppermute(first, "col", down("col"))
        last = lax.ppermute(last, "col", up("col"))
        pieces = exchange(pieces, LINES)
        totals = own + first + last
        tile = tile + OBJECT_STEP * totals[0:2] / (totals[2:3] + OBJECT_REG)
        last_iteration = iteration + 1 == ITERS
        if last_iteration:
            pieces = after(pieces, tile)
        else:
            left, right, band = beside(tile)
            pieces = after(pieces, band)
        pieces, old = update(pieces, old)
        mine = exchange(pieces, PLANES)
        if not last_iteration:
            above, below = beyond(band)
            mine = after(mine, above, below)
        parts = (mine, lax.ppermute(mine, "col", SWAP))
    probe = pl.pallas_call(
        lay_out_kernel,
        out_shape=jax.ShapeDtypeStruct((4, 2 * GROUPS, 8, SIDE), F32),
        in_specs=[SMEM_SPEC, VMEM_SPEC, VMEM_SPEC],
        out_specs=VMEM_SPEC,
        compiler_params=params(8),
        name="lay_out",
    )(core, *parts)
    return (tile, probe.reshape(2, 2, SIDE, SIDE))


def solution(mesh):
    return jax.shard_map(
        local,
        mesh=mesh,
        in_specs=(
            P(None, "row", "col"),
            P(),
            P("row", "col", None, None, None),
            P("row", "col", None, None),
        ),
        out_specs=(P(None, "row", "col"), P()),
        check_vma=False,
    )
```

```python
import functools
import math

import jax
import jax.numpy as jnp
import ml_dtypes
import numpy as np
from jax import lax
from jax.experimental import pallas as pl
from jax.experimental.pallas import tpu as pltpu
from jax.sharding import PartitionSpec as P

ITERS = 2
FLOOR = 0.5
OBJECT_STEP = 0.5
OBJECT_REG = 0.5
PROBE_STEP = 1.0
PROBE_REG = 1.0
TILE = 128
SIDE = 256
HALF = SIDE // 2
WIDE = 3 * TILE
CHUNK = 64
GROUPS = 16
DEPTH = 8
F32 = jnp.float32
BF16 = jnp.bfloat16


def split_np(table):
    high = table.astype(np.float32).astype(ml_dtypes.bfloat16)
    low = (table - high.astype(np.float64)).astype(np.float32).astype(ml_dtypes.bfloat16)
    return np.stack([high, low])


def tables():
    out = []
    for parity in range(2):
        u = 2 * np.arange(HALF)[:, None] + parity
        angle = 2.0 * math.pi * ((u * np.arange(HALF)[None, :]) % SIDE) / SIDE
        cos, sin = np.cos(angle) / 16.0, np.sin(angle) / 16.0
        forward = np.block([[cos, sin], [-sin, cos]])
        out.append(np.stack([split_np(forward), split_np(forward.T)]))
    return np.stack(out)


def split(x):
    high = x.astype(BF16)
    return high, (x - high.astype(F32)).astype(BF16)


def split_whole(x):
    high = x.astype(BF16)
    rest = x - high.astype(F32)
    middle = rest.astype(BF16)
    return high, middle, (rest - middle.astype(F32)).astype(BF16)


def dot(a, b):
    return jnp.dot(a, b, preferred_element_type=F32)


def sort_kernel(measured_ref, out_ref):
    source = lax.broadcasted_iota(jnp.int32, (SIDE, SIDE), 0)
    place = lax.broadcasted_iota(jnp.int32, (SIDE, SIDE), 1)
    wanted = jnp.where(place < HALF, 2 * place, 2 * place - (SIDE - 1))
    select = jnp.where(source == wanted, 1.0, 0.0).astype(BF16)
    wanted = jnp.where(source < HALF, 2 * source, 2 * source - (SIDE - 1))
    select_rows = jnp.where(place == wanted, 1.0, 0.0).astype(BF16)
    for scan in range(2):
        high, middle, low = split_whole(measured_ref[scan])
        turned = (dot(low, select) + dot(middle, select)) + dot(high, select)
        high, middle, low = split_whole(turned)
        turned = (dot(select_rows, low) + dot(select_rows, middle)) + dot(select_rows, high)
        out_ref[scan, 0] = turned[:HALF]
        out_ref[scan, 1] = turned[HALF:]


def lay_out_kernel(parity_ref, mine_ref, other_ref, out_ref):
    for half, ref in enumerate((mine_ref, other_ref)):
        place = parity_ref[1] if half == 0 else 1 - parity_ref[1]
        for part in range(4):
            out_ref[part, pl.ds(place * GROUPS, GROUPS)] = ref[:, part]


def step_kernel(halves, offsets_ref, parity_ref, table_in, *refs):
    probe_in, refs = refs[: 1 + halves], refs[1 + halves :]
    (
        measured_in,
        outer_in,
        tile_in,
        inner_in,
        second_in,
        first_in,
        mine_out,
        other_out,
        grad_second,
        grad_middle,
        grad_first,
        table_ref,
        probe,
        measured_ref,
        padded,
        windows,
        folded,
        stacked,
        far,
        back,
        contrib,
        power_ref,
        total,
        sums,
        semaphores,
    ) = refs
    row_parity, core = parity_ref[0], parity_ref[1]
    across = (row_parity * 2, 1, 2 - row_parity * 2)
    along = (core * 2, 1, 2 - core * 2)
    copies = []

    def start(source, target):
        copy = pltpu.make_async_copy(source, target, semaphores.at[len(copies)])
        copy.start()
        copies.append(copy)

    def third(block):
        return pl.ds(pl.multiple_of(block * TILE, TILE), TILE)

    for place, piece in enumerate((outer_in, tile_in, inner_in)):
        columns = third(along[place])
        start(piece, padded.at[:, third(1), columns])
        start(second_in.at[place], padded.at[:, third(across[0]), columns])
        start(first_in.at[place], padded.at[:, third(across[2]), columns])
    near = len(copies)
    if halves:
        for half, ref in enumerate(probe_in):
            place = core if half == 0 else 1 - core
            for part in range(4):
                start(ref.at[:, part], probe.at[part, pl.ds(place * GROUPS, GROUPS)])
    else:
        start(probe_in[0], probe)
    start(table_in, table_ref)
    operands = len(copies)
    start(measured_in, measured_ref)

    def probe_rows(part, mode, piece, columns=slice(None)):
        groups = pl.ds(piece * (CHUNK // 8), CHUNK // 8)
        value = probe[2 * part + mode, groups, :, columns]
        return value.reshape(CHUNK, value.shape[-1])

    lane = lax.broadcasted_iota(jnp.int32, (CHUNK // 8, 8, TILE), 2)
    sublane = lax.broadcasted_iota(jnp.int32, (CHUNK // 8, 8, TILE), 1)
    for channel in range(3):
        total[channel] = jnp.zeros((WIDE + 8, WIDE), F32)
    for copy in copies[:near]:
        copy.wait()

    def cut(scan, carry):
        row, column = offsets_ref[0, 0, scan, 0] + HALF, offsets_ref[0, 0, scan, 1] + HALF
        inner = lax.rem(row, 8)
        base = pl.multiple_of(row - inner, 8)
        turn, keep = lax.rem(TILE - column, TILE), lane < TILE - column
        lift, stay = lax.rem(8 - inner, 8), sublane < 8 - inner
        for channel in range(2):
            for piece in range(SIDE // CHUNK):
                turned = []
                for b in range(3):
                    rows = padded[channel, pl.ds(base + piece * CHUNK, CHUNK + 8), pl.ds(b * TILE, TILE)]
                    rows = pltpu.roll(rows.reshape(CHUNK // 8 + 1, 8, TILE), lift, 1)
                    rows = jnp.where(stay, rows[:-1], rows[1:])
                    turned.append(pltpu.roll(rows, turn, 2))
                for b in range(2):
                    windows[scan, channel, pl.ds(piece * CHUNK, CHUNK), pl.ds(b * TILE, TILE)] = (
                        jnp.where(keep, turned[b], turned[b + 1]).reshape(CHUNK, TILE)
                    )
        return carry

    lax.fori_loop(0, 2, cut, 0)
    for copy in copies[near:operands]:
        copy.wait()

    def forward(image, carry):
        scan, mode = image // 2, image % 2
        for piece in range(SIDE // CHUNK):
            rows = pl.ds(piece * CHUNK, CHUNK)
            p_re, p_im = probe_rows(0, mode, piece), probe_rows(1, mode, piece)
            w_re, w_im = windows[scan, 0, rows, :], windows[scan, 1, rows, :]
            e_re = p_re * w_re - p_im * w_im
            e_im = p_re * w_im + p_im * w_re
            for parity in range(2):
                sign = 1.0 if parity == 0 else -1.0
                for part, value in enumerate((e_re, e_im)):
                    half = value[:, :HALF] + sign * value[:, HALF:]
                    high, low = split(half)
                    folded[parity, 0, rows, part * HALF : (part + 1) * HALF] = high
                    folded[parity, 1, rows, part * HALF : (part + 1) * HALF] = low
        for parity in range(2):
            out = (
                dot(folded[parity, 1], table_ref[parity, 1, 0])
                + dot(folded[parity, 0], table_ref[parity, 1, 1])
                + dot(folded[parity, 0], table_ref[parity, 1, 0])
            )
            for other in range(2):
                sign = 1.0 if other == 0 else -1.0
                half = out[:HALF] + sign * out[HALF:]
                high, low = split(half)
                place = pl.ds(parity * HALF, HALF)
                stacked[other, 0, 0:HALF, place] = high[:, :HALF]
                stacked[other, 0, HALF:, place] = high[:, HALF:]
                stacked[other, 1, 0:HALF, place] = low[:, :HALF]
                stacked[other, 1, HALF:, place] = low[:, HALF:]
        for other in range(2):
            far[image, other] = (
                dot(table_ref[other, 0, 0], stacked[other, 1])
                + dot(table_ref[other, 0, 1], stacked[other, 0])
                + dot(table_ref[other, 0, 0], stacked[other, 0])
            )
        return carry

    lax.fori_loop(0, 4, forward, 0)

    def scale(index, carry):
        scan, other = index // 2, index % 2
        for piece in range(HALF // 32):
            upper, lower = pl.ds(piece * 32, 32), pl.ds(HALF + piece * 32, 32)
            parts = [
                far[2 * scan + mode, other, rows, :] for mode in range(2) for rows in (upper, lower)
            ]
            intensity = (parts[0] * parts[0] + parts[1] * parts[1]) + (
                parts[2] * parts[2] + parts[3] * parts[3]
            )
            measured = measured_ref[scan, other, upper, :]
            factor = measured / jnp.maximum(jnp.sqrt(intensity), FLOOR) - 1.0
            for mode in range(2):
                far[2 * scan + mode, other, upper, :] = parts[2 * mode] * factor
                far[2 * scan + mode, other, lower, :] = parts[2 * mode + 1] * factor
        return carry

    copies[operands].wait()
    lax.fori_loop(0, 4, scale, 0)

    def backward(image, carry):
        scan, mode = image // 2, image % 2
        halves = []
        for other in range(2):
            high, low = split(far[image, other])
            halves.append(
                dot(table_ref[other, 1, 0], low)
                + dot(table_ref[other, 1, 1], high)
                + dot(table_ref[other, 1, 0], high)
            )
        for place, value in ((0, halves[0] + halves[1]), (HALF, halves[0] - halves[1])):
            high, low = split(value)
            for parity in range(2):
                columns = slice(parity * HALF, (parity + 1) * HALF)
                for part in range(2):
                    rows = slice(part * HALF, (part + 1) * HALF)
                    target = pl.ds(part * HALF, HALF)
                    folded[parity, 0, pl.ds(place, HALF), target] = high[rows, columns]
                    folded[parity, 1, pl.ds(place, HALF), target] = low[rows, columns]
        for parity in range(2):
            back[parity] = (
                dot(folded[parity, 1], table_ref[parity, 0, 0])
                + dot(folded[parity, 0], table_ref[parity, 0, 1])
                + dot(folded[parity, 0], table_ref[parity, 0, 0])
            )
        first_scan, first_mode = scan == 0, mode == 0
        for piece in range(SIDE // CHUNK):
            rows = pl.ds(piece * CHUNK, CHUNK)
            even, odd = back[0, rows, :], back[1, rows, :]
            for b in range(2):
                columns = pl.ds(b * HALF, HALF)
                sign = 1.0 if b == 0 else -1.0
                b_re = even[:, :HALF] + sign * odd[:, :HALF]
                b_im = even[:, HALF:] + sign * odd[:, HALF:]
                p_re = probe_rows(0, mode, piece, columns)
                p_im = probe_rows(1, mode, piece, columns)
                w_re, w_im = windows[scan, 0, rows, columns], windows[scan, 1, rows, columns]
                o_re = p_re * b_re + p_im * b_im
                o_im = p_re * b_im - p_im * b_re
                zero = jnp.zeros_like(o_re)
                contrib[scan, 0, rows, columns] = o_re + jnp.where(
                    first_mode, zero, contrib[scan, 0, rows, columns]
                )
                contrib[scan, 1, rows, columns] = o_im + jnp.where(
                    first_mode, zero, contrib[scan, 1, rows, columns]
                )
                g_re = w_re * b_re + w_im * b_im
                g_im = w_re * b_im - w_im * b_re
                for slot in range(CHUNK // 8):
                    group = piece * (CHUNK // 8) + slot
                    inner = slice(slot * 8, slot * 8 + 8)
                    for part, value in enumerate((g_re, g_im)):
                        place = 2 * part + mode
                        old = sums[group, place, :, columns]
                        sums[group, place, :, columns] = value[inner] + jnp.where(
                            first_scan, jnp.zeros_like(old), old
                        )

        return carry

    for piece in range(SIDE // CHUNK):
        rows = pl.ds(piece * CHUNK, CHUNK)
        power = None
        for mode in range(2):
            for part in range(2):
                value = probe_rows(part, mode, piece)
                power = value * value if power is None else power + value * value
        power_ref[rows, :] = power
        weight = None
        for scan in range(2):
            for part in range(2):
                value = windows[scan, part, rows, :]
                weight = value * value if weight is None else weight + value * value
        for slot in range(CHUNK // 8):
            sums[piece * (CHUNK // 8) + slot, 4] = weight[slot * 8 : slot * 8 + 8]

    lax.fori_loop(0, 4, backward, 0)

    def scatter(scan, carry):
        row, column = offsets_ref[0, 0, scan, 0] + HALF, offsets_ref[0, 0, scan, 1] + HALF
        inner = lax.rem(row, 8)
        base = pl.multiple_of(row - inner, 8)
        turn, keep = lax.rem(column, TILE), lane >= column
        zero = jnp.zeros((CHUNK // 8, 8, TILE), F32)
        edge = jnp.zeros((1, 8, TILE), F32)
        stay = lax.broadcasted_iota(jnp.int32, (CHUNK // 8 + 1, 8, TILE), 1) >= inner
        for channel in range(3):
            for piece in range(SIDE // CHUNK):
                halves = []
                for b in range(2):
                    value = (power_ref if channel == 2 else contrib.at[scan, channel])[
                        pl.ds(piece * CHUNK, CHUNK), pl.ds(b * TILE, TILE)
                    ]
                    halves.append(pltpu.roll(value.reshape(CHUNK // 8, 8, TILE), turn, 2))
                thirds = (
                    jnp.where(keep, halves[0], zero),
                    jnp.where(keep, halves[1], halves[0]),
                    jnp.where(keep, zero, halves[1]),
                )
                place = pl.ds(base + piece * CHUNK, CHUNK + 8)
                for b in range(3):
                    value = pltpu.roll(thirds[b], inner, 1)
                    value = jnp.where(
                        stay,
                        jnp.concatenate([value, edge]),
                        jnp.concatenate([edge, value]),
                    )
                    total[channel, place, pl.ds(b * TILE, TILE)] += value.reshape(CHUNK + 8, TILE)
        return carry

    done = len(copies)
    start(sums.at[pl.ds(core * GROUPS, GROUPS)], mine_out)
    start(sums.at[pl.ds((1 - core) * GROUPS, GROUPS)], other_out)
    lax.fori_loop(0, 2, scatter, 0)
    for block, ref in enumerate((grad_second, grad_middle, grad_first)):
        for column in range(3):
            start(total.at[:, third(across[block]), third(along[column])], ref.at[column])
    for copy in copies[done:]:
        copy.wait()


def spread_kernel(pieces_ref, out_ref):
    total = pieces_ref[0]
    for piece in range(1, GROUPS):
        total = total + pieces_ref[piece]
    for copy in range(DEPTH):
        out_ref[copy] = total


def update_kernel(pieces_ref, old_ref, out_ref, new_ref):
    total = pieces_ref[0]
    for piece in range(1, DEPTH):
        total = total + pieces_ref[piece]
    new = old_ref[...] + PROBE_STEP * total[:4] / (total[4:] + PROBE_REG)
    new_ref[...] = new
    for copy in range(GROUPS):
        out_ref[copy] = new


VMEM_SPEC = pl.BlockSpec(memory_space=pltpu.VMEM)
SMEM_SPEC = pl.BlockSpec(memory_space=pltpu.SMEM)
ANY_SPEC = pl.BlockSpec(memory_space=pl.ANY)


def in_hbm(value):
    return pltpu.with_memory_space_constraint(value, pltpu.HBM)


def params(mebibytes):
    return pltpu.CompilerParams(vmem_limit_bytes=mebibytes * 2**20)


def sort_measured(measured):
    return pl.pallas_call(
        sort_kernel,
        out_shape=jax.ShapeDtypeStruct((2, 2, HALF, SIDE), F32),
        in_specs=[VMEM_SPEC],
        out_specs=VMEM_SPEC,
        compiler_params=params(8),
        name="sort_measured",
    )(measured)


def step(offsets, parity, table, probe, measured, around):
    halves = len(probe) - 1
    band = jax.ShapeDtypeStruct((3, 3, TILE, TILE), F32)
    half = jax.ShapeDtypeStruct((GROUPS, 5, 8, SIDE), F32)
    return pl.pallas_call(
        functools.partial(step_kernel, halves),
        out_shape=[half, half, band, band, band],
        in_specs=[SMEM_SPEC, SMEM_SPEC] + [ANY_SPEC] * (8 + halves),
        out_specs=[ANY_SPEC] * 5,
        scratch_shapes=[
            pltpu.VMEM(table.shape, BF16),
            pltpu.VMEM((4, 2 * GROUPS, 8, SIDE), F32),
            pltpu.VMEM(measured.shape, F32),
            pltpu.VMEM((2, WIDE + 8, WIDE), F32),
            pltpu.VMEM((2, 2, SIDE, SIDE), F32),
            pltpu.VMEM((2, 2, SIDE, SIDE), BF16),
            pltpu.VMEM((2, 2, SIDE, SIDE), BF16),
            pltpu.VMEM((4, 2, SIDE, SIDE), F32),
            pltpu.VMEM((2, SIDE, SIDE), F32),
            pltpu.VMEM((2, 2, SIDE, SIDE), F32),
            pltpu.VMEM((SIDE, SIDE), F32),
            pltpu.VMEM((3, WIDE + 8, WIDE), F32),
            pltpu.VMEM((2 * GROUPS, 5, 8, SIDE), F32),
            pltpu.SemaphoreType.DMA((32,)),
        ],
        compiler_params=params(20),
        name="step",
    )(offsets, parity, table, *probe, measured, *around)


def pairs(first):
    both = [(i, i + 1) for i in range(first, 15, 2)]
    return both + [(j, i) for i, j in both]


def neighbourhood(tile):
    inner = lax.ppermute(tile, "col", pairs(0))
    outer = lax.ppermute(tile, "col", pairs(1))
    band = jnp.stack([outer, tile, inner])
    first = lax.ppermute(band, "row", pairs(0))
    second = lax.ppermute(band, "row", pairs(1))
    return outer, tile, inner, second, first


def fold(second, middle, first):
    first = lax.ppermute(first, "row", pairs(0))
    second = lax.ppermute(second, "row", pairs(1))
    outer, own, inner = (middle[i] + first[i] + second[i] for i in range(3))
    inner = lax.ppermute(inner, "col", pairs(0))
    outer = lax.ppermute(outer, "col", pairs(1))
    return own + inner + outer


def places(device):
    row, column = divmod(device, 16)
    return (column // 8) * 4 + row // 4, row % 4, column // 2 % 4, column % 2


def grouped(key):
    groups = {}
    for device in range(256):
        groups.setdefault(key(*places(device)), []).append(device)
    return list(groups.values())


PLANES = grouped(lambda z, y, x, core: (z, core))
LINES = grouped(lambda z, y, x, core: (y, x, core))
BOTH = ("row", "col")
SWAP = [(i, i ^ 1) for i in range(16)]


def exchange(value, groups):
    return lax.all_to_all(value, BOTH, 0, 0, axis_index_groups=groups, tiled=True)


def new_probe(mine, other, old):
    mine = mine + lax.ppermute(other, "col", SWAP)
    pieces = exchange(mine, PLANES)
    pieces = pl.pallas_call(
        spread_kernel,
        out_shape=jax.ShapeDtypeStruct((DEPTH, 5, 8, SIDE), F32),
        compiler_params=params(8),
        name="spread",
    )(pieces)
    pieces = exchange(pieces, LINES)
    pieces, new = pl.pallas_call(
        update_kernel,
        out_shape=[
            jax.ShapeDtypeStruct((GROUPS, 4, 8, SIDE), F32),
            jax.ShapeDtypeStruct((4, 8, SIDE), F32),
        ],
        compiler_params=params(8),
        name="update",
    )(pieces, old)
    mine = exchange(pieces, PLANES)
    other = lax.ppermute(mine, "col", SWAP)
    return mine, other, new


def local(object_field, probe, amplitudes, offsets):
    table = in_hbm(jnp.asarray(tables()))
    row, column = lax.axis_index("row"), lax.axis_index("col")
    core = column & 1
    group = core * GROUPS + (row & 3) * 4 + (lax.shift_right_logical(column, 1) & 3)
    probe = probe.reshape(4, 2 * GROUPS, 8, SIDE)
    old = lax.dynamic_index_in_dim(probe, group, 1, False)
    parity = jnp.stack([row & 1, core])
    measured = sort_measured(amplitudes[0, 0])
    parts = (in_hbm(probe),)
    for iteration in range(ITERS):
        mine, other, second, middle, first = step(
            offsets, parity, table, parts, measured, neighbourhood(object_field)
        )
        mine, other, old = new_probe(mine, other, old)
        parts = (mine, other)
        totals = fold(second, middle, first)
        object_field = object_field + OBJECT_STEP * totals[0:2] / (totals[2:3] + OBJECT_REG)
    probe = pl.pallas_call(
        lay_out_kernel,
        out_shape=jax.ShapeDtypeStruct((4, 2 * GROUPS, 8, SIDE), F32),
        in_specs=[SMEM_SPEC, VMEM_SPEC, VMEM_SPEC],
        out_specs=VMEM_SPEC,
        compiler_params=params(8),
        name="lay_out",
    )(parity, *parts)
    return (object_field, probe.reshape(2, 2, SIDE, SIDE))


def solution(mesh):
    return jax.shard_map(
        local,
        mesh=mesh,
        in_specs=(
            P(None, "row", "col"),
            P(),
            P("row", "col", None, None, None),
            P("row", "col", None, None),
        ),
        out_specs=(P(None, "row", "col"), P()),
        check_vma=False,
    )
```

```python
import functools
import math

import jax
import jax.numpy as jnp
import ml_dtypes
import numpy as np
from jax import lax
from jax.experimental import pallas as pl
from jax.experimental.pallas import tpu as pltpu
from jax.sharding import PartitionSpec as P

ITERS = 2
FLOOR = 0.5
OBJECT_STEP = 0.5
OBJECT_REG = 0.5
PROBE_STEP = 1.0
PROBE_REG = 1.0
TILE = 128
SIDE = 256
HALF = SIDE // 2
WIDE = 3 * TILE
CHUNK = 64
GROUPS = 16
DEPTH = 8
F32 = jnp.float32
BF16 = jnp.bfloat16


def split_np(table):
    high = table.astype(np.float32).astype(ml_dtypes.bfloat16)
    low = (table - high.astype(np.float64)).astype(np.float32).astype(ml_dtypes.bfloat16)
    return np.stack([high, low])


def tables():
    out = []
    for parity in range(2):
        u = 2 * np.arange(HALF)[:, None] + parity
        angle = 2.0 * math.pi * ((u * np.arange(HALF)[None, :]) % SIDE) / SIDE
        cos, sin = np.cos(angle) / 16.0, np.sin(angle) / 16.0
        forward = np.block([[cos, sin], [-sin, cos]])
        out.append(np.stack([split_np(forward), split_np(forward.T)]))
    return np.stack(out)


def split(x):
    high = x.astype(BF16)
    return high, (x - high.astype(F32)).astype(BF16)


def split_whole(x):
    high = x.astype(BF16)
    rest = x - high.astype(F32)
    middle = rest.astype(BF16)
    return high, middle, (rest - middle.astype(F32)).astype(BF16)


def dot(a, b):
    return jnp.dot(a, b, preferred_element_type=F32)


def sort_kernel(measured_ref, out_ref):
    source = lax.broadcasted_iota(jnp.int32, (SIDE, SIDE), 0)
    place = lax.broadcasted_iota(jnp.int32, (SIDE, SIDE), 1)
    wanted = jnp.where(place < HALF, 2 * place, 2 * place - (SIDE - 1))
    select = jnp.where(source == wanted, 1.0, 0.0).astype(BF16)
    wanted = jnp.where(source < HALF, 2 * source, 2 * source - (SIDE - 1))
    select_rows = jnp.where(place == wanted, 1.0, 0.0).astype(BF16)
    for scan in range(2):
        high, middle, low = split_whole(measured_ref[scan])
        turned = (dot(low, select) + dot(middle, select)) + dot(high, select)
        high, middle, low = split_whole(turned)
        turned = (dot(select_rows, low) + dot(select_rows, middle)) + dot(select_rows, high)
        out_ref[scan, 0] = turned[:HALF]
        out_ref[scan, 1] = turned[HALF:]


def lay_out_kernel(parity_ref, mine_ref, other_ref, out_ref):
    for half, ref in enumerate((mine_ref, other_ref)):
        place = parity_ref[1] if half == 0 else 1 - parity_ref[1]
        for part in range(4):
            out_ref[part, pl.ds(place * GROUPS, GROUPS)] = ref[:, part]


def step_kernel(halves, offsets_ref, parity_ref, table_in, *refs):
    probe_in, refs = refs[: 1 + halves], refs[1 + halves :]
    (
        measured_in,
        outer_in,
        tile_in,
        inner_in,
        second_in,
        first_in,
        mine_out,
        other_out,
        grad_second,
        grad_middle,
        grad_first,
        table_ref,
        probe,
        measured_ref,
        padded,
        windows,
        folded,
        stacked,
        far,
        back,
        contrib,
        power_ref,
        total,
        sums,
        semaphores,
    ) = refs
    row_parity, core = parity_ref[0], parity_ref[1]
    across = (row_parity * 2, 1, 2 - row_parity * 2)
    along = (core * 2, 1, 2 - core * 2)
    copies = []

    def start(source, target):
        copy = pltpu.make_async_copy(source, target, semaphores.at[len(copies)])
        copy.start()
        copies.append(copy)

    def third(block):
        return pl.ds(pl.multiple_of(block * TILE, TILE), TILE)

    for place, piece in enumerate((outer_in, tile_in, inner_in)):
        columns = third(along[place])
        start(piece, padded.at[:, third(1), columns])
        start(second_in.at[place], padded.at[:, third(across[0]), columns])
        start(first_in.at[place], padded.at[:, third(across[2]), columns])
    near = len(copies)
    if halves:
        for half, ref in enumerate(probe_in):
            place = core if half == 0 else 1 - core
            for part in range(4):
                start(ref.at[:, part], probe.at[part, pl.ds(place * GROUPS, GROUPS)])
    else:
        start(probe_in[0], probe)
    start(table_in, table_ref)
    operands = len(copies)
    start(measured_in, measured_ref)

    def probe_rows(part, mode, piece, columns=slice(None)):
        groups = pl.ds(piece * (CHUNK // 8), CHUNK // 8)
        value = probe[2 * part + mode, groups, :, columns]
        return value.reshape(CHUNK, value.shape[-1])

    lane = lax.broadcasted_iota(jnp.int32, (CHUNK // 8, 8, TILE), 2)
    sublane = lax.broadcasted_iota(jnp.int32, (CHUNK // 8, 8, TILE), 1)
    for channel in range(3):
        total[channel] = jnp.zeros((WIDE + 8, WIDE), F32)
    for copy in copies[:near]:
        copy.wait()

    def cut(scan, carry):
        row, column = offsets_ref[0, 0, scan, 0] + HALF, offsets_ref[0, 0, scan, 1] + HALF
        inner = lax.rem(row, 8)
        base = pl.multiple_of(row - inner, 8)
        turn, keep = lax.rem(TILE - column, TILE), lane < TILE - column
        lift, stay = lax.rem(8 - inner, 8), sublane < 8 - inner
        for channel in range(2):
            for piece in range(SIDE // CHUNK):
                turned = []
                for b in range(3):
                    rows = padded[channel, pl.ds(base + piece * CHUNK, CHUNK + 8), pl.ds(b * TILE, TILE)]
                    rows = pltpu.roll(rows.reshape(CHUNK // 8 + 1, 8, TILE), lift, 1)
                    rows = jnp.where(stay, rows[:-1], rows[1:])
                    turned.append(pltpu.roll(rows, turn, 2))
                for b in range(2):
                    windows[scan, channel, pl.ds(piece * CHUNK, CHUNK), pl.ds(b * TILE, TILE)] = (
                        jnp.where(keep, turned[b], turned[b + 1]).reshape(CHUNK, TILE)
                    )
        return carry

    lax.fori_loop(0, 2, cut, 0)
    for copy in copies[near:operands]:
        copy.wait()

    def forward(image, carry):
        scan, mode = image // 2, image % 2
        for piece in range(SIDE // CHUNK):
            rows = pl.ds(piece * CHUNK, CHUNK)
            p_re, p_im = probe_rows(0, mode, piece), probe_rows(1, mode, piece)
            w_re, w_im = windows[scan, 0, rows, :], windows[scan, 1, rows, :]
            e_re = p_re * w_re - p_im * w_im
            e_im = p_re * w_im + p_im * w_re
            for parity in range(2):
                sign = 1.0 if parity == 0 else -1.0
                for part, value in enumerate((e_re, e_im)):
                    half = value[:, :HALF] + sign * value[:, HALF:]
                    high, low = split(half)
                    folded[parity, 0, rows, part * HALF : (part + 1) * HALF] = high
                    folded[parity, 1, rows, part * HALF : (part + 1) * HALF] = low
        for parity in range(2):
            out = (
                dot(folded[parity, 1], table_ref[parity, 1, 0])
                + dot(folded[parity, 0], table_ref[parity, 1, 1])
                + dot(folded[parity, 0], table_ref[parity, 1, 0])
            )
            for other in range(2):
                sign = 1.0 if other == 0 else -1.0
                half = out[:HALF] + sign * out[HALF:]
                high, low = split(half)
                place = pl.ds(parity * HALF, HALF)
                stacked[other, 0, 0:HALF, place] = high[:, :HALF]
                stacked[other, 0, HALF:, place] = high[:, HALF:]
                stacked[other, 1, 0:HALF, place] = low[:, :HALF]
                stacked[other, 1, HALF:, place] = low[:, HALF:]
        for other in range(2):
            far[image, other] = (
                dot(table_ref[other, 0, 0], stacked[other, 1])
                + dot(table_ref[other, 0, 1], stacked[other, 0])
                + dot(table_ref[other, 0, 0], stacked[other, 0])
            )
        return carry

    lax.fori_loop(0, 4, forward, 0)

    def scale(index, carry):
        scan, other = index // 2, index % 2
        for piece in range(HALF // 32):
            upper, lower = pl.ds(piece * 32, 32), pl.ds(HALF + piece * 32, 32)
            parts = [
                far[2 * scan + mode, other, rows, :] for mode in range(2) for rows in (upper, lower)
            ]
            intensity = (parts[0] * parts[0] + parts[1] * parts[1]) + (
                parts[2] * parts[2] + parts[3] * parts[3]
            )
            measured = measured_ref[scan, other, upper, :]
            factor = measured / jnp.maximum(jnp.sqrt(intensity), FLOOR) - 1.0
            for mode in range(2):
                far[2 * scan + mode, other, upper, :] = parts[2 * mode] * factor
                far[2 * scan + mode, other, lower, :] = parts[2 * mode + 1] * factor
        return carry

    copies[operands].wait()
    lax.fori_loop(0, 4, scale, 0)

    def backward(image, carry):
        scan, mode = image // 2, image % 2
        halves = []
        for other in range(2):
            high, low = split(far[image, other])
            halves.append(
                dot(table_ref[other, 1, 0], low)
                + dot(table_ref[other, 1, 1], high)
                + dot(table_ref[other, 1, 0], high)
            )
        for place, value in ((0, halves[0] + halves[1]), (HALF, halves[0] - halves[1])):
            high, low = split(value)
            for parity in range(2):
                columns = slice(parity * HALF, (parity + 1) * HALF)
                for part in range(2):
                    rows = slice(part * HALF, (part + 1) * HALF)
                    target = pl.ds(part * HALF, HALF)
                    folded[parity, 0, pl.ds(place, HALF), target] = high[rows, columns]
                    folded[parity, 1, pl.ds(place, HALF), target] = low[rows, columns]
        for parity in range(2):
            back[parity] = (
                dot(folded[parity, 1], table_ref[parity, 0, 0])
                + dot(folded[parity, 0], table_ref[parity, 0, 1])
                + dot(folded[parity, 0], table_ref[parity, 0, 0])
            )
        first_scan, first_mode = scan == 0, mode == 0
        for piece in range(SIDE // CHUNK):
            rows = pl.ds(piece * CHUNK, CHUNK)
            even, odd = back[0, rows, :], back[1, rows, :]
            for b in range(2):
                columns = pl.ds(b * HALF, HALF)
                sign = 1.0 if b == 0 else -1.0
                b_re = even[:, :HALF] + sign * odd[:, :HALF]
                b_im = even[:, HALF:] + sign * odd[:, HALF:]
                p_re = probe_rows(0, mode, piece, columns)
                p_im = probe_rows(1, mode, piece, columns)
                w_re, w_im = windows[scan, 0, rows, columns], windows[scan, 1, rows, columns]
                o_re = p_re * b_re + p_im * b_im
                o_im = p_re * b_im - p_im * b_re
                zero = jnp.zeros_like(o_re)
                contrib[scan, 0, rows, columns] = o_re + jnp.where(
                    first_mode, zero, contrib[scan, 0, rows, columns]
                )
                contrib[scan, 1, rows, columns] = o_im + jnp.where(
                    first_mode, zero, contrib[scan, 1, rows, columns]
                )
                g_re = w_re * b_re + w_im * b_im
                g_im = w_re * b_im - w_im * b_re
                for slot in range(CHUNK // 8):
                    group = piece * (CHUNK // 8) + slot
                    inner = slice(slot * 8, slot * 8 + 8)
                    for part, value in enumerate((g_re, g_im)):
                        place = 2 * part + mode
                        old = sums[group, place, :, columns]
                        sums[group, place, :, columns] = value[inner] + jnp.where(
                            first_scan, jnp.zeros_like(old), old
                        )

        return carry

    for piece in range(SIDE // CHUNK):
        rows = pl.ds(piece * CHUNK, CHUNK)
        power = None
        for mode in range(2):
            for part in range(2):
                value = probe_rows(part, mode, piece)
                power = value * value if power is None else power + value * value
        power_ref[rows, :] = power
        weight = None
        for scan in range(2):
            for part in range(2):
                value = windows[scan, part, rows, :]
                weight = value * value if weight is None else weight + value * value
        for slot in range(CHUNK // 8):
            sums[piece * (CHUNK // 8) + slot, 4] = weight[slot * 8 : slot * 8 + 8]

    lax.fori_loop(0, 4, backward, 0)

    def scatter(scan, carry):
        row, column = offsets_ref[0, 0, scan, 0] + HALF, offsets_ref[0, 0, scan, 1] + HALF
        inner = lax.rem(row, 8)
        base = pl.multiple_of(row - inner, 8)
        turn, keep = lax.rem(column, TILE), lane >= column
        zero = jnp.zeros((CHUNK // 8, 8, TILE), F32)
        edge = jnp.zeros((1, 8, TILE), F32)
        stay = lax.broadcasted_iota(jnp.int32, (CHUNK // 8 + 1, 8, TILE), 1) >= inner
        for channel in range(3):
            for piece in range(SIDE // CHUNK):
                halves = []
                for b in range(2):
                    value = (power_ref if channel == 2 else contrib.at[scan, channel])[
                        pl.ds(piece * CHUNK, CHUNK), pl.ds(b * TILE, TILE)
                    ]
                    halves.append(pltpu.roll(value.reshape(CHUNK // 8, 8, TILE), turn, 2))
                thirds = (
                    jnp.where(keep, halves[0], zero),
                    jnp.where(keep, halves[1], halves[0]),
                    jnp.where(keep, zero, halves[1]),
                )
                place = pl.ds(base + piece * CHUNK, CHUNK + 8)
                for b in range(3):
                    value = pltpu.roll(thirds[b], inner, 1)
                    value = jnp.where(
                        stay,
                        jnp.concatenate([value, edge]),
                        jnp.concatenate([edge, value]),
                    )
                    total[channel, place, pl.ds(b * TILE, TILE)] += value.reshape(CHUNK + 8, TILE)
        return carry

    done = len(copies)
    start(sums.at[pl.ds(core * GROUPS, GROUPS)], mine_out)
    start(sums.at[pl.ds((1 - core) * GROUPS, GROUPS)], other_out)
    lax.fori_loop(0, 2, scatter, 0)
    for block, ref in enumerate((grad_second, grad_middle, grad_first)):
        for column in range(3):
            start(total.at[:, third(across[block]), third(along[column])], ref.at[column])
    for copy in copies[done:]:
        copy.wait()


def spread_kernel(pieces_ref, out_ref):
    total = pieces_ref[0]
    for piece in range(1, GROUPS):
        total = total + pieces_ref[piece]
    for copy in range(DEPTH):
        out_ref[copy] = total


def update_kernel(pieces_ref, old_ref, out_ref, new_ref):
    total = pieces_ref[0]
    for piece in range(1, DEPTH):
        total = total + pieces_ref[piece]
    new = old_ref[...] + PROBE_STEP * total[:4] / (total[4:] + PROBE_REG)
    new_ref[...] = new
    for copy in range(GROUPS):
        out_ref[copy] = new


VMEM_SPEC = pl.BlockSpec(memory_space=pltpu.VMEM)
SMEM_SPEC = pl.BlockSpec(memory_space=pltpu.SMEM)
ANY_SPEC = pl.BlockSpec(memory_space=pl.ANY)


def in_hbm(value):
    return pltpu.with_memory_space_constraint(value, pltpu.HBM)


def params(mebibytes):
    return pltpu.CompilerParams(vmem_limit_bytes=mebibytes * 2**20)


def sort_measured(measured):
    return pl.pallas_call(
        sort_kernel,
        out_shape=jax.ShapeDtypeStruct((2, 2, HALF, SIDE), F32),
        in_specs=[VMEM_SPEC],
        out_specs=VMEM_SPEC,
        compiler_params=params(8),
        name="sort_measured",
    )(measured)


def step(offsets, parity, table, probe, measured, around):
    halves = len(probe) - 1
    band = jax.ShapeDtypeStruct((3, 3, TILE, TILE), F32)
    half = jax.ShapeDtypeStruct((GROUPS, 5, 8, SIDE), F32)
    return pl.pallas_call(
        functools.partial(step_kernel, halves),
        out_shape=[half, half, band, band, band],
        in_specs=[SMEM_SPEC, SMEM_SPEC] + [ANY_SPEC] * (8 + halves),
        out_specs=[ANY_SPEC] * 5,
        scratch_shapes=[
            pltpu.VMEM(table.shape, BF16),
            pltpu.VMEM((4, 2 * GROUPS, 8, SIDE), F32),
            pltpu.VMEM(measured.shape, F32),
            pltpu.VMEM((2, WIDE + 8, WIDE), F32),
            pltpu.VMEM((2, 2, SIDE, SIDE), F32),
            pltpu.VMEM((2, 2, SIDE, SIDE), BF16),
            pltpu.VMEM((2, 2, SIDE, SIDE), BF16),
            pltpu.VMEM((4, 2, SIDE, SIDE), F32),
            pltpu.VMEM((2, SIDE, SIDE), F32),
            pltpu.VMEM((2, 2, SIDE, SIDE), F32),
            pltpu.VMEM((SIDE, SIDE), F32),
            pltpu.VMEM((3, WIDE + 8, WIDE), F32),
            pltpu.VMEM((2 * GROUPS, 5, 8, SIDE), F32),
            pltpu.SemaphoreType.DMA((32,)),
        ],
        compiler_params=params(20),
        name="step",
    )(offsets, parity, table, *probe, measured, *around)


def pairs(first):
    both = [(i, i + 1) for i in range(first, 15, 2)]
    return both + [(j, i) for i, j in both]


def neighbourhood(tile):
    inner = lax.ppermute(tile, "col", pairs(0))
    outer = lax.ppermute(tile, "col", pairs(1))
    band = jnp.stack([outer, tile, inner])
    first = lax.ppermute(band, "row", pairs(0))
    second = lax.ppermute(band, "row", pairs(1))
    return outer, tile, inner, second, first


def after(value, other):
    return lax.optimization_barrier((value, other))[0]


def places(device):
    row, column = divmod(device, 16)
    return (column // 8) * 4 + row // 4, row % 4, column // 2 % 4, column % 2


def grouped(key):
    groups = {}
    for device in range(256):
        groups.setdefault(key(*places(device)), []).append(device)
    return list(groups.values())


PLANES = grouped(lambda z, y, x, core: (z, core))
LINES = grouped(lambda z, y, x, core: (y, x, core))
BOTH = ("row", "col")
SWAP = [(i, i ^ 1) for i in range(16)]


def exchange(value, groups):
    return lax.all_to_all(value, BOTH, 0, 0, axis_index_groups=groups, tiled=True)


def spread(pieces):
    return pl.pallas_call(
        spread_kernel,
        out_shape=jax.ShapeDtypeStruct((DEPTH, 5, 8, SIDE), F32),
        compiler_params=params(8),
        name="spread",
    )(pieces)


def update(pieces, old):
    return pl.pallas_call(
        update_kernel,
        out_shape=[
            jax.ShapeDtypeStruct((GROUPS, 4, 8, SIDE), F32),
            jax.ShapeDtypeStruct((4, 8, SIDE), F32),
        ],
        compiler_params=params(8),
        name="update",
    )(pieces, old)


def local(object_field, probe, amplitudes, offsets):
    table = in_hbm(jnp.asarray(tables()))
    row, column = lax.axis_index("row"), lax.axis_index("col")
    core = column & 1
    group = core * GROUPS + (row & 3) * 4 + (lax.shift_right_logical(column, 1) & 3)
    probe = probe.reshape(4, 2 * GROUPS, 8, SIDE)
    old = lax.dynamic_index_in_dim(probe, group, 1, False)
    parity = jnp.stack([row & 1, core])
    measured = sort_measured(amplitudes[0, 0])
    parts = (in_hbm(probe),)
    tile = object_field
    for iteration in range(ITERS):
        mine, other, second, middle, first = step(
            offsets, parity, table, parts, measured, neighbourhood(tile)
        )
        first = lax.ppermute(first, "row", pairs(0))
        second = lax.ppermute(second, "row", pairs(1))
        mine = mine + lax.ppermute(other, "col", SWAP)
        pieces = exchange(mine, PLANES)
        outer, own, inner = (middle[i] + first[i] + second[i] for i in range(3))
        pieces = spread(after(pieces, (outer, own, inner)))
        inner = lax.ppermute(after(inner, pieces), "col", pairs(0))
        outer = lax.ppermute(after(outer, pieces), "col", pairs(1))
        pieces = exchange(pieces, LINES)
        pieces, old = update(pieces, old)
        totals = after(own, old) + inner + outer
        tile = tile + OBJECT_STEP * totals[0:2] / (totals[2:3] + OBJECT_REG)
        mine = exchange(pieces, PLANES)
        parts = (mine, lax.ppermute(mine, "col", SWAP))
    probe = pl.pallas_call(
        lay_out_kernel,
        out_shape=jax.ShapeDtypeStruct((4, 2 * GROUPS, 8, SIDE), F32),
        in_specs=[SMEM_SPEC, VMEM_SPEC, VMEM_SPEC],
        out_specs=VMEM_SPEC,
        compiler_params=params(8),
        name="lay_out",
    )(parity, *parts)
    return (tile, probe.reshape(2, 2, SIDE, SIDE))


def solution(mesh):
    return jax.shard_map(
        local,
        mesh=mesh,
        in_specs=(
            P(None, "row", "col"),
            P(),
            P("row", "col", None, None, None),
            P("row", "col", None, None),
        ),
        out_specs=(P(None, "row", "col"), P()),
        check_vma=False,
    )
```

```python
import functools
import math

import jax
import jax.numpy as jnp
import ml_dtypes
import numpy as np
from jax import lax
from jax.experimental import pallas as pl
from jax.experimental.pallas import tpu as pltpu
from jax.sharding import PartitionSpec as P

ITERS = 2
FLOOR = 0.5
OBJECT_STEP = 0.5
OBJECT_REG = 0.5
PROBE_STEP = 1.0
PROBE_REG = 1.0
TILE = 128
SIDE = 256
HALF = SIDE // 2
WIDE = 3 * TILE
CHUNK = 64
GROUPS = 16
DEPTH = 8
F32 = jnp.float32
BF16 = jnp.bfloat16


def split_np(table):
    high = table.astype(np.float32).astype(ml_dtypes.bfloat16)
    low = (table - high.astype(np.float64)).astype(np.float32).astype(ml_dtypes.bfloat16)
    return np.stack([high, low])


def tables():
    out = []
    for parity in range(2):
        u = 2 * np.arange(HALF)[:, None] + parity
        angle = 2.0 * math.pi * ((u * np.arange(HALF)[None, :]) % SIDE) / SIDE
        cos, sin = np.cos(angle) / 16.0, np.sin(angle) / 16.0
        forward = np.block([[cos, sin], [-sin, cos]])
        out.append(np.stack([split_np(forward), split_np(forward.T)]))
    return np.stack(out)


def split(x):
    high = x.astype(BF16)
    return high, (x - high.astype(F32)).astype(BF16)


def split_whole(x):
    high = x.astype(BF16)
    rest = x - high.astype(F32)
    middle = rest.astype(BF16)
    return high, middle, (rest - middle.astype(F32)).astype(BF16)


def dot(a, b):
    return jnp.dot(a, b, preferred_element_type=F32)


def sort_kernel(measured_ref, out_ref):
    source = lax.broadcasted_iota(jnp.int32, (SIDE, SIDE), 0)
    place = lax.broadcasted_iota(jnp.int32, (SIDE, SIDE), 1)
    wanted = jnp.where(place < HALF, 2 * place, 2 * place - (SIDE - 1))
    select = jnp.where(source == wanted, 1.0, 0.0).astype(BF16)
    wanted = jnp.where(source < HALF, 2 * source, 2 * source - (SIDE - 1))
    select_rows = jnp.where(place == wanted, 1.0, 0.0).astype(BF16)
    for scan in range(2):
        high, middle, low = split_whole(measured_ref[scan])
        turned = (dot(low, select) + dot(middle, select)) + dot(high, select)
        high, middle, low = split_whole(turned)
        turned = (dot(select_rows, low) + dot(select_rows, middle)) + dot(select_rows, high)
        out_ref[scan, 0] = turned[:HALF]
        out_ref[scan, 1] = turned[HALF:]


def lay_out_kernel(parity_ref, mine_ref, other_ref, out_ref):
    for half, ref in enumerate((mine_ref, other_ref)):
        place = parity_ref[1] if half == 0 else 1 - parity_ref[1]
        for part in range(4):
            out_ref[part, pl.ds(place * GROUPS, GROUPS)] = ref[:, part]


def step_kernel(halves, offsets_ref, parity_ref, table_in, *refs):
    probe_in, refs = refs[: 1 + halves], refs[1 + halves :]
    (
        measured_in,
        second_in,
        tile_in,
        first_in,
        outer_in,
        inner_in,
        mine_out,
        other_out,
        grad_second,
        grad_middle,
        grad_first,
        table_ref,
        probe,
        measured_ref,
        padded,
        windows,
        folded,
        stacked,
        far,
        back,
        contrib,
        power_ref,
        total,
        sums,
        semaphores,
    ) = refs
    row_parity, core = parity_ref[0], parity_ref[1]
    across = (row_parity * 2, 1, 2 - row_parity * 2)
    along = (core * 2, 1, 2 - core * 2)
    copies = []

    def start(source, target):
        copy = pltpu.make_async_copy(source, target, semaphores.at[len(copies)])
        copy.start()
        copies.append(copy)

    def third(block):
        return pl.ds(pl.multiple_of(block * TILE, TILE), TILE)

    for place, piece in enumerate((second_in, tile_in, first_in)):
        rows = third(across[place])
        start(piece, padded.at[:, rows, third(1)])
        start(outer_in.at[place], padded.at[:, rows, third(along[0])])
        start(inner_in.at[place], padded.at[:, rows, third(along[2])])
    near = len(copies)
    if halves:
        for half, ref in enumerate(probe_in):
            place = core if half == 0 else 1 - core
            for part in range(4):
                start(ref.at[:, part], probe.at[part, pl.ds(place * GROUPS, GROUPS)])
    else:
        start(probe_in[0], probe)
    start(table_in, table_ref)
    operands = len(copies)
    start(measured_in, measured_ref)

    def probe_rows(part, mode, piece, columns=slice(None)):
        groups = pl.ds(piece * (CHUNK // 8), CHUNK // 8)
        value = probe[2 * part + mode, groups, :, columns]
        return value.reshape(CHUNK, value.shape[-1])

    lane = lax.broadcasted_iota(jnp.int32, (CHUNK // 8, 8, TILE), 2)
    sublane = lax.broadcasted_iota(jnp.int32, (CHUNK // 8, 8, TILE), 1)
    for channel in range(3):
        total[channel] = jnp.zeros((WIDE + 8, WIDE), F32)
    for copy in copies[:near]:
        copy.wait()

    def cut(scan, carry):
        row, column = offsets_ref[0, 0, scan, 0] + HALF, offsets_ref[0, 0, scan, 1] + HALF
        inner = lax.rem(row, 8)
        base = pl.multiple_of(row - inner, 8)
        turn, keep = lax.rem(TILE - column, TILE), lane < TILE - column
        lift, stay = lax.rem(8 - inner, 8), sublane < 8 - inner
        for channel in range(2):
            for piece in range(SIDE // CHUNK):
                turned = []
                for b in range(3):
                    rows = padded[channel, pl.ds(base + piece * CHUNK, CHUNK + 8), pl.ds(b * TILE, TILE)]
                    rows = pltpu.roll(rows.reshape(CHUNK // 8 + 1, 8, TILE), lift, 1)
                    rows = jnp.where(stay, rows[:-1], rows[1:])
                    turned.append(pltpu.roll(rows, turn, 2))
                for b in range(2):
                    windows[scan, channel, pl.ds(piece * CHUNK, CHUNK), pl.ds(b * TILE, TILE)] = (
                        jnp.where(keep, turned[b], turned[b + 1]).reshape(CHUNK, TILE)
                    )
        return carry

    lax.fori_loop(0, 2, cut, 0)
    for copy in copies[near:operands]:
        copy.wait()

    def forward(image, carry):
        scan, mode = image // 2, image % 2
        for piece in range(SIDE // CHUNK):
            rows = pl.ds(piece * CHUNK, CHUNK)
            p_re, p_im = probe_rows(0, mode, piece), probe_rows(1, mode, piece)
            w_re, w_im = windows[scan, 0, rows, :], windows[scan, 1, rows, :]
            e_re = p_re * w_re - p_im * w_im
            e_im = p_re * w_im + p_im * w_re
            for parity in range(2):
                sign = 1.0 if parity == 0 else -1.0
                for part, value in enumerate((e_re, e_im)):
                    half = value[:, :HALF] + sign * value[:, HALF:]
                    high, low = split(half)
                    folded[parity, 0, rows, part * HALF : (part + 1) * HALF] = high
                    folded[parity, 1, rows, part * HALF : (part + 1) * HALF] = low
        for parity in range(2):
            out = (
                dot(folded[parity, 1], table_ref[parity, 1, 0])
                + dot(folded[parity, 0], table_ref[parity, 1, 1])
                + dot(folded[parity, 0], table_ref[parity, 1, 0])
            )
            for other in range(2):
                sign = 1.0 if other == 0 else -1.0
                half = out[:HALF] + sign * out[HALF:]
                high, low = split(half)
                place = pl.ds(parity * HALF, HALF)
                stacked[other, 0, 0:HALF, place] = high[:, :HALF]
                stacked[other, 0, HALF:, place] = high[:, HALF:]
                stacked[other, 1, 0:HALF, place] = low[:, :HALF]
                stacked[other, 1, HALF:, place] = low[:, HALF:]
        for other in range(2):
            far[image, other] = (
                dot(table_ref[other, 0, 0], stacked[other, 1])
                + dot(table_ref[other, 0, 1], stacked[other, 0])
                + dot(table_ref[other, 0, 0], stacked[other, 0])
            )
        return carry

    lax.fori_loop(0, 4, forward, 0)

    def scale(index, carry):
        scan, other = index // 2, index % 2
        for piece in range(HALF // 32):
            upper, lower = pl.ds(piece * 32, 32), pl.ds(HALF + piece * 32, 32)
            parts = [
                far[2 * scan + mode, other, rows, :] for mode in range(2) for rows in (upper, lower)
            ]
            intensity = (parts[0] * parts[0] + parts[1] * parts[1]) + (
                parts[2] * parts[2] + parts[3] * parts[3]
            )
            measured = measured_ref[scan, other, upper, :]
            factor = measured / jnp.maximum(jnp.sqrt(intensity), FLOOR) - 1.0
            for mode in range(2):
                far[2 * scan + mode, other, upper, :] = parts[2 * mode] * factor
                far[2 * scan + mode, other, lower, :] = parts[2 * mode + 1] * factor
        return carry

    copies[operands].wait()
    lax.fori_loop(0, 4, scale, 0)

    def backward(image, carry):
        scan, mode = image // 2, image % 2
        halves = []
        for other in range(2):
            high, low = split(far[image, other])
            halves.append(
                dot(table_ref[other, 1, 0], low)
                + dot(table_ref[other, 1, 1], high)
                + dot(table_ref[other, 1, 0], high)
            )
        for place, value in ((0, halves[0] + halves[1]), (HALF, halves[0] - halves[1])):
            high, low = split(value)
            for parity in range(2):
                columns = slice(parity * HALF, (parity + 1) * HALF)
                for part in range(2):
                    rows = slice(part * HALF, (part + 1) * HALF)
                    target = pl.ds(part * HALF, HALF)
                    folded[parity, 0, pl.ds(place, HALF), target] = high[rows, columns]
                    folded[parity, 1, pl.ds(place, HALF), target] = low[rows, columns]
        for parity in range(2):
            back[parity] = (
                dot(folded[parity, 1], table_ref[parity, 0, 0])
                + dot(folded[parity, 0], table_ref[parity, 0, 1])
                + dot(folded[parity, 0], table_ref[parity, 0, 0])
            )
        first_scan, first_mode = scan == 0, mode == 0
        for piece in range(SIDE // CHUNK):
            rows = pl.ds(piece * CHUNK, CHUNK)
            even, odd = back[0, rows, :], back[1, rows, :]
            for b in range(2):
                columns = pl.ds(b * HALF, HALF)
                sign = 1.0 if b == 0 else -1.0
                b_re = even[:, :HALF] + sign * odd[:, :HALF]
                b_im = even[:, HALF:] + sign * odd[:, HALF:]
                p_re = probe_rows(0, mode, piece, columns)
                p_im = probe_rows(1, mode, piece, columns)
                w_re, w_im = windows[scan, 0, rows, columns], windows[scan, 1, rows, columns]
                o_re = p_re * b_re + p_im * b_im
                o_im = p_re * b_im - p_im * b_re
                zero = jnp.zeros_like(o_re)
                contrib[scan, 0, rows, columns] = o_re + jnp.where(
                    first_mode, zero, contrib[scan, 0, rows, columns]
                )
                contrib[scan, 1, rows, columns] = o_im + jnp.where(
                    first_mode, zero, contrib[scan, 1, rows, columns]
                )
                g_re = w_re * b_re + w_im * b_im
                g_im = w_re * b_im - w_im * b_re
                for slot in range(CHUNK // 8):
                    group = piece * (CHUNK // 8) + slot
                    inner = slice(slot * 8, slot * 8 + 8)
                    for part, value in enumerate((g_re, g_im)):
                        place = 2 * part + mode
                        old = sums[group, place, :, columns]
                        sums[group, place, :, columns] = value[inner] + jnp.where(
                            first_scan, jnp.zeros_like(old), old
                        )

        return carry

    for piece in range(SIDE // CHUNK):
        rows = pl.ds(piece * CHUNK, CHUNK)
        power = None
        for mode in range(2):
            for part in range(2):
                value = probe_rows(part, mode, piece)
                power = value * value if power is None else power + value * value
        power_ref[rows, :] = power
        weight = None
        for scan in range(2):
            for part in range(2):
                value = windows[scan, part, rows, :]
                weight = value * value if weight is None else weight + value * value
        for slot in range(CHUNK // 8):
            sums[piece * (CHUNK // 8) + slot, 4] = weight[slot * 8 : slot * 8 + 8]

    lax.fori_loop(0, 4, backward, 0)

    def scatter(scan, carry):
        row, column = offsets_ref[0, 0, scan, 0] + HALF, offsets_ref[0, 0, scan, 1] + HALF
        inner = lax.rem(row, 8)
        base = pl.multiple_of(row - inner, 8)
        turn, keep = lax.rem(column, TILE), lane >= column
        zero = jnp.zeros((CHUNK // 8, 8, TILE), F32)
        edge = jnp.zeros((1, 8, TILE), F32)
        stay = lax.broadcasted_iota(jnp.int32, (CHUNK // 8 + 1, 8, TILE), 1) >= inner
        for channel in range(3):
            for piece in range(SIDE // CHUNK):
                halves = []
                for b in range(2):
                    value = (power_ref if channel == 2 else contrib.at[scan, channel])[
                        pl.ds(piece * CHUNK, CHUNK), pl.ds(b * TILE, TILE)
                    ]
                    halves.append(pltpu.roll(value.reshape(CHUNK // 8, 8, TILE), turn, 2))
                thirds = (
                    jnp.where(keep, halves[0], zero),
                    jnp.where(keep, halves[1], halves[0]),
                    jnp.where(keep, zero, halves[1]),
                )
                place = pl.ds(base + piece * CHUNK, CHUNK + 8)
                for b in range(3):
                    value = pltpu.roll(thirds[b], inner, 1)
                    value = jnp.where(
                        stay,
                        jnp.concatenate([value, edge]),
                        jnp.concatenate([edge, value]),
                    )
                    total[channel, place, pl.ds(b * TILE, TILE)] += value.reshape(CHUNK + 8, TILE)
        return carry

    done = len(copies)
    start(sums.at[pl.ds(core * GROUPS, GROUPS)], mine_out)
    start(sums.at[pl.ds((1 - core) * GROUPS, GROUPS)], other_out)
    lax.fori_loop(0, 2, scatter, 0)
    for block, ref in enumerate((grad_second, grad_middle, grad_first)):
        for column in range(3):
            start(total.at[:, third(across[block]), third(along[column])], ref.at[column])
    for copy in copies[done:]:
        copy.wait()


def spread_kernel(pieces_ref, out_ref):
    total = pieces_ref[0]
    for piece in range(1, GROUPS):
        total = total + pieces_ref[piece]
    for copy in range(DEPTH):
        out_ref[copy] = total


def update_kernel(pieces_ref, old_ref, out_ref, new_ref):
    total = pieces_ref[0]
    for piece in range(1, DEPTH):
        total = total + pieces_ref[piece]
    new = old_ref[...] + PROBE_STEP * total[:4] / (total[4:] + PROBE_REG)
    new_ref[...] = new
    for copy in range(GROUPS):
        out_ref[copy] = new


VMEM_SPEC = pl.BlockSpec(memory_space=pltpu.VMEM)
SMEM_SPEC = pl.BlockSpec(memory_space=pltpu.SMEM)
ANY_SPEC = pl.BlockSpec(memory_space=pl.ANY)


def in_hbm(value):
    return pltpu.with_memory_space_constraint(value, pltpu.HBM)


def params(mebibytes):
    return pltpu.CompilerParams(vmem_limit_bytes=mebibytes * 2**20)


def sort_measured(measured):
    return pl.pallas_call(
        sort_kernel,
        out_shape=jax.ShapeDtypeStruct((2, 2, HALF, SIDE), F32),
        in_specs=[VMEM_SPEC],
        out_specs=VMEM_SPEC,
        compiler_params=params(8),
        name="sort_measured",
    )(measured)


def step(offsets, parity, table, probe, measured, around):
    halves = len(probe) - 1
    band = jax.ShapeDtypeStruct((3, 3, TILE, TILE), F32)
    half = jax.ShapeDtypeStruct((GROUPS, 5, 8, SIDE), F32)
    return pl.pallas_call(
        functools.partial(step_kernel, halves),
        out_shape=[half, half, band, band, band],
        in_specs=[SMEM_SPEC, SMEM_SPEC] + [ANY_SPEC] * (8 + halves),
        out_specs=[ANY_SPEC] * 5,
        scratch_shapes=[
            pltpu.VMEM(table.shape, BF16),
            pltpu.VMEM((4, 2 * GROUPS, 8, SIDE), F32),
            pltpu.VMEM(measured.shape, F32),
            pltpu.VMEM((2, WIDE + 8, WIDE), F32),
            pltpu.VMEM((2, 2, SIDE, SIDE), F32),
            pltpu.VMEM((2, 2, SIDE, SIDE), BF16),
            pltpu.VMEM((2, 2, SIDE, SIDE), BF16),
            pltpu.VMEM((4, 2, SIDE, SIDE), F32),
            pltpu.VMEM((2, SIDE, SIDE), F32),
            pltpu.VMEM((2, 2, SIDE, SIDE), F32),
            pltpu.VMEM((SIDE, SIDE), F32),
            pltpu.VMEM((3, WIDE + 8, WIDE), F32),
            pltpu.VMEM((2 * GROUPS, 5, 8, SIDE), F32),
            pltpu.SemaphoreType.DMA((32,)),
        ],
        compiler_params=params(20),
        name="step",
    )(offsets, parity, table, *probe, measured, *around)


def pairs(first):
    both = [(i, i + 1) for i in range(first, 15, 2)]
    return both + [(j, i) for i, j in both]


def neighbourhood(tile):
    first = lax.ppermute(tile, "row", pairs(0))
    second = lax.ppermute(tile, "row", pairs(1))
    band = jnp.stack([second, tile, first])
    inner = lax.ppermute(band, "col", pairs(0))
    outer = lax.ppermute(band, "col", pairs(1))
    return second, tile, first, outer, inner


def after(value, other):
    return lax.optimization_barrier((value, other))[0]


def places(device):
    row, column = divmod(device, 16)
    return (column // 8) * 4 + row // 4, row % 4, column // 2 % 4, column % 2


def grouped(key):
    groups = {}
    for device in range(256):
        groups.setdefault(key(*places(device)), []).append(device)
    return list(groups.values())


PLANES = grouped(lambda z, y, x, core: (z, core))
LINES = grouped(lambda z, y, x, core: (y, x, core))
BOTH = ("row", "col")
SWAP = [(i, i ^ 1) for i in range(16)]


def exchange(value, groups):
    return lax.all_to_all(value, BOTH, 0, 0, axis_index_groups=groups, tiled=True)


def spread(pieces):
    return pl.pallas_call(
        spread_kernel,
        out_shape=jax.ShapeDtypeStruct((DEPTH, 5, 8, SIDE), F32),
        compiler_params=params(8),
        name="spread",
    )(pieces)


def update(pieces, old):
    return pl.pallas_call(
        update_kernel,
        out_shape=[
            jax.ShapeDtypeStruct((GROUPS, 4, 8, SIDE), F32),
            jax.ShapeDtypeStruct((4, 8, SIDE), F32),
        ],
        compiler_params=params(8),
        name="update",
    )(pieces, old)


def local(object_field, probe, amplitudes, offsets):
    table = in_hbm(jnp.asarray(tables()))
    row, column = lax.axis_index("row"), lax.axis_index("col")
    core = column & 1
    group = core * GROUPS + (row & 3) * 4 + (lax.shift_right_logical(column, 1) & 3)
    probe = probe.reshape(4, 2 * GROUPS, 8, SIDE)
    old = lax.dynamic_index_in_dim(probe, group, 1, False)
    parity = jnp.stack([row & 1, core])
    measured = sort_measured(amplitudes[0, 0])
    parts = (in_hbm(probe),)
    tile = object_field
    for iteration in range(ITERS):
        mine, other, second, middle, first = step(
            offsets, parity, table, parts, measured, neighbourhood(tile)
        )
        first = lax.ppermute(first, "row", pairs(0))
        second = lax.ppermute(second, "row", pairs(1))
        mine = mine + lax.ppermute(other, "col", SWAP)
        pieces = exchange(mine, PLANES)
        outer, own, inner = (middle[i] + first[i] + second[i] for i in range(3))
        pieces = spread(after(pieces, (outer, own, inner)))
        inner = lax.ppermute(after(inner, pieces), "col", pairs(0))
        outer = lax.ppermute(after(outer, pieces), "col", pairs(1))
        pieces = exchange(pieces, LINES)
        pieces, old = update(pieces, old)
        totals = after(own, old) + inner + outer
        tile = tile + OBJECT_STEP * totals[0:2] / (totals[2:3] + OBJECT_REG)
        mine = exchange(pieces, PLANES)
        parts = (mine, lax.ppermute(mine, "col", SWAP))
    probe = pl.pallas_call(
        lay_out_kernel,
        out_shape=jax.ShapeDtypeStruct((4, 2 * GROUPS, 8, SIDE), F32),
        in_specs=[SMEM_SPEC, VMEM_SPEC, VMEM_SPEC],
        out_specs=VMEM_SPEC,
        compiler_params=params(8),
        name="lay_out",
    )(parity, *parts)
    return (tile, probe.reshape(2, 2, SIDE, SIDE))


def solution(mesh):
    return jax.shard_map(
        local,
        mesh=mesh,
        in_specs=(
            P(None, "row", "col"),
            P(),
            P("row", "col", None, None, None),
            P("row", "col", None, None),
        ),
        out_specs=(P(None, "row", "col"), P()),
        check_vma=False,
    )
```

```python
import functools
import math

import jax
import jax.numpy as jnp
import ml_dtypes
import numpy as np
from jax import lax
from jax.experimental import pallas as pl
from jax.experimental.pallas import tpu as pltpu
from jax.sharding import PartitionSpec as P

ITERS = 2
FLOOR = 0.5
OBJECT_STEP = 0.5
OBJECT_REG = 0.5
PROBE_STEP = 1.0
PROBE_REG = 1.0
TILE = 128
SIDE = 256
HALF = SIDE // 2
WIDE = 3 * TILE
CHUNK = 64
GROUPS = 16
DEPTH = 8
SHIFT = TILE + 1
F32 = jnp.float32
BF16 = jnp.bfloat16


def split_np(table):
    high = table.astype(np.float32).astype(ml_dtypes.bfloat16)
    low = (table - high.astype(np.float64)).astype(np.float32).astype(ml_dtypes.bfloat16)
    return np.stack([high, low])


def tables():
    out = []
    for parity in range(2):
        u = 2 * np.arange(HALF)[:, None] + parity
        angle = 2.0 * math.pi * ((u * np.arange(HALF)[None, :]) % SIDE) / SIDE
        cos, sin = np.cos(angle) / 16.0, np.sin(angle) / 16.0
        forward = np.block([[cos, sin], [-sin, cos]])
        out.append(np.stack([split_np(forward), split_np(forward.T)]))
    return np.stack(out)


def split(x):
    high = x.astype(BF16)
    return high, (x - high.astype(F32)).astype(BF16)


def split_whole(x):
    high = x.astype(BF16)
    rest = x - high.astype(F32)
    middle = rest.astype(BF16)
    return high, middle, (rest - middle.astype(F32)).astype(BF16)


def dot(a, b):
    return jnp.dot(a, b, preferred_element_type=F32)


def sort_kernel(measured_ref, out_ref):
    source = lax.broadcasted_iota(jnp.int32, (SIDE, SIDE), 0)
    place = lax.broadcasted_iota(jnp.int32, (SIDE, SIDE), 1)
    wanted = jnp.where(place < HALF, 2 * place, 2 * place - (SIDE - 1))
    select = jnp.where(source == wanted, 1.0, 0.0).astype(BF16)
    wanted = jnp.where(source < HALF, 2 * source, 2 * source - (SIDE - 1))
    select_rows = jnp.where(place == wanted, 1.0, 0.0).astype(BF16)
    for scan in range(2):
        high, middle, low = split_whole(measured_ref[scan])
        turned = (dot(low, select) + dot(middle, select)) + dot(high, select)
        high, middle, low = split_whole(turned)
        turned = (dot(select_rows, low) + dot(select_rows, middle)) + dot(select_rows, high)
        out_ref[scan, 0] = turned[:HALF]
        out_ref[scan, 1] = turned[HALF:]


def lay_out_kernel(parity_ref, mine_ref, other_ref, out_ref):
    for half, ref in enumerate((mine_ref, other_ref)):
        place = parity_ref[1] if half == 0 else 1 - parity_ref[1]
        for part in range(4):
            out_ref[part, pl.ds(place * GROUPS, GROUPS)] = ref[:, part]


def step_kernel(halves, offsets_ref, parity_ref, table_in, *refs):
    probe_in, refs = refs[: 1 + halves], refs[1 + halves :]
    (
        measured_in,
        outer_in,
        tile_in,
        inner_in,
        second_in,
        first_in,
        mine_out,
        other_out,
        grad_second,
        grad_middle,
        grad_first,
        power_out,
        table_ref,
        probe,
        measured_ref,
        padded,
        windows,
        folded,
        stacked,
        far,
        back,
        contrib,
        total,
        sums,
        semaphores,
    ) = refs
    row_parity, core = parity_ref[0], parity_ref[1]
    across = (row_parity * 2, 1, 2 - row_parity * 2)
    along = (core * 2, 1, 2 - core * 2)
    copies = []

    def start(source, target):
        copy = pltpu.make_async_copy(source, target, semaphores.at[len(copies)])
        copy.start()
        copies.append(copy)

    def third(block):
        return pl.ds(block * TILE if isinstance(block, int) else pl.multiple_of(block * TILE, TILE), TILE)

    for place, piece in enumerate((outer_in, tile_in, inner_in)):
        columns = third(along[place])
        start(piece.at[:, third(0)], padded.at[:, third(1), columns])
        start(second_in.at[place, :, third(0)], padded.at[:, third(across[0]), columns])
        start(first_in.at[place, :, third(0)], padded.at[:, third(across[2]), columns])
    near = len(copies)
    if halves:
        for half, ref in enumerate(probe_in):
            place = core if half == 0 else 1 - core
            for part in range(4):
                start(ref.at[:, part], probe.at[part, pl.ds(place * GROUPS, GROUPS)])
    else:
        start(probe_in[0], probe)
    start(table_in, table_ref)
    operands = len(copies)
    start(measured_in, measured_ref)

    def probe_rows(part, mode, piece, columns=slice(None)):
        groups = pl.ds(piece * (CHUNK // 8), CHUNK // 8)
        value = probe[2 * part + mode, groups, :, columns]
        return value.reshape(CHUNK, value.shape[-1])

    lane = lax.broadcasted_iota(jnp.int32, (CHUNK // 8, 8, TILE), 2)
    sublane = lax.broadcasted_iota(jnp.int32, (CHUNK // 8, 8, TILE), 1)
    for channel in range(2):
        total[channel] = jnp.zeros((WIDE + 8, WIDE), F32)
    for copy in copies[:near]:
        copy.wait()

    def cut(scan, carry):
        row, column = offsets_ref[0, 0, scan, 0] + HALF, offsets_ref[0, 0, scan, 1] + HALF
        inner = lax.rem(row, 8)
        base = pl.multiple_of(row - inner, 8)
        turn, keep = lax.rem(TILE - column, TILE), lane < TILE - column
        lift, stay = lax.rem(8 - inner, 8), sublane < 8 - inner
        for channel in range(2):
            for piece in range(SIDE // CHUNK):
                turned = []
                for b in range(3):
                    rows = padded[channel, pl.ds(base + piece * CHUNK, CHUNK + 8), pl.ds(b * TILE, TILE)]
                    rows = pltpu.roll(rows.reshape(CHUNK // 8 + 1, 8, TILE), lift, 1)
                    rows = jnp.where(stay, rows[:-1], rows[1:])
                    turned.append(pltpu.roll(rows, turn, 2))
                for b in range(2):
                    windows[scan, channel, pl.ds(piece * CHUNK, CHUNK), pl.ds(b * TILE, TILE)] = (
                        jnp.where(keep, turned[b], turned[b + 1]).reshape(CHUNK, TILE)
                    )
        return carry

    lax.fori_loop(0, 2, cut, 0)
    for copy in copies[near:operands]:
        copy.wait()

    def forward(image, carry):
        scan, mode = image // 2, image % 2
        for piece in range(SIDE // CHUNK):
            rows = pl.ds(piece * CHUNK, CHUNK)
            p_re, p_im = probe_rows(0, mode, piece), probe_rows(1, mode, piece)
            w_re, w_im = windows[scan, 0, rows, :], windows[scan, 1, rows, :]
            e_re = p_re * w_re - p_im * w_im
            e_im = p_re * w_im + p_im * w_re
            for parity in range(2):
                sign = 1.0 if parity == 0 else -1.0
                for part, value in enumerate((e_re, e_im)):
                    half = value[:, :HALF] + sign * value[:, HALF:]
                    high, low = split(half)
                    folded[parity, 0, rows, part * HALF : (part + 1) * HALF] = high
                    folded[parity, 1, rows, part * HALF : (part + 1) * HALF] = low
        for parity in range(2):
            out = (
                dot(folded[parity, 1], table_ref[parity, 1, 0])
                + dot(folded[parity, 0], table_ref[parity, 1, 1])
                + dot(folded[parity, 0], table_ref[parity, 1, 0])
            )
            for other in range(2):
                sign = 1.0 if other == 0 else -1.0
                half = out[:HALF] + sign * out[HALF:]
                high, low = split(half)
                place = pl.ds(parity * HALF, HALF)
                stacked[other, 0, 0:HALF, place] = high[:, :HALF]
                stacked[other, 0, HALF:, place] = high[:, HALF:]
                stacked[other, 1, 0:HALF, place] = low[:, :HALF]
                stacked[other, 1, HALF:, place] = low[:, HALF:]
        for other in range(2):
            far[image, other] = (
                dot(table_ref[other, 0, 0], stacked[other, 1])
                + dot(table_ref[other, 0, 1], stacked[other, 0])
                + dot(table_ref[other, 0, 0], stacked[other, 0])
            )
        return carry

    lax.fori_loop(0, 4, forward, 0)

    def scale(index, carry):
        scan, other = index // 2, index % 2
        for piece in range(HALF // 32):
            upper, lower = pl.ds(piece * 32, 32), pl.ds(HALF + piece * 32, 32)
            parts = [
                far[2 * scan + mode, other, rows, :] for mode in range(2) for rows in (upper, lower)
            ]
            intensity = (parts[0] * parts[0] + parts[1] * parts[1]) + (
                parts[2] * parts[2] + parts[3] * parts[3]
            )
            measured = measured_ref[scan, other, upper, :]
            factor = measured / jnp.maximum(jnp.sqrt(intensity), FLOOR) - 1.0
            for mode in range(2):
                far[2 * scan + mode, other, upper, :] = parts[2 * mode] * factor
                far[2 * scan + mode, other, lower, :] = parts[2 * mode + 1] * factor
        return carry

    copies[operands].wait()
    lax.fori_loop(0, 4, scale, 0)

    def backward(image, carry):
        scan, mode = image // 2, image % 2
        halves = []
        for other in range(2):
            high, low = split(far[image, other])
            halves.append(
                dot(table_ref[other, 1, 0], low)
                + dot(table_ref[other, 1, 1], high)
                + dot(table_ref[other, 1, 0], high)
            )
        for place, value in ((0, halves[0] + halves[1]), (HALF, halves[0] - halves[1])):
            high, low = split(value)
            for parity in range(2):
                columns = slice(parity * HALF, (parity + 1) * HALF)
                for part in range(2):
                    rows = slice(part * HALF, (part + 1) * HALF)
                    target = pl.ds(part * HALF, HALF)
                    folded[parity, 0, pl.ds(place, HALF), target] = high[rows, columns]
                    folded[parity, 1, pl.ds(place, HALF), target] = low[rows, columns]
        for parity in range(2):
            back[parity] = (
                dot(folded[parity, 1], table_ref[parity, 0, 0])
                + dot(folded[parity, 0], table_ref[parity, 0, 1])
                + dot(folded[parity, 0], table_ref[parity, 0, 0])
            )
        first_scan, first_mode = scan == 0, mode == 0
        for piece in range(SIDE // CHUNK):
            rows = pl.ds(piece * CHUNK, CHUNK)
            even, odd = back[0, rows, :], back[1, rows, :]
            for b in range(2):
                columns = pl.ds(b * HALF, HALF)
                sign = 1.0 if b == 0 else -1.0
                b_re = even[:, :HALF] + sign * odd[:, :HALF]
                b_im = even[:, HALF:] + sign * odd[:, HALF:]
                p_re = probe_rows(0, mode, piece, columns)
                p_im = probe_rows(1, mode, piece, columns)
                w_re, w_im = windows[scan, 0, rows, columns], windows[scan, 1, rows, columns]
                o_re = p_re * b_re + p_im * b_im
                o_im = p_re * b_im - p_im * b_re
                zero = jnp.zeros_like(o_re)
                contrib[scan, 0, rows, columns] = o_re + jnp.where(
                    first_mode, zero, contrib[scan, 0, rows, columns]
                )
                contrib[scan, 1, rows, columns] = o_im + jnp.where(
                    first_mode, zero, contrib[scan, 1, rows, columns]
                )
                g_re = w_re * b_re + w_im * b_im
                g_im = w_re * b_im - w_im * b_re
                for slot in range(CHUNK // 8):
                    group = piece * (CHUNK // 8) + slot
                    inner = slice(slot * 8, slot * 8 + 8)
                    for part, value in enumerate((g_re, g_im)):
                        place = 2 * part + mode
                        old = sums[group, place, :, columns]
                        sums[group, place, :, columns] = value[inner] + jnp.where(
                            first_scan, jnp.zeros_like(old), old
                        )

        return carry

    for piece in range(SIDE // CHUNK):
        rows = pl.ds(piece * CHUNK, CHUNK)
        power = None
        for mode in range(2):
            for part in range(2):
                value = probe_rows(part, mode, piece)
                power = value * value if power is None else power + value * value
        power_out[rows, :] = power
        weight = None
        for scan in range(2):
            for part in range(2):
                value = windows[scan, part, rows, :]
                weight = value * value if weight is None else weight + value * value
        for slot in range(CHUNK // 8):
            sums[piece * (CHUNK // 8) + slot, 4] = weight[slot * 8 : slot * 8 + 8]

    lax.fori_loop(0, 4, backward, 0)

    def scatter(scan, carry):
        row, column = offsets_ref[0, 0, scan, 0] + HALF, offsets_ref[0, 0, scan, 1] + HALF
        inner = lax.rem(row, 8)
        base = pl.multiple_of(row - inner, 8)
        turn, keep = lax.rem(column, TILE), lane >= column
        zero = jnp.zeros((CHUNK // 8, 8, TILE), F32)
        edge = jnp.zeros((1, 8, TILE), F32)
        stay = lax.broadcasted_iota(jnp.int32, (CHUNK // 8 + 1, 8, TILE), 1) >= inner
        for channel in range(2):
            for piece in range(SIDE // CHUNK):
                halves = []
                for b in range(2):
                    value = contrib[scan, channel, pl.ds(piece * CHUNK, CHUNK), pl.ds(b * TILE, TILE)]
                    halves.append(pltpu.roll(value.reshape(CHUNK // 8, 8, TILE), turn, 2))
                thirds = (
                    jnp.where(keep, halves[0], zero),
                    jnp.where(keep, halves[1], halves[0]),
                    jnp.where(keep, zero, halves[1]),
                )
                place = pl.ds(base + piece * CHUNK, CHUNK + 8)
                for b in range(3):
                    value = pltpu.roll(thirds[b], inner, 1)
                    value = jnp.where(
                        stay,
                        jnp.concatenate([value, edge]),
                        jnp.concatenate([edge, value]),
                    )
                    total[channel, place, pl.ds(b * TILE, TILE)] += value.reshape(CHUNK + 8, TILE)
        return carry

    done = len(copies)
    start(sums.at[pl.ds(core * GROUPS, GROUPS)], mine_out)
    start(sums.at[pl.ds((1 - core) * GROUPS, GROUPS)], other_out)
    lax.fori_loop(0, 2, scatter, 0)
    for block, ref in enumerate((grad_second, grad_middle, grad_first)):
        for column in range(3):
            start(total.at[:, third(across[block]), third(along[column])], ref.at[column])
    for copy in copies[done:]:
        copy.wait()


def weigh_kernel(parity_ref, near_ref, power_ref, out_ref, padded):
    padded[...] = jnp.zeros_like(padded)
    padded[pl.ds(TILE, SIDE), pl.ds(TILE, SIDE)] = power_ref[...]
    lane = lax.broadcasted_iota(jnp.int32, (TILE // 8, 8, TILE), 2)
    sublane = lax.broadcasted_iota(jnp.int32, (TILE // 8, 8, TILE), 1)

    def add(index, total):
        place, scan = index // 2, index % 2
        across, along = place // 3, place % 3
        across = 1 + (across - 1) * (1 - 2 * parity_ref[0])
        along = 1 + (along - 1) * (1 - 2 * parity_ref[1])
        row, column = near_ref[place, 2 * scan], near_ref[place, 2 * scan + 1]
        column = jnp.where(row == 0, 0, 2 * TILE - along * TILE - (column - SHIFT))
        row = jnp.where(row == 0, WIDE, 2 * TILE - across * TILE - (row - SHIFT))
        inner = lax.rem(row, 8)
        base = pl.multiple_of(row - inner, 8)
        offset = lax.rem(column, TILE)
        block = pl.multiple_of(column - offset, TILE)
        turned = []
        for b in range(2):
            rows = padded[pl.ds(base, TILE + 8), pl.ds(block + b * TILE, TILE)]
            rows = pltpu.roll(rows.reshape(TILE // 8 + 1, 8, TILE), lax.rem(8 - inner, 8), 1)
            rows = jnp.where(sublane < 8 - inner, rows[:-1], rows[1:])
            turned.append(pltpu.roll(rows, lax.rem(TILE - offset, TILE), 2))
        return total + jnp.where(lane < TILE - offset, turned[0], turned[1])

    total = lax.fori_loop(0, 18, add, jnp.zeros((TILE // 8, 8, TILE), F32))
    out_ref[...] = total.reshape(TILE, TILE)


def spread_kernel(pieces_ref, out_ref):
    total = pieces_ref[0]
    for piece in range(1, GROUPS):
        total = total + pieces_ref[piece]
    for copy in range(DEPTH):
        out_ref[copy] = total


def update_kernel(pieces_ref, old_ref, out_ref, new_ref):
    total = pieces_ref[0]
    for piece in range(1, DEPTH):
        total = total + pieces_ref[piece]
    new = old_ref[...] + PROBE_STEP * total[:4] / (total[4:] + PROBE_REG)
    new_ref[...] = new
    for copy in range(GROUPS):
        out_ref[copy] = new


VMEM_SPEC = pl.BlockSpec(memory_space=pltpu.VMEM)
SMEM_SPEC = pl.BlockSpec(memory_space=pltpu.SMEM)
ANY_SPEC = pl.BlockSpec(memory_space=pl.ANY)


def in_hbm(value):
    return pltpu.with_memory_space_constraint(value, pltpu.HBM)


def params(mebibytes):
    return pltpu.CompilerParams(vmem_limit_bytes=mebibytes * 2**20)


def sort_measured(measured):
    return pl.pallas_call(
        sort_kernel,
        out_shape=jax.ShapeDtypeStruct((2, 2, HALF, SIDE), F32),
        in_specs=[VMEM_SPEC],
        out_specs=VMEM_SPEC,
        compiler_params=params(8),
        name="sort_measured",
    )(measured)


def step(offsets, parity, table, probe, measured, around):
    halves = len(probe) - 1
    band = jax.ShapeDtypeStruct((3, 2, TILE, TILE), F32)
    half = jax.ShapeDtypeStruct((GROUPS, 5, 8, SIDE), F32)
    return pl.pallas_call(
        functools.partial(step_kernel, halves),
        out_shape=[half, half, band, band, band, jax.ShapeDtypeStruct((SIDE, SIDE), F32)],
        in_specs=[SMEM_SPEC, SMEM_SPEC] + [ANY_SPEC] * (8 + halves),
        out_specs=[ANY_SPEC] * 5 + [VMEM_SPEC],
        scratch_shapes=[
            pltpu.VMEM(table.shape, BF16),
            pltpu.VMEM((4, 2 * GROUPS, 8, SIDE), F32),
            pltpu.VMEM(measured.shape, F32),
            pltpu.VMEM((2, WIDE + 8, WIDE), F32),
            pltpu.VMEM((2, 2, SIDE, SIDE), F32),
            pltpu.VMEM((2, 2, SIDE, SIDE), BF16),
            pltpu.VMEM((2, 2, SIDE, SIDE), BF16),
            pltpu.VMEM((4, 2, SIDE, SIDE), F32),
            pltpu.VMEM((2, SIDE, SIDE), F32),
            pltpu.VMEM((2, 2, SIDE, SIDE), F32),
            pltpu.VMEM((2, WIDE + 8, WIDE), F32),
            pltpu.VMEM((2 * GROUPS, 5, 8, SIDE), F32),
            pltpu.SemaphoreType.DMA((32,)),
        ],
        compiler_params=params(20),
        name="step",
    )(offsets, parity, table, *probe, measured, *around)


def pairs(first):
    both = [(i, i + 1) for i in range(first, 15, 2)]
    return both + [(j, i) for i, j in both]


def neighbourhood(tile):
    inner = lax.ppermute(tile, "col", pairs(0))
    outer = lax.ppermute(tile, "col", pairs(1))
    band = jnp.stack([outer, tile, inner])
    first = lax.ppermute(band, "row", pairs(0))
    second = lax.ppermute(band, "row", pairs(1))
    return outer, tile, inner, second, first


def after(value, other):
    return lax.optimization_barrier((value, other))[0]


def places(device):
    row, column = divmod(device, 16)
    return (column // 8) * 4 + row // 4, row % 4, column // 2 % 4, column % 2


def grouped(key):
    groups = {}
    for device in range(256):
        groups.setdefault(key(*places(device)), []).append(device)
    return list(groups.values())


PLANES = grouped(lambda z, y, x, core: (z, core))
LINES = grouped(lambda z, y, x, core: (y, x, core))
BOTH = ("row", "col")
SWAP = [(i, i ^ 1) for i in range(16)]


def exchange(value, groups):
    return lax.all_to_all(value, BOTH, 0, 0, axis_index_groups=groups, tiled=True)


def weigh(parity, near, power):
    return pl.pallas_call(
        weigh_kernel,
        out_shape=jax.ShapeDtypeStruct((TILE, TILE), F32),
        in_specs=[SMEM_SPEC, SMEM_SPEC, VMEM_SPEC],
        out_specs=VMEM_SPEC,
        scratch_shapes=[pltpu.VMEM((4 * TILE + 8, 5 * TILE), F32)],
        compiler_params=params(8),
        name="weigh",
    )(parity, near, power)


def offsets_near(outer, tile, inner, second, first):
    rows = [[band[i, 0, TILE, :4] for i in range(3)] for band in (second, first)]
    rows.insert(1, [piece[0, TILE, :4] for piece in (outer, tile, inner)])
    return jnp.stack([value for row in rows for value in row]).astype(jnp.int32)


def spread(pieces):
    return pl.pallas_call(
        spread_kernel,
        out_shape=jax.ShapeDtypeStruct((DEPTH, 5, 8, SIDE), F32),
        compiler_params=params(8),
        name="spread",
    )(pieces)


def update(pieces, old):
    return pl.pallas_call(
        update_kernel,
        out_shape=[
            jax.ShapeDtypeStruct((GROUPS, 4, 8, SIDE), F32),
            jax.ShapeDtypeStruct((4, 8, SIDE), F32),
        ],
        compiler_params=params(8),
        name="update",
    )(pieces, old)


def local(object_field, probe, amplitudes, offsets):
    table = in_hbm(jnp.asarray(tables()))
    row, column = lax.axis_index("row"), lax.axis_index("col")
    core = column & 1
    group = core * GROUPS + (row & 3) * 4 + (lax.shift_right_logical(column, 1) & 3)
    probe = probe.reshape(4, 2 * GROUPS, 8, SIDE)
    old = lax.dynamic_index_in_dim(probe, group, 1, False)
    parity = jnp.stack([row & 1, core])
    measured = sort_measured(amplitudes[0, 0])
    parts = (in_hbm(probe),)
    tile = object_field
    marks = jnp.pad((offsets + SHIFT).astype(F32).reshape(1, 1, 4), ((0, 1), (0, 7), (0, TILE - 4)))
    around = neighbourhood(jnp.concatenate([tile, marks], axis=1))
    near = offsets_near(*around)
    for iteration in range(ITERS):
        mine, other, second, middle, first, power = step(
            offsets, parity, table, parts, measured, around
        )
        first = lax.ppermute(first, "row", pairs(0))
        second = lax.ppermute(second, "row", pairs(1))
        mine = mine + lax.ppermute(other, "col", SWAP)
        pieces = exchange(mine, PLANES)
        outer, own, inner = (middle[i] + first[i] + second[i] for i in range(3))
        pieces = spread(after(pieces, (outer, own, inner)))
        inner = lax.ppermute(after(inner, pieces), "col", pairs(0))
        outer = lax.ppermute(after(outer, pieces), "col", pairs(1))
        weight = weigh(parity, near, after(power, pieces))
        pieces = after(exchange(pieces, LINES), weight)
        pieces, old = update(pieces, old)
        totals = after(own, old) + inner + outer
        tile = tile + OBJECT_STEP * totals / (weight + OBJECT_REG)
        if iteration + 1 < ITERS:
            around = neighbourhood(tile)
        mine = exchange(pieces, PLANES)
        if iteration + 1 == ITERS:
            mine = after(mine, (inner, outer))
        parts = (mine, lax.ppermute(mine, "col", SWAP))
    probe = pl.pallas_call(
        lay_out_kernel,
        out_shape=jax.ShapeDtypeStruct((4, 2 * GROUPS, 8, SIDE), F32),
        in_specs=[SMEM_SPEC, VMEM_SPEC, VMEM_SPEC],
        out_specs=VMEM_SPEC,
        compiler_params=params(8),
        name="lay_out",
    )(parity, *parts)
    return (tile, probe.reshape(2, 2, SIDE, SIDE))


def solution(mesh):
    return jax.shard_map(
        local,
        mesh=mesh,
        in_specs=(
            P(None, "row", "col"),
            P(),
            P("row", "col", None, None, None),
            P("row", "col", None, None),
        ),
        out_specs=(P(None, "row", "col"), P()),
        check_vma=False,
    )
```

```python
import functools
import math

import jax
import jax.numpy as jnp
import ml_dtypes
import numpy as np
from jax import lax
from jax.experimental import pallas as pl
from jax.experimental.pallas import tpu as pltpu
from jax.sharding import PartitionSpec as P

ITERS = 2
FLOOR = 0.5
OBJECT_STEP = 0.5
OBJECT_REG = 0.5
PROBE_STEP = 1.0
PROBE_REG = 1.0
TILE = 128
SIDE = 256
HALF = SIDE // 2
WIDE = 3 * TILE
CHUNK = 64
GROUPS = 16
DEPTH = 8
SHIFT = TILE + 1
F32 = jnp.float32
BF16 = jnp.bfloat16


def split_np(table):
    high = table.astype(np.float32).astype(ml_dtypes.bfloat16)
    low = (table - high.astype(np.float64)).astype(np.float32).astype(ml_dtypes.bfloat16)
    return np.stack([high, low])


def tables():
    out = []
    for parity in range(2):
        u = 2 * np.arange(HALF)[:, None] + parity
        angle = 2.0 * math.pi * ((u * np.arange(HALF)[None, :]) % SIDE) / SIDE
        cos, sin = np.cos(angle) / 16.0, np.sin(angle) / 16.0
        forward = np.block([[cos, sin], [-sin, cos]])
        out.append(np.stack([split_np(forward), split_np(forward.T)]))
    return np.stack(out)


def split(x):
    high = x.astype(BF16)
    return high, (x - high.astype(F32)).astype(BF16)


def split_whole(x):
    high = x.astype(BF16)
    rest = x - high.astype(F32)
    middle = rest.astype(BF16)
    return high, middle, (rest - middle.astype(F32)).astype(BF16)


def dot(a, b):
    return jnp.dot(a, b, preferred_element_type=F32)


def sort_kernel(measured_ref, out_ref):
    source = lax.broadcasted_iota(jnp.int32, (SIDE, SIDE), 0)
    place = lax.broadcasted_iota(jnp.int32, (SIDE, SIDE), 1)
    wanted = jnp.where(place < HALF, 2 * place, 2 * place - (SIDE - 1))
    select = jnp.where(source == wanted, 1.0, 0.0).astype(BF16)
    wanted = jnp.where(source < HALF, 2 * source, 2 * source - (SIDE - 1))
    select_rows = jnp.where(place == wanted, 1.0, 0.0).astype(BF16)
    for scan in range(2):
        high, middle, low = split_whole(measured_ref[scan])
        turned = (dot(low, select) + dot(middle, select)) + dot(high, select)
        high, middle, low = split_whole(turned)
        turned = (dot(select_rows, low) + dot(select_rows, middle)) + dot(select_rows, high)
        out_ref[scan, 0] = turned[:HALF]
        out_ref[scan, 1] = turned[HALF:]


def lay_out_kernel(parity_ref, mine_ref, other_ref, out_ref):
    for half, ref in enumerate((mine_ref, other_ref)):
        place = parity_ref[1] if half == 0 else 1 - parity_ref[1]
        for part in range(4):
            out_ref[part, pl.ds(place * GROUPS, GROUPS)] = ref[:, part]


def step_kernel(halves, offsets_ref, parity_ref, table_in, *refs):
    probe_in, refs = refs[: 1 + halves], refs[1 + halves :]
    (
        measured_in,
        outer_in,
        tile_in,
        inner_in,
        second_in,
        first_in,
        mine_out,
        other_out,
        grad_second,
        grad_middle,
        grad_first,
        power_out,
        table_ref,
        probe,
        measured_ref,
        padded,
        windows,
        folded,
        stacked,
        far,
        back,
        contrib,
        total,
        sums,
        semaphores,
    ) = refs
    row_parity, core = parity_ref[0], parity_ref[1]
    across = (row_parity * 2, 1, 2 - row_parity * 2)
    along = (core * 2, 1, 2 - core * 2)
    copies = []

    def start(source, target):
        copy = pltpu.make_async_copy(source, target, semaphores.at[len(copies)])
        copy.start()
        copies.append(copy)

    def third(block):
        return pl.ds(block * TILE if isinstance(block, int) else pl.multiple_of(block * TILE, TILE), TILE)

    for place, piece in enumerate((outer_in, tile_in, inner_in)):
        columns = third(along[place])
        start(piece.at[:, third(0)], padded.at[:, third(1), columns])
        start(second_in.at[place, :, third(0)], padded.at[:, third(across[0]), columns])
        start(first_in.at[place, :, third(0)], padded.at[:, third(across[2]), columns])
    near = len(copies)
    if halves:
        for half, ref in enumerate(probe_in):
            place = core if half == 0 else 1 - core
            for part in range(4):
                start(ref.at[:, part], probe.at[part, pl.ds(place * GROUPS, GROUPS)])
    else:
        start(probe_in[0], probe)
    start(table_in, table_ref)
    operands = len(copies)
    start(measured_in, measured_ref)

    def probe_rows(part, mode, piece, columns=slice(None)):
        groups = pl.ds(piece * (CHUNK // 8), CHUNK // 8)
        value = probe[2 * part + mode, groups, :, columns]
        return value.reshape(CHUNK, value.shape[-1])

    lane = lax.broadcasted_iota(jnp.int32, (CHUNK // 8, 8, TILE), 2)
    sublane = lax.broadcasted_iota(jnp.int32, (CHUNK // 8, 8, TILE), 1)
    for channel in range(2):
        total[channel] = jnp.zeros((WIDE + 8, WIDE), F32)
    for copy in copies[:near]:
        copy.wait()

    def cut(scan, carry):
        row, column = offsets_ref[0, 0, scan, 0] + HALF, offsets_ref[0, 0, scan, 1] + HALF
        inner = lax.rem(row, 8)
        base = pl.multiple_of(row - inner, 8)
        turn, keep = lax.rem(TILE - column, TILE), lane < TILE - column
        lift, stay = lax.rem(8 - inner, 8), sublane < 8 - inner
        for channel in range(2):
            for piece in range(SIDE // CHUNK):
                turned = []
                for b in range(3):
                    rows = padded[channel, pl.ds(base + piece * CHUNK, CHUNK + 8), pl.ds(b * TILE, TILE)]
                    rows = pltpu.roll(rows.reshape(CHUNK // 8 + 1, 8, TILE), lift, 1)
                    rows = jnp.where(stay, rows[:-1], rows[1:])
                    turned.append(pltpu.roll(rows, turn, 2))
                for b in range(2):
                    windows[scan, channel, pl.ds(piece * CHUNK, CHUNK), pl.ds(b * TILE, TILE)] = (
                        jnp.where(keep, turned[b], turned[b + 1]).reshape(CHUNK, TILE)
                    )
        return carry

    lax.fori_loop(0, 2, cut, 0)
    for copy in copies[near:operands]:
        copy.wait()

    def forward(image, carry):
        scan, mode = image // 2, image % 2
        for piece in range(SIDE // CHUNK):
            rows = pl.ds(piece * CHUNK, CHUNK)
            p_re, p_im = probe_rows(0, mode, piece), probe_rows(1, mode, piece)
            w_re, w_im = windows[scan, 0, rows, :], windows[scan, 1, rows, :]
            e_re = p_re * w_re - p_im * w_im
            e_im = p_re * w_im + p_im * w_re
            for parity in range(2):
                sign = 1.0 if parity == 0 else -1.0
                for part, value in enumerate((e_re, e_im)):
                    half = value[:, :HALF] + sign * value[:, HALF:]
                    high, low = split(half)
                    folded[parity, 0, rows, part * HALF : (part + 1) * HALF] = high
                    folded[parity, 1, rows, part * HALF : (part + 1) * HALF] = low
        for parity in range(2):
            out = (
                dot(folded[parity, 1], table_ref[parity, 1, 0])
                + dot(folded[parity, 0], table_ref[parity, 1, 1])
                + dot(folded[parity, 0], table_ref[parity, 1, 0])
            )
            for other in range(2):
                sign = 1.0 if other == 0 else -1.0
                half = out[:HALF] + sign * out[HALF:]
                high, low = split(half)
                place = pl.ds(parity * HALF, HALF)
                stacked[other, 0, 0:HALF, place] = high[:, :HALF]
                stacked[other, 0, HALF:, place] = high[:, HALF:]
                stacked[other, 1, 0:HALF, place] = low[:, :HALF]
                stacked[other, 1, HALF:, place] = low[:, HALF:]
        for other in range(2):
            far[image, other] = (
                dot(table_ref[other, 0, 0], stacked[other, 1])
                + dot(table_ref[other, 0, 1], stacked[other, 0])
                + dot(table_ref[other, 0, 0], stacked[other, 0])
            )
        return carry

    lax.fori_loop(0, 4, forward, 0, unroll=4)

    def scale(index, carry):
        scan, other = index // 2, index % 2
        for piece in range(HALF // 32):
            upper, lower = pl.ds(piece * 32, 32), pl.ds(HALF + piece * 32, 32)
            parts = [
                far[2 * scan + mode, other, rows, :] for mode in range(2) for rows in (upper, lower)
            ]
            intensity = (parts[0] * parts[0] + parts[1] * parts[1]) + (
                parts[2] * parts[2] + parts[3] * parts[3]
            )
            measured = measured_ref[scan, other, upper, :]
            factor = measured / jnp.maximum(jnp.sqrt(intensity), FLOOR) - 1.0
            for mode in range(2):
                far[2 * scan + mode, other, upper, :] = parts[2 * mode] * factor
                far[2 * scan + mode, other, lower, :] = parts[2 * mode + 1] * factor
        return carry

    copies[operands].wait()
    lax.fori_loop(0, 4, scale, 0)

    def backward(image, carry):
        scan, mode = image // 2, image % 2
        halves = []
        for other in range(2):
            high, low = split(far[image, other])
            halves.append(
                dot(table_ref[other, 1, 0], low)
                + dot(table_ref[other, 1, 1], high)
                + dot(table_ref[other, 1, 0], high)
            )
        for place, value in ((0, halves[0] + halves[1]), (HALF, halves[0] - halves[1])):
            high, low = split(value)
            for parity in range(2):
                columns = slice(parity * HALF, (parity + 1) * HALF)
                for part in range(2):
                    rows = slice(part * HALF, (part + 1) * HALF)
                    target = pl.ds(part * HALF, HALF)
                    folded[parity, 0, pl.ds(place, HALF), target] = high[rows, columns]
                    folded[parity, 1, pl.ds(place, HALF), target] = low[rows, columns]
        for parity in range(2):
            back[parity] = (
                dot(folded[parity, 1], table_ref[parity, 0, 0])
                + dot(folded[parity, 0], table_ref[parity, 0, 1])
                + dot(folded[parity, 0], table_ref[parity, 0, 0])
            )
        first_scan, first_mode = scan == 0, mode == 0
        for piece in range(SIDE // CHUNK):
            rows = pl.ds(piece * CHUNK, CHUNK)
            even, odd = back[0, rows, :], back[1, rows, :]
            for b in range(2):
                columns = pl.ds(b * HALF, HALF)
                sign = 1.0 if b == 0 else -1.0
                b_re = even[:, :HALF] + sign * odd[:, :HALF]
                b_im = even[:, HALF:] + sign * odd[:, HALF:]
                p_re = probe_rows(0, mode, piece, columns)
                p_im = probe_rows(1, mode, piece, columns)
                w_re, w_im = windows[scan, 0, rows, columns], windows[scan, 1, rows, columns]
                o_re = p_re * b_re + p_im * b_im
                o_im = p_re * b_im - p_im * b_re
                zero = jnp.zeros_like(o_re)
                contrib[scan, 0, rows, columns] = o_re + jnp.where(
                    first_mode, zero, contrib[scan, 0, rows, columns]
                )
                contrib[scan, 1, rows, columns] = o_im + jnp.where(
                    first_mode, zero, contrib[scan, 1, rows, columns]
                )
                g_re = w_re * b_re + w_im * b_im
                g_im = w_re * b_im - w_im * b_re
                for slot in range(CHUNK // 8):
                    group = piece * (CHUNK // 8) + slot
                    inner = slice(slot * 8, slot * 8 + 8)
                    for part, value in enumerate((g_re, g_im)):
                        place = 2 * part + mode
                        old = sums[group, place, :, columns]
                        sums[group, place, :, columns] = value[inner] + jnp.where(
                            first_scan, jnp.zeros_like(old), old
                        )

        return carry

    for piece in range(SIDE // CHUNK):
        rows = pl.ds(piece * CHUNK, CHUNK)
        power = None
        for mode in range(2):
            for part in range(2):
                value = probe_rows(part, mode, piece)
                power = value * value if power is None else power + value * value
        power_out[rows, :] = power
        weight = None
        for scan in range(2):
            for part in range(2):
                value = windows[scan, part, rows, :]
                weight = value * value if weight is None else weight + value * value
        for slot in range(CHUNK // 8):
            sums[piece * (CHUNK // 8) + slot, 4] = weight[slot * 8 : slot * 8 + 8]

    lax.fori_loop(0, 4, backward, 0, unroll=4)

    def scatter(scan, carry):
        row, column = offsets_ref[0, 0, scan, 0] + HALF, offsets_ref[0, 0, scan, 1] + HALF
        inner = lax.rem(row, 8)
        base = pl.multiple_of(row - inner, 8)
        turn, keep = lax.rem(column, TILE), lane >= column
        zero = jnp.zeros((CHUNK // 8, 8, TILE), F32)
        edge = jnp.zeros((1, 8, TILE), F32)
        stay = lax.broadcasted_iota(jnp.int32, (CHUNK // 8 + 1, 8, TILE), 1) >= inner
        for channel in range(2):
            for piece in range(SIDE // CHUNK):
                halves = []
                for b in range(2):
                    value = contrib[scan, channel, pl.ds(piece * CHUNK, CHUNK), pl.ds(b * TILE, TILE)]
                    halves.append(pltpu.roll(value.reshape(CHUNK // 8, 8, TILE), turn, 2))
                thirds = (
                    jnp.where(keep, halves[0], zero),
                    jnp.where(keep, halves[1], halves[0]),
                    jnp.where(keep, zero, halves[1]),
                )
                place = pl.ds(base + piece * CHUNK, CHUNK + 8)
                for b in range(3):
                    value = pltpu.roll(thirds[b], inner, 1)
                    value = jnp.where(
                        stay,
                        jnp.concatenate([value, edge]),
                        jnp.concatenate([edge, value]),
                    )
                    total[channel, place, pl.ds(b * TILE, TILE)] += value.reshape(CHUNK + 8, TILE)
        return carry

    done = len(copies)
    start(sums.at[pl.ds(core * GROUPS, GROUPS)], mine_out)
    start(sums.at[pl.ds((1 - core) * GROUPS, GROUPS)], other_out)
    lax.fori_loop(0, 2, scatter, 0)
    for block, ref in enumerate((grad_second, grad_middle, grad_first)):
        for column in range(3):
            start(total.at[:, third(across[block]), third(along[column])], ref.at[column])
    for copy in copies[done:]:
        copy.wait()


def weigh_kernel(parity_ref, near_ref, power_ref, out_ref, padded):
    padded[...] = jnp.zeros_like(padded)
    padded[pl.ds(TILE, SIDE), pl.ds(TILE, SIDE)] = power_ref[...]
    lane = lax.broadcasted_iota(jnp.int32, (TILE // 8, 8, TILE), 2)
    sublane = lax.broadcasted_iota(jnp.int32, (TILE // 8, 8, TILE), 1)

    def add(index, total):
        place, scan = index // 2, index % 2
        across, along = place // 3, place % 3
        across = 1 + (across - 1) * (1 - 2 * parity_ref[0])
        along = 1 + (along - 1) * (1 - 2 * parity_ref[1])
        row, column = near_ref[place, 2 * scan], near_ref[place, 2 * scan + 1]
        column = jnp.where(row == 0, 0, 2 * TILE - along * TILE - (column - SHIFT))
        row = jnp.where(row == 0, WIDE, 2 * TILE - across * TILE - (row - SHIFT))
        inner = lax.rem(row, 8)
        base = pl.multiple_of(row - inner, 8)
        offset = lax.rem(column, TILE)
        block = pl.multiple_of(column - offset, TILE)
        turned = []
        for b in range(2):
            rows = padded[pl.ds(base, TILE + 8), pl.ds(block + b * TILE, TILE)]
            rows = pltpu.roll(rows.reshape(TILE // 8 + 1, 8, TILE), lax.rem(8 - inner, 8), 1)
            rows = jnp.where(sublane < 8 - inner, rows[:-1], rows[1:])
            turned.append(pltpu.roll(rows, lax.rem(TILE - offset, TILE), 2))
        return total + jnp.where(lane < TILE - offset, turned[0], turned[1])

    total = lax.fori_loop(0, 18, add, jnp.zeros((TILE // 8, 8, TILE), F32))
    out_ref[...] = total.reshape(TILE, TILE)


def spread_kernel(pieces_ref, out_ref):
    total = pieces_ref[0]
    for piece in range(1, GROUPS):
        total = total + pieces_ref[piece]
    for copy in range(DEPTH):
        out_ref[copy] = total


def update_kernel(pieces_ref, old_ref, out_ref, new_ref):
    total = pieces_ref[0]
    for piece in range(1, DEPTH):
        total = total + pieces_ref[piece]
    new = old_ref[...] + PROBE_STEP * total[:4] / (total[4:] + PROBE_REG)
    new_ref[...] = new
    for copy in range(GROUPS):
        out_ref[copy] = new


VMEM_SPEC = pl.BlockSpec(memory_space=pltpu.VMEM)
SMEM_SPEC = pl.BlockSpec(memory_space=pltpu.SMEM)
ANY_SPEC = pl.BlockSpec(memory_space=pl.ANY)


def in_hbm(value):
    return pltpu.with_memory_space_constraint(value, pltpu.HBM)


def params(mebibytes):
    return pltpu.CompilerParams(vmem_limit_bytes=mebibytes * 2**20)


def sort_measured(measured):
    return pl.pallas_call(
        sort_kernel,
        out_shape=jax.ShapeDtypeStruct((2, 2, HALF, SIDE), F32),
        in_specs=[VMEM_SPEC],
        out_specs=VMEM_SPEC,
        compiler_params=params(8),
        name="sort_measured",
    )(measured)


def step(offsets, parity, table, probe, measured, around):
    halves = len(probe) - 1
    band = jax.ShapeDtypeStruct((3, 2, TILE, TILE), F32)
    half = jax.ShapeDtypeStruct((GROUPS, 5, 8, SIDE), F32)
    return pl.pallas_call(
        functools.partial(step_kernel, halves),
        out_shape=[half, half, band, band, band, jax.ShapeDtypeStruct((SIDE, SIDE), F32)],
        in_specs=[SMEM_SPEC, SMEM_SPEC] + [ANY_SPEC] * (8 + halves),
        out_specs=[ANY_SPEC] * 5 + [VMEM_SPEC],
        scratch_shapes=[
            pltpu.VMEM(table.shape, BF16),
            pltpu.VMEM((4, 2 * GROUPS, 8, SIDE), F32),
            pltpu.VMEM(measured.shape, F32),
            pltpu.VMEM((2, WIDE + 8, WIDE), F32),
            pltpu.VMEM((2, 2, SIDE, SIDE), F32),
            pltpu.VMEM((2, 2, SIDE, SIDE), BF16),
            pltpu.VMEM((2, 2, SIDE, SIDE), BF16),
            pltpu.VMEM((4, 2, SIDE, SIDE), F32),
            pltpu.VMEM((2, SIDE, SIDE), F32),
            pltpu.VMEM((2, 2, SIDE, SIDE), F32),
            pltpu.VMEM((2, WIDE + 8, WIDE), F32),
            pltpu.VMEM((2 * GROUPS, 5, 8, SIDE), F32),
            pltpu.SemaphoreType.DMA((32,)),
        ],
        compiler_params=params(20),
        name="step",
    )(offsets, parity, table, *probe, measured, *around)


def pairs(first):
    both = [(i, i + 1) for i in range(first, 15, 2)]
    return both + [(j, i) for i, j in both]


def neighbourhood(tile):
    inner = lax.ppermute(tile, "col", pairs(0))
    outer = lax.ppermute(tile, "col", pairs(1))
    band = jnp.stack([outer, tile, inner])
    first = lax.ppermute(band, "row", pairs(0))
    second = lax.ppermute(band, "row", pairs(1))
    return outer, tile, inner, second, first


def after(value, other):
    return lax.optimization_barrier((value, other))[0]


def places(device):
    row, column = divmod(device, 16)
    return (column // 8) * 4 + row // 4, row % 4, column // 2 % 4, column % 2


def grouped(key):
    groups = {}
    for device in range(256):
        groups.setdefault(key(*places(device)), []).append(device)
    return list(groups.values())


PLANES = grouped(lambda z, y, x, core: (z, core))
LINES = grouped(lambda z, y, x, core: (y, x, core))
BOTH = ("row", "col")
SWAP = [(i, i ^ 1) for i in range(16)]


def exchange(value, groups):
    return lax.all_to_all(value, BOTH, 0, 0, axis_index_groups=groups, tiled=True)


def weigh(parity, near, power):
    return pl.pallas_call(
        weigh_kernel,
        out_shape=jax.ShapeDtypeStruct((TILE, TILE), F32),
        in_specs=[SMEM_SPEC, SMEM_SPEC, VMEM_SPEC],
        out_specs=VMEM_SPEC,
        scratch_shapes=[pltpu.VMEM((4 * TILE + 8, 5 * TILE), F32)],
        compiler_params=params(8),
        name="weigh",
    )(parity, near, power)


def offsets_near(outer, tile, inner, second, first):
    rows = [[band[i, 0, TILE, :4] for i in range(3)] for band in (second, first)]
    rows.insert(1, [piece[0, TILE, :4] for piece in (outer, tile, inner)])
    return jnp.stack([value for row in rows for value in row]).astype(jnp.int32)


def spread(pieces):
    return pl.pallas_call(
        spread_kernel,
        out_shape=jax.ShapeDtypeStruct((DEPTH, 5, 8, SIDE), F32),
        compiler_params=params(8),
        name="spread",
    )(pieces)


def update(pieces, old):
    return pl.pallas_call(
        update_kernel,
        out_shape=[
            jax.ShapeDtypeStruct((GROUPS, 4, 8, SIDE), F32),
            jax.ShapeDtypeStruct((4, 8, SIDE), F32),
        ],
        compiler_params=params(8),
        name="update",
    )(pieces, old)


def local(object_field, probe, amplitudes, offsets):
    table = in_hbm(jnp.asarray(tables()))
    row, column = lax.axis_index("row"), lax.axis_index("col")
    core = column & 1
    group = core * GROUPS + (row & 3) * 4 + (lax.shift_right_logical(column, 1) & 3)
    probe = probe.reshape(4, 2 * GROUPS, 8, SIDE)
    old = lax.dynamic_index_in_dim(probe, group, 1, False)
    parity = jnp.stack([row & 1, core])
    measured = sort_measured(amplitudes[0, 0])
    parts = (in_hbm(probe),)
    tile = object_field
    marks = jnp.pad((offsets + SHIFT).astype(F32).reshape(1, 1, 4), ((0, 1), (0, 7), (0, TILE - 4)))
    around = neighbourhood(jnp.concatenate([tile, marks], axis=1))
    near = offsets_near(*around)
    for iteration in range(ITERS):
        mine, other, second, middle, first, power = step(
            offsets, parity, table, parts, measured, around
        )
        mine = mine + lax.ppermute(other, "col", SWAP)
        first = lax.ppermute(after(first, mine), "row", pairs(0))
        second = lax.ppermute(after(second, mine), "row", pairs(1))
        pieces = spread(exchange(mine, PLANES))
        middle = after(middle, pieces)
        outer, own, inner = (middle[i] + first[i] + second[i] for i in range(3))
        folds = (outer, own, inner)
        inner = lax.ppermute(inner, "col", pairs(0))
        outer = lax.ppermute(outer, "col", pairs(1))
        weight = weigh(parity, near, after(power, pieces))
        pieces = after(exchange(pieces, LINES), (weight, folds))
        pieces, old = update(pieces, old)
        totals = after(own, old) + inner + outer
        tile = tile + OBJECT_STEP * totals / (weight + OBJECT_REG)
        if iteration + 1 < ITERS:
            around = neighbourhood(tile)
        mine = exchange(pieces, PLANES)
        if iteration + 1 == ITERS:
            mine = after(mine, (inner, outer))
        parts = (mine, lax.ppermute(mine, "col", SWAP))
    probe = pl.pallas_call(
        lay_out_kernel,
        out_shape=jax.ShapeDtypeStruct((4, 2 * GROUPS, 8, SIDE), F32),
        in_specs=[SMEM_SPEC, VMEM_SPEC, VMEM_SPEC],
        out_specs=VMEM_SPEC,
        compiler_params=params(8),
        name="lay_out",
    )(parity, *parts)
    return (tile, probe.reshape(2, 2, SIDE, SIDE))


def solution(mesh):
    return jax.shard_map(
        local,
        mesh=mesh,
        in_specs=(
            P(None, "row", "col"),
            P(),
            P("row", "col", None, None, None),
            P("row", "col", None, None),
        ),
        out_specs=(P(None, "row", "col"), P()),
        check_vma=False,
    )
```

```python
import functools
import math

import jax
import jax.numpy as jnp
import ml_dtypes
import numpy as np
from jax import lax
from jax.experimental import pallas as pl
from jax.experimental.pallas import tpu as pltpu
from jax.sharding import PartitionSpec as P

ITERS = 2
FLOOR = 0.5
OBJECT_STEP = 0.5
OBJECT_REG = 0.5
PROBE_STEP = 1.0
PROBE_REG = 1.0
TILE = 128
SIDE = 256
HALF = SIDE // 2
WIDE = 3 * TILE
CHUNK = 64
GROUPS = 16
DEPTH = 8
SHIFT = TILE + 1
F32 = jnp.float32
BF16 = jnp.bfloat16


def split_np(table):
    high = table.astype(np.float32).astype(ml_dtypes.bfloat16)
    low = (table - high.astype(np.float64)).astype(np.float32).astype(ml_dtypes.bfloat16)
    return np.stack([high, low])


def tables():
    out = []
    for parity in range(2):
        u = 2 * np.arange(HALF)[:, None] + parity
        angle = 2.0 * math.pi * ((u * np.arange(HALF)[None, :]) % SIDE) / SIDE
        cos, sin = np.cos(angle) / 16.0, np.sin(angle) / 16.0
        forward = np.block([[cos, sin], [-sin, cos]])
        out.append(np.stack([split_np(forward), split_np(forward.T)]))
    return np.stack(out)


def split(x):
    high = x.astype(BF16)
    return high, (x - high.astype(F32)).astype(BF16)


def split_whole(x):
    high = x.astype(BF16)
    rest = x - high.astype(F32)
    middle = rest.astype(BF16)
    return high, middle, (rest - middle.astype(F32)).astype(BF16)


def dot(a, b):
    return jnp.dot(a, b, preferred_element_type=F32)


def sort_kernel(measured_ref, out_ref):
    source = lax.broadcasted_iota(jnp.int32, (SIDE, SIDE), 0)
    place = lax.broadcasted_iota(jnp.int32, (SIDE, SIDE), 1)
    wanted = jnp.where(place < HALF, 2 * place, 2 * place - (SIDE - 1))
    select = jnp.where(source == wanted, 1.0, 0.0).astype(BF16)
    wanted = jnp.where(source < HALF, 2 * source, 2 * source - (SIDE - 1))
    select_rows = jnp.where(place == wanted, 1.0, 0.0).astype(BF16)
    for scan in range(2):
        high, middle, low = split_whole(measured_ref[scan])
        turned = (dot(low, select) + dot(middle, select)) + dot(high, select)
        high, middle, low = split_whole(turned)
        turned = (dot(select_rows, low) + dot(select_rows, middle)) + dot(select_rows, high)
        out_ref[scan, 0] = turned[:HALF]
        out_ref[scan, 1] = turned[HALF:]


def lay_out_kernel(whose, parity_ref, half_ref, *refs):
    out_ref, semaphores = refs[-2:]
    place = parity_ref[1] if whose == 0 else 1 - parity_ref[1]
    copies = []
    for part in range(4):
        target = out_ref.at[part, pl.ds(place * GROUPS, GROUPS)]
        copies.append(pltpu.make_async_copy(half_ref.at[:, part], target, semaphores.at[part]))
        copies[-1].start()
    for copy in copies:
        copy.wait()


def mark_kernel(offsets_ref, tile_ref, out_ref):
    out_ref[:, :TILE, :] = tile_ref[...]
    lane = lax.broadcasted_iota(jnp.int32, (8, TILE), 1)
    values = jnp.zeros((8, TILE), jnp.int32)
    for scan in range(2):
        for axis in range(2):
            value = offsets_ref[0, 0, scan, axis] + SHIFT
            values = jnp.where(lane == 2 * scan + axis, value, values)
    out_ref[0, TILE:, :] = values.astype(F32)
    out_ref[1, TILE:, :] = jnp.zeros((8, TILE), F32)


def step_kernel(halves, offsets_ref, parity_ref, table_in, *refs):
    probe_in, refs = refs[: 1 + halves], refs[1 + halves :]
    (
        measured_in,
        outer_in,
        tile_in,
        inner_in,
        second_in,
        first_in,
        mine_out,
        other_out,
        grad_second,
        grad_middle,
        grad_first,
        power_out,
        table_ref,
        probe,
        measured_ref,
        padded,
        windows,
        folded,
        stacked,
        far,
        back,
        contrib,
        total,
        sums,
        semaphores,
    ) = refs
    row_parity, core = parity_ref[0], parity_ref[1]
    across = (row_parity * 2, 1, 2 - row_parity * 2)
    along = (core * 2, 1, 2 - core * 2)
    copies = []

    def start(source, target):
        copy = pltpu.make_async_copy(source, target, semaphores.at[len(copies)])
        copy.start()
        copies.append(copy)

    def third(block):
        return pl.ds(block * TILE if isinstance(block, int) else pl.multiple_of(block * TILE, TILE), TILE)

    for place, piece in enumerate((outer_in, tile_in, inner_in)):
        columns = third(along[place])
        start(piece.at[:, third(0)], padded.at[:, third(1), columns])
        start(second_in.at[place, :, third(0)], padded.at[:, third(across[0]), columns])
        start(first_in.at[place, :, third(0)], padded.at[:, third(across[2]), columns])
    near = len(copies)
    if halves:
        for half, ref in enumerate(probe_in):
            place = core if half == 0 else 1 - core
            for part in range(4):
                start(ref.at[:, part], probe.at[part, pl.ds(place * GROUPS, GROUPS)])
    else:
        start(probe_in[0], probe)
    start(table_in, table_ref)
    operands = len(copies)
    start(measured_in, measured_ref)

    def probe_rows(part, mode, piece, columns=slice(None)):
        groups = pl.ds(piece * (CHUNK // 8), CHUNK // 8)
        value = probe[2 * part + mode, groups, :, columns]
        return value.reshape(CHUNK, value.shape[-1])

    lane = lax.broadcasted_iota(jnp.int32, (CHUNK // 8, 8, TILE), 2)
    sublane = lax.broadcasted_iota(jnp.int32, (CHUNK // 8, 8, TILE), 1)
    for channel in range(2):
        total[channel] = jnp.zeros((WIDE + 8, WIDE), F32)
    for copy in copies[:near]:
        copy.wait()

    def cut(scan, carry):
        row, column = offsets_ref[0, 0, scan, 0] + HALF, offsets_ref[0, 0, scan, 1] + HALF
        inner = lax.rem(row, 8)
        base = pl.multiple_of(row - inner, 8)
        turn, keep = lax.rem(TILE - column, TILE), lane < TILE - column
        lift, stay = lax.rem(8 - inner, 8), sublane < 8 - inner
        for channel in range(2):
            for piece in range(SIDE // CHUNK):
                turned = []
                for b in range(3):
                    rows = padded[channel, pl.ds(base + piece * CHUNK, CHUNK + 8), pl.ds(b * TILE, TILE)]
                    rows = pltpu.roll(rows.reshape(CHUNK // 8 + 1, 8, TILE), lift, 1)
                    rows = jnp.where(stay, rows[:-1], rows[1:])
                    turned.append(pltpu.roll(rows, turn, 2))
                for b in range(2):
                    windows[scan, channel, pl.ds(piece * CHUNK, CHUNK), pl.ds(b * TILE, TILE)] = (
                        jnp.where(keep, turned[b], turned[b + 1]).reshape(CHUNK, TILE)
                    )
        return carry

    lax.fori_loop(0, 2, cut, 0)
    for copy in copies[near:operands]:
        copy.wait()

    def forward(image, carry):
        scan, mode = image // 2, image % 2
        for piece in range(SIDE // CHUNK):
            rows = pl.ds(piece * CHUNK, CHUNK)
            p_re, p_im = probe_rows(0, mode, piece), probe_rows(1, mode, piece)
            w_re, w_im = windows[scan, 0, rows, :], windows[scan, 1, rows, :]
            e_re = p_re * w_re - p_im * w_im
            e_im = p_re * w_im + p_im * w_re
            for parity in range(2):
                sign = 1.0 if parity == 0 else -1.0
                for part, value in enumerate((e_re, e_im)):
                    half = value[:, :HALF] + sign * value[:, HALF:]
                    high, low = split(half)
                    folded[parity, 0, rows, part * HALF : (part + 1) * HALF] = high
                    folded[parity, 1, rows, part * HALF : (part + 1) * HALF] = low
        for parity in range(2):
            out = (
                dot(folded[parity, 1], table_ref[parity, 1, 0])
                + dot(folded[parity, 0], table_ref[parity, 1, 1])
                + dot(folded[parity, 0], table_ref[parity, 1, 0])
            )
            for other in range(2):
                sign = 1.0 if other == 0 else -1.0
                half = out[:HALF] + sign * out[HALF:]
                high, low = split(half)
                place = pl.ds(parity * HALF, HALF)
                stacked[other, 0, 0:HALF, place] = high[:, :HALF]
                stacked[other, 0, HALF:, place] = high[:, HALF:]
                stacked[other, 1, 0:HALF, place] = low[:, :HALF]
                stacked[other, 1, HALF:, place] = low[:, HALF:]
        for other in range(2):
            far[image, other] = (
                dot(table_ref[other, 0, 0], stacked[other, 1])
                + dot(table_ref[other, 0, 1], stacked[other, 0])
                + dot(table_ref[other, 0, 0], stacked[other, 0])
            )
        return carry

    lax.fori_loop(0, 4, forward, 0, unroll=4)

    def scale(index, carry):
        scan, other = index // 2, index % 2
        for piece in range(HALF // 32):
            upper, lower = pl.ds(piece * 32, 32), pl.ds(HALF + piece * 32, 32)
            parts = [
                far[2 * scan + mode, other, rows, :] for mode in range(2) for rows in (upper, lower)
            ]
            intensity = (parts[0] * parts[0] + parts[1] * parts[1]) + (
                parts[2] * parts[2] + parts[3] * parts[3]
            )
            measured = measured_ref[scan, other, upper, :]
            factor = measured / jnp.maximum(jnp.sqrt(intensity), FLOOR) - 1.0
            for mode in range(2):
                far[2 * scan + mode, other, upper, :] = parts[2 * mode] * factor
                far[2 * scan + mode, other, lower, :] = parts[2 * mode + 1] * factor
        return carry

    copies[operands].wait()
    lax.fori_loop(0, 4, scale, 0)

    def backward(image, carry):
        scan, mode = image // 2, image % 2
        halves = []
        for other in range(2):
            high, low = split(far[image, other])
            halves.append(
                dot(table_ref[other, 1, 0], low)
                + dot(table_ref[other, 1, 1], high)
                + dot(table_ref[other, 1, 0], high)
            )
        for place, value in ((0, halves[0] + halves[1]), (HALF, halves[0] - halves[1])):
            high, low = split(value)
            for parity in range(2):
                columns = slice(parity * HALF, (parity + 1) * HALF)
                for part in range(2):
                    rows = slice(part * HALF, (part + 1) * HALF)
                    target = pl.ds(part * HALF, HALF)
                    folded[parity, 0, pl.ds(place, HALF), target] = high[rows, columns]
                    folded[parity, 1, pl.ds(place, HALF), target] = low[rows, columns]
        for parity in range(2):
            back[parity] = (
                dot(folded[parity, 1], table_ref[parity, 0, 0])
                + dot(folded[parity, 0], table_ref[parity, 0, 1])
                + dot(folded[parity, 0], table_ref[parity, 0, 0])
            )
        first_scan, first_mode = scan == 0, mode == 0
        for piece in range(SIDE // CHUNK):
            rows = pl.ds(piece * CHUNK, CHUNK)
            even, odd = back[0, rows, :], back[1, rows, :]
            for b in range(2):
                columns = pl.ds(b * HALF, HALF)
                sign = 1.0 if b == 0 else -1.0
                b_re = even[:, :HALF] + sign * odd[:, :HALF]
                b_im = even[:, HALF:] + sign * odd[:, HALF:]
                p_re = probe_rows(0, mode, piece, columns)
                p_im = probe_rows(1, mode, piece, columns)
                w_re, w_im = windows[scan, 0, rows, columns], windows[scan, 1, rows, columns]
                o_re = p_re * b_re + p_im * b_im
                o_im = p_re * b_im - p_im * b_re
                zero = jnp.zeros_like(o_re)
                contrib[scan, 0, rows, columns] = o_re + jnp.where(
                    first_mode, zero, contrib[scan, 0, rows, columns]
                )
                contrib[scan, 1, rows, columns] = o_im + jnp.where(
                    first_mode, zero, contrib[scan, 1, rows, columns]
                )
                g_re = w_re * b_re + w_im * b_im
                g_im = w_re * b_im - w_im * b_re
                for slot in range(CHUNK // 8):
                    group = piece * (CHUNK // 8) + slot
                    inner = slice(slot * 8, slot * 8 + 8)
                    for part, value in enumerate((g_re, g_im)):
                        place = 2 * part + mode
                        old = sums[group, place, :, columns]
                        sums[group, place, :, columns] = value[inner] + jnp.where(
                            first_scan, jnp.zeros_like(old), old
                        )

        return carry

    for piece in range(SIDE // CHUNK):
        rows = pl.ds(piece * CHUNK, CHUNK)
        power = None
        for mode in range(2):
            for part in range(2):
                value = probe_rows(part, mode, piece)
                power = value * value if power is None else power + value * value
        power_out[rows, :] = power
        weight = None
        for scan in range(2):
            for part in range(2):
                value = windows[scan, part, rows, :]
                weight = value * value if weight is None else weight + value * value
        for slot in range(CHUNK // 8):
            sums[piece * (CHUNK // 8) + slot, 4] = weight[slot * 8 : slot * 8 + 8]

    lax.fori_loop(0, 4, backward, 0, unroll=4)

    def scatter(scan, carry):
        row, column = offsets_ref[0, 0, scan, 0] + HALF, offsets_ref[0, 0, scan, 1] + HALF
        inner = lax.rem(row, 8)
        base = pl.multiple_of(row - inner, 8)
        turn, keep = lax.rem(column, TILE), lane >= column
        zero = jnp.zeros((CHUNK // 8, 8, TILE), F32)
        edge = jnp.zeros((1, 8, TILE), F32)
        stay = lax.broadcasted_iota(jnp.int32, (CHUNK // 8 + 1, 8, TILE), 1) >= inner
        for channel in range(2):
            for piece in range(SIDE // CHUNK):
                halves = []
                for b in range(2):
                    value = contrib[scan, channel, pl.ds(piece * CHUNK, CHUNK), pl.ds(b * TILE, TILE)]
                    halves.append(pltpu.roll(value.reshape(CHUNK // 8, 8, TILE), turn, 2))
                thirds = (
                    jnp.where(keep, halves[0], zero),
                    jnp.where(keep, halves[1], halves[0]),
                    jnp.where(keep, zero, halves[1]),
                )
                place = pl.ds(base + piece * CHUNK, CHUNK + 8)
                for b in range(3):
                    value = pltpu.roll(thirds[b], inner, 1)
                    value = jnp.where(
                        stay,
                        jnp.concatenate([value, edge]),
                        jnp.concatenate([edge, value]),
                    )
                    total[channel, place, pl.ds(b * TILE, TILE)] += value.reshape(CHUNK + 8, TILE)
        return carry

    done = len(copies)
    start(sums.at[pl.ds(core * GROUPS, GROUPS)], mine_out)
    start(sums.at[pl.ds((1 - core) * GROUPS, GROUPS)], other_out)
    lax.fori_loop(0, 2, scatter, 0)
    for block, ref in enumerate((grad_second, grad_middle, grad_first)):
        for column in range(3):
            start(total.at[:, third(across[block]), third(along[column])], ref.at[column])
    for copy in copies[done:]:
        copy.wait()


def weigh_kernel(parity_ref, near_ref, power_ref, out_ref, padded):
    padded[...] = jnp.zeros_like(padded)
    padded[pl.ds(TILE, SIDE), pl.ds(TILE, SIDE)] = power_ref[...]
    lane = lax.broadcasted_iota(jnp.int32, (TILE // 8, 8, TILE), 2)
    sublane = lax.broadcasted_iota(jnp.int32, (TILE // 8, 8, TILE), 1)

    def add(index, total):
        place, scan = index // 2, index % 2
        across, along = place // 3, place % 3
        across = 1 + (across - 1) * (1 - 2 * parity_ref[0])
        along = 1 + (along - 1) * (1 - 2 * parity_ref[1])
        row, column = near_ref[place, 2 * scan], near_ref[place, 2 * scan + 1]
        column = jnp.where(row == 0, 0, 2 * TILE - along * TILE - (column - SHIFT))
        row = jnp.where(row == 0, WIDE, 2 * TILE - across * TILE - (row - SHIFT))
        inner = lax.rem(row, 8)
        base = pl.multiple_of(row - inner, 8)
        offset = lax.rem(column, TILE)
        block = pl.multiple_of(column - offset, TILE)
        turned = []
        for b in range(2):
            rows = padded[pl.ds(base, TILE + 8), pl.ds(block + b * TILE, TILE)]
            rows = pltpu.roll(rows.reshape(TILE // 8 + 1, 8, TILE), lax.rem(8 - inner, 8), 1)
            rows = jnp.where(sublane < 8 - inner, rows[:-1], rows[1:])
            turned.append(pltpu.roll(rows, lax.rem(TILE - offset, TILE), 2))
        return total + jnp.where(lane < TILE - offset, turned[0], turned[1])

    total = lax.fori_loop(0, 18, add, jnp.zeros((TILE // 8, 8, TILE), F32))
    out_ref[...] = total.reshape(TILE, TILE)


def spread_kernel(pieces_ref, out_ref):
    total = pieces_ref[0]
    for piece in range(1, GROUPS):
        total = total + pieces_ref[piece]
    for copy in range(DEPTH):
        out_ref[copy] = total


def update_kernel(pieces_ref, old_ref, out_ref, new_ref):
    total = pieces_ref[0]
    for piece in range(1, DEPTH):
        total = total + pieces_ref[piece]
    new = old_ref[...] + PROBE_STEP * total[:4] / (total[4:] + PROBE_REG)
    new_ref[...] = new
    for copy in range(GROUPS):
        out_ref[copy] = new


VMEM_SPEC = pl.BlockSpec(memory_space=pltpu.VMEM)
SMEM_SPEC = pl.BlockSpec(memory_space=pltpu.SMEM)
ANY_SPEC = pl.BlockSpec(memory_space=pl.ANY)


def in_hbm(value):
    return pltpu.with_memory_space_constraint(value, pltpu.HBM)


def params(mebibytes):
    return pltpu.CompilerParams(vmem_limit_bytes=mebibytes * 2**20)


def sort_measured(measured):
    return pl.pallas_call(
        sort_kernel,
        out_shape=jax.ShapeDtypeStruct((2, 2, HALF, SIDE), F32),
        in_specs=[VMEM_SPEC],
        out_specs=VMEM_SPEC,
        compiler_params=params(8),
        name="sort_measured",
    )(measured)


def step(offsets, parity, table, probe, measured, around):
    halves = len(probe) - 1
    band = jax.ShapeDtypeStruct((3, 2, TILE, TILE), F32)
    half = jax.ShapeDtypeStruct((GROUPS, 5, 8, SIDE), F32)
    return pl.pallas_call(
        functools.partial(step_kernel, halves),
        out_shape=[half, half, band, band, band, jax.ShapeDtypeStruct((SIDE, SIDE), F32)],
        in_specs=[SMEM_SPEC, SMEM_SPEC] + [ANY_SPEC] * (8 + halves),
        out_specs=[ANY_SPEC] * 5 + [VMEM_SPEC],
        scratch_shapes=[
            pltpu.VMEM(table.shape, BF16),
            pltpu.VMEM((4, 2 * GROUPS, 8, SIDE), F32),
            pltpu.VMEM(measured.shape, F32),
            pltpu.VMEM((2, WIDE + 8, WIDE), F32),
            pltpu.VMEM((2, 2, SIDE, SIDE), F32),
            pltpu.VMEM((2, 2, SIDE, SIDE), BF16),
            pltpu.VMEM((2, 2, SIDE, SIDE), BF16),
            pltpu.VMEM((4, 2, SIDE, SIDE), F32),
            pltpu.VMEM((2, SIDE, SIDE), F32),
            pltpu.VMEM((2, 2, SIDE, SIDE), F32),
            pltpu.VMEM((2, WIDE + 8, WIDE), F32),
            pltpu.VMEM((2 * GROUPS, 5, 8, SIDE), F32),
            pltpu.SemaphoreType.DMA((32,)),
        ],
        compiler_params=params(20),
        name="step",
    )(offsets, parity, table, *probe, measured, *around)


def pairs(first):
    both = [(i, i + 1) for i in range(first, 15, 2)]
    return both + [(j, i) for i, j in both]


def neighbourhood(tile):
    inner = lax.ppermute(tile, "col", pairs(0))
    outer = lax.ppermute(tile, "col", pairs(1))
    band = jnp.stack([outer, tile, inner])
    first = lax.ppermute(band, "row", pairs(0))
    second = lax.ppermute(band, "row", pairs(1))
    return outer, tile, inner, second, first


def after(value, other):
    return lax.optimization_barrier((value, other))[0]


def places(device):
    row, column = divmod(device, 16)
    return (column // 8) * 4 + row // 4, row % 4, column // 2 % 4, column % 2


def grouped(key):
    groups = {}
    for device in range(256):
        groups.setdefault(key(*places(device)), []).append(device)
    return list(groups.values())


PLANES = grouped(lambda z, y, x, core: (z, core))
LINES = grouped(lambda z, y, x, core: (y, x, core))
BOTH = ("row", "col")
SWAP = [(i, i ^ 1) for i in range(16)]


def exchange(value, groups):
    return lax.all_to_all(value, BOTH, 0, 0, axis_index_groups=groups, tiled=True)


def weigh(parity, near, power):
    return pl.pallas_call(
        weigh_kernel,
        out_shape=jax.ShapeDtypeStruct((TILE, TILE), F32),
        in_specs=[SMEM_SPEC, SMEM_SPEC, VMEM_SPEC],
        out_specs=VMEM_SPEC,
        scratch_shapes=[pltpu.VMEM((4 * TILE + 8, 5 * TILE), F32)],
        compiler_params=params(8),
        name="weigh",
    )(parity, near, power)


def offsets_near(outer, tile, inner, second, first):
    rows = [[band[i, 0, TILE, :4] for i in range(3)] for band in (second, first)]
    rows.insert(1, [piece[0, TILE, :4] for piece in (outer, tile, inner)])
    return jnp.stack([value for row in rows for value in row]).astype(jnp.int32)


def mark(offsets, tile):
    return pl.pallas_call(
        mark_kernel,
        out_shape=jax.ShapeDtypeStruct((2, TILE + 8, TILE), F32),
        in_specs=[SMEM_SPEC, pl.BlockSpec()],
        compiler_params=params(4),
        name="mark",
    )(offsets, tile)


def lay_out(whose, parity, half, into=None):
    return pl.pallas_call(
        functools.partial(lay_out_kernel, whose),
        out_shape=jax.ShapeDtypeStruct((4, 2 * GROUPS, 8, SIDE), F32),
        in_specs=[SMEM_SPEC] + [ANY_SPEC] * (1 + whose),
        out_specs=ANY_SPEC,
        scratch_shapes=[pltpu.SemaphoreType.DMA((4,))],
        input_output_aliases={2: 0} if whose else {},
        compiler_params=params(4),
        name="lay_out",
    )(parity, half, *([into] if whose else []))


def spread(pieces):
    return pl.pallas_call(
        spread_kernel,
        out_shape=jax.ShapeDtypeStruct((DEPTH, 5, 8, SIDE), F32),
        compiler_params=params(8),
        name="spread",
    )(pieces)


def update(pieces, old):
    return pl.pallas_call(
        update_kernel,
        out_shape=[
            jax.ShapeDtypeStruct((GROUPS, 4, 8, SIDE), F32),
            jax.ShapeDtypeStruct((4, 8, SIDE), F32),
        ],
        compiler_params=params(8),
        name="update",
    )(pieces, old)


def local(object_field, probe, amplitudes, offsets):
    table = in_hbm(jnp.asarray(tables()))
    row, column = lax.axis_index("row"), lax.axis_index("col")
    core = column & 1
    group = core * GROUPS + (row & 3) * 4 + (lax.shift_right_logical(column, 1) & 3)
    probe = probe.reshape(4, 2 * GROUPS, 8, SIDE)
    old = lax.dynamic_index_in_dim(probe, group, 1, False)
    parity = jnp.stack([row & 1, core])
    measured = sort_measured(amplitudes[0, 0])
    parts = (in_hbm(probe),)
    tile = object_field
    around = neighbourhood(mark(offsets, tile))
    near = offsets_near(*around)
    for iteration in range(ITERS):
        mine, other, second, middle, first, power = step(
            offsets, parity, table, parts, measured, around
        )
        mine = mine + lax.ppermute(other, "col", SWAP)
        first = lax.ppermute(after(first, mine), "row", pairs(0))
        second = lax.ppermute(after(second, mine), "row", pairs(1))
        weight = weigh(parity, near, after(power, mine))
        pieces = spread(after(exchange(mine, PLANES), weight))
        middle = after(middle, pieces)
        outer, own, inner = (middle[i] + first[i] + second[i] for i in range(3))
        folds = (outer, own, inner)
        inner = lax.ppermute(inner, "col", pairs(0))
        outer = lax.ppermute(outer, "col", pairs(1))
        pieces = after(exchange(pieces, LINES), folds)
        pieces, old = update(pieces, old)
        totals = after(own, old) + inner + outer
        tile = tile + OBJECT_STEP * totals / (weight + OBJECT_REG)
        if iteration + 1 < ITERS:
            around = neighbourhood(tile)
        mine = exchange(pieces, PLANES)
        if iteration + 1 == ITERS:
            mine = after(mine, (inner, outer))
        parts = (mine, lax.ppermute(mine, "col", SWAP))
    mine, other = parts
    probe = lay_out(1, parity, other, lay_out(0, parity, mine))
    return (tile, probe.reshape(2, 2, SIDE, SIDE))


def solution(mesh):
    return jax.shard_map(
        local,
        mesh=mesh,
        in_specs=(
            P(None, "row", "col"),
            P(),
            P("row", "col", None, None, None),
            P("row", "col", None, None),
        ),
        out_specs=(P(None, "row", "col"), P()),
        check_vma=False,
    )
```

```python
import functools
import math

import jax
import jax.numpy as jnp
import ml_dtypes
import numpy as np
from jax import lax
from jax.experimental import pallas as pl
from jax.experimental.pallas import tpu as pltpu
from jax.sharding import PartitionSpec as P

ITERS = 2
FLOOR = 0.5
OBJECT_STEP = 0.5
OBJECT_REG = 0.5
PROBE_STEP = 1.0
PROBE_REG = 1.0
TILE = 128
SIDE = 256
HALF = SIDE // 2
WIDE = 3 * TILE
CHUNK = 64
GROUPS = 16
DEPTH = 8
SHIFT = TILE + 1
F32 = jnp.float32
BF16 = jnp.bfloat16


def split_np(table):
    high = table.astype(np.float32).astype(ml_dtypes.bfloat16)
    low = (table - high.astype(np.float64)).astype(np.float32).astype(ml_dtypes.bfloat16)
    return np.stack([high, low])


def tables():
    out = []
    for parity in range(2):
        u = 2 * np.arange(HALF)[:, None] + parity
        angle = 2.0 * math.pi * ((u * np.arange(HALF)[None, :]) % SIDE) / SIDE
        cos, sin = np.cos(angle) / 16.0, np.sin(angle) / 16.0
        forward = np.block([[cos, sin], [-sin, cos]])
        out.append(np.stack([split_np(forward), split_np(forward.T)]))
    return np.stack(out)


def split(x):
    high = x.astype(BF16)
    return high, (x - high.astype(F32)).astype(BF16)


def split_whole(x):
    high = x.astype(BF16)
    rest = x - high.astype(F32)
    middle = rest.astype(BF16)
    return high, middle, (rest - middle.astype(F32)).astype(BF16)


def dot(a, b):
    return jnp.dot(a, b, preferred_element_type=F32)


def sort_kernel(measured_ref, out_ref):
    source = lax.broadcasted_iota(jnp.int32, (SIDE, SIDE), 0)
    place = lax.broadcasted_iota(jnp.int32, (SIDE, SIDE), 1)
    wanted = jnp.where(place < HALF, 2 * place, 2 * place - (SIDE - 1))
    select = jnp.where(source == wanted, 1.0, 0.0).astype(BF16)
    wanted = jnp.where(source < HALF, 2 * source, 2 * source - (SIDE - 1))
    select_rows = jnp.where(place == wanted, 1.0, 0.0).astype(BF16)
    for scan in range(2):
        high, middle, low = split_whole(measured_ref[scan])
        turned = (dot(low, select) + dot(middle, select)) + dot(high, select)
        high, middle, low = split_whole(turned)
        turned = (dot(select_rows, low) + dot(select_rows, middle)) + dot(select_rows, high)
        out_ref[scan, 0] = turned[:HALF]
        out_ref[scan, 1] = turned[HALF:]


def lay_out_kernel(parity_ref, mine_ref, other_ref, out_ref):
    for half, ref in enumerate((mine_ref, other_ref)):
        place = parity_ref[1] if half == 0 else 1 - parity_ref[1]
        for part in range(4):
            out_ref[part, pl.ds(place * GROUPS, GROUPS)] = ref[:, part]


def step_kernel(halves, offsets_ref, parity_ref, table_in, *refs):
    probe_in, refs = refs[: 1 + halves], refs[1 + halves :]
    (
        measured_in,
        *around_in,
        mine_out,
        other_out,
        grad_second,
        grad_middle,
        grad_first,
        power_out,
        table_ref,
        probe,
        measured_ref,
        padded,
        windows,
        folded,
        stacked,
        far,
        back,
        contrib,
        total,
        sums,
        semaphores,
    ) = refs
    row_parity, core = parity_ref[0], parity_ref[1]
    across = (row_parity * 2, 1, 2 - row_parity * 2)
    along = (core * 2, 1, 2 - core * 2)
    copies = []

    def start(source, target):
        copy = pltpu.make_async_copy(source, target, semaphores.at[len(copies)])
        copy.start()
        copies.append(copy)

    def third(block):
        return pl.ds(block * TILE if isinstance(block, int) else pl.multiple_of(block * TILE, TILE), TILE)

    for place, piece in enumerate(around_in):
        rows, columns = third(across[place // 3]), third(along[place % 3])
        start(piece.at[:, third(0)], padded.at[:, rows, columns])
    near = len(copies)
    if halves:
        for half, ref in enumerate(probe_in):
            place = core if half == 0 else 1 - core
            for part in range(4):
                start(ref.at[:, part], probe.at[part, pl.ds(place * GROUPS, GROUPS)])
    else:
        start(probe_in[0], probe)
    start(table_in, table_ref)
    operands = len(copies)
    start(measured_in, measured_ref)

    def probe_rows(part, mode, piece, columns=slice(None)):
        groups = pl.ds(piece * (CHUNK // 8), CHUNK // 8)
        value = probe[2 * part + mode, groups, :, columns]
        return value.reshape(CHUNK, value.shape[-1])

    lane = lax.broadcasted_iota(jnp.int32, (CHUNK // 8, 8, TILE), 2)
    sublane = lax.broadcasted_iota(jnp.int32, (CHUNK // 8, 8, TILE), 1)
    for channel in range(2):
        total[channel] = jnp.zeros((WIDE + 8, WIDE), F32)
    for copy in copies[:near]:
        copy.wait()

    def cut(scan, carry):
        row, column = offsets_ref[0, 0, scan, 0] + HALF, offsets_ref[0, 0, scan, 1] + HALF
        inner = lax.rem(row, 8)
        base = pl.multiple_of(row - inner, 8)
        turn, keep = lax.rem(TILE - column, TILE), lane < TILE - column
        lift, stay = lax.rem(8 - inner, 8), sublane < 8 - inner
        for channel in range(2):
            for piece in range(SIDE // CHUNK):
                turned = []
                for b in range(3):
                    rows = padded[channel, pl.ds(base + piece * CHUNK, CHUNK + 8), pl.ds(b * TILE, TILE)]
                    rows = pltpu.roll(rows.reshape(CHUNK // 8 + 1, 8, TILE), lift, 1)
                    rows = jnp.where(stay, rows[:-1], rows[1:])
                    turned.append(pltpu.roll(rows, turn, 2))
                for b in range(2):
                    windows[scan, channel, pl.ds(piece * CHUNK, CHUNK), pl.ds(b * TILE, TILE)] = (
                        jnp.where(keep, turned[b], turned[b + 1]).reshape(CHUNK, TILE)
                    )
        return carry

    lax.fori_loop(0, 2, cut, 0)
    for copy in copies[near:operands]:
        copy.wait()

    def forward(image, carry):
        scan, mode = image // 2, image % 2
        for piece in range(SIDE // CHUNK):
            rows = pl.ds(piece * CHUNK, CHUNK)
            p_re, p_im = probe_rows(0, mode, piece), probe_rows(1, mode, piece)
            w_re, w_im = windows[scan, 0, rows, :], windows[scan, 1, rows, :]
            e_re = p_re * w_re - p_im * w_im
            e_im = p_re * w_im + p_im * w_re
            for parity in range(2):
                sign = 1.0 if parity == 0 else -1.0
                for part, value in enumerate((e_re, e_im)):
                    half = value[:, :HALF] + sign * value[:, HALF:]
                    high, low = split(half)
                    folded[parity, 0, rows, part * HALF : (part + 1) * HALF] = high
                    folded[parity, 1, rows, part * HALF : (part + 1) * HALF] = low
        for parity in range(2):
            out = (
                dot(folded[parity, 1], table_ref[parity, 1, 0])
                + dot(folded[parity, 0], table_ref[parity, 1, 1])
                + dot(folded[parity, 0], table_ref[parity, 1, 0])
            )
            for other in range(2):
                sign = 1.0 if other == 0 else -1.0
                half = out[:HALF] + sign * out[HALF:]
                high, low = split(half)
                place = pl.ds(parity * HALF, HALF)
                stacked[other, 0, 0:HALF, place] = high[:, :HALF]
                stacked[other, 0, HALF:, place] = high[:, HALF:]
                stacked[other, 1, 0:HALF, place] = low[:, :HALF]
                stacked[other, 1, HALF:, place] = low[:, HALF:]
        for other in range(2):
            far[image, other] = (
                dot(table_ref[other, 0, 0], stacked[other, 1])
                + dot(table_ref[other, 0, 1], stacked[other, 0])
                + dot(table_ref[other, 0, 0], stacked[other, 0])
            )
        return carry

    lax.fori_loop(0, 4, forward, 0, unroll=4)

    def scale(index, carry):
        scan, other = index // 2, index % 2
        for piece in range(HALF // 32):
            upper, lower = pl.ds(piece * 32, 32), pl.ds(HALF + piece * 32, 32)
            parts = [
                far[2 * scan + mode, other, rows, :] for mode in range(2) for rows in (upper, lower)
            ]
            intensity = (parts[0] * parts[0] + parts[1] * parts[1]) + (
                parts[2] * parts[2] + parts[3] * parts[3]
            )
            measured = measured_ref[scan, other, upper, :]
            factor = measured / jnp.maximum(jnp.sqrt(intensity), FLOOR) - 1.0
            for mode in range(2):
                far[2 * scan + mode, other, upper, :] = parts[2 * mode] * factor
                far[2 * scan + mode, other, lower, :] = parts[2 * mode + 1] * factor
        return carry

    copies[operands].wait()
    lax.fori_loop(0, 4, scale, 0)

    def backward(image, carry):
        scan, mode = image // 2, image % 2
        halves = []
        for other in range(2):
            high, low = split(far[image, other])
            halves.append(
                dot(table_ref[other, 1, 0], low)
                + dot(table_ref[other, 1, 1], high)
                + dot(table_ref[other, 1, 0], high)
            )
        for place, value in ((0, halves[0] + halves[1]), (HALF, halves[0] - halves[1])):
            high, low = split(value)
            for parity in range(2):
                columns = slice(parity * HALF, (parity + 1) * HALF)
                for part in range(2):
                    rows = slice(part * HALF, (part + 1) * HALF)
                    target = pl.ds(part * HALF, HALF)
                    folded[parity, 0, pl.ds(place, HALF), target] = high[rows, columns]
                    folded[parity, 1, pl.ds(place, HALF), target] = low[rows, columns]
        for parity in range(2):
            back[parity] = (
                dot(folded[parity, 1], table_ref[parity, 0, 0])
                + dot(folded[parity, 0], table_ref[parity, 0, 1])
                + dot(folded[parity, 0], table_ref[parity, 0, 0])
            )
        first_scan, first_mode = scan == 0, mode == 0
        for piece in range(SIDE // CHUNK):
            rows = pl.ds(piece * CHUNK, CHUNK)
            even, odd = back[0, rows, :], back[1, rows, :]
            for b in range(2):
                columns = pl.ds(b * HALF, HALF)
                sign = 1.0 if b == 0 else -1.0
                b_re = even[:, :HALF] + sign * odd[:, :HALF]
                b_im = even[:, HALF:] + sign * odd[:, HALF:]
                p_re = probe_rows(0, mode, piece, columns)
                p_im = probe_rows(1, mode, piece, columns)
                w_re, w_im = windows[scan, 0, rows, columns], windows[scan, 1, rows, columns]
                o_re = p_re * b_re + p_im * b_im
                o_im = p_re * b_im - p_im * b_re
                zero = jnp.zeros_like(o_re)
                contrib[scan, 0, rows, columns] = o_re + jnp.where(
                    first_mode, zero, contrib[scan, 0, rows, columns]
                )
                contrib[scan, 1, rows, columns] = o_im + jnp.where(
                    first_mode, zero, contrib[scan, 1, rows, columns]
                )
                g_re = w_re * b_re + w_im * b_im
                g_im = w_re * b_im - w_im * b_re
                for slot in range(CHUNK // 8):
                    group = piece * (CHUNK // 8) + slot
                    inner = slice(slot * 8, slot * 8 + 8)
                    for part, value in enumerate((g_re, g_im)):
                        place = 2 * part + mode
                        old = sums[group, place, :, columns]
                        sums[group, place, :, columns] = value[inner] + jnp.where(
                            first_scan, jnp.zeros_like(old), old
                        )

        return carry

    for piece in range(SIDE // CHUNK):
        rows = pl.ds(piece * CHUNK, CHUNK)
        power = None
        for mode in range(2):
            for part in range(2):
                value = probe_rows(part, mode, piece)
                power = value * value if power is None else power + value * value
        power_out[rows, :] = power
        weight = None
        for scan in range(2):
            for part in range(2):
                value = windows[scan, part, rows, :]
                weight = value * value if weight is None else weight + value * value
        for slot in range(CHUNK // 8):
            sums[piece * (CHUNK // 8) + slot, 4] = weight[slot * 8 : slot * 8 + 8]

    lax.fori_loop(0, 4, backward, 0, unroll=4)

    def scatter(scan, carry):
        row, column = offsets_ref[0, 0, scan, 0] + HALF, offsets_ref[0, 0, scan, 1] + HALF
        inner = lax.rem(row, 8)
        base = pl.multiple_of(row - inner, 8)
        turn, keep = lax.rem(column, TILE), lane >= column
        zero = jnp.zeros((CHUNK // 8, 8, TILE), F32)
        edge = jnp.zeros((1, 8, TILE), F32)
        stay = lax.broadcasted_iota(jnp.int32, (CHUNK // 8 + 1, 8, TILE), 1) >= inner
        for channel in range(2):
            for piece in range(SIDE // CHUNK):
                halves = []
                for b in range(2):
                    value = contrib[scan, channel, pl.ds(piece * CHUNK, CHUNK), pl.ds(b * TILE, TILE)]
                    halves.append(pltpu.roll(value.reshape(CHUNK // 8, 8, TILE), turn, 2))
                thirds = (
                    jnp.where(keep, halves[0], zero),
                    jnp.where(keep, halves[1], halves[0]),
                    jnp.where(keep, zero, halves[1]),
                )
                place = pl.ds(base + piece * CHUNK, CHUNK + 8)
                for b in range(3):
                    value = pltpu.roll(thirds[b], inner, 1)
                    value = jnp.where(
                        stay,
                        jnp.concatenate([value, edge]),
                        jnp.concatenate([edge, value]),
                    )
                    total[channel, place, pl.ds(b * TILE, TILE)] += value.reshape(CHUNK + 8, TILE)
        return carry

    done = len(copies)
    start(sums.at[pl.ds(core * GROUPS, GROUPS)], mine_out)
    start(sums.at[pl.ds((1 - core) * GROUPS, GROUPS)], other_out)
    lax.fori_loop(0, 2, scatter, 0)
    for block, ref in enumerate((grad_second, grad_middle, grad_first)):
        for column in range(3):
            start(total.at[:, third(across[block]), third(along[column])], ref.at[column])
    for copy in copies[done:]:
        copy.wait()


def weigh_kernel(parity_ref, near_ref, power_ref, out_ref, padded):
    padded[...] = jnp.zeros_like(padded)
    padded[pl.ds(TILE, SIDE), pl.ds(TILE, SIDE)] = power_ref[...]
    lane = lax.broadcasted_iota(jnp.int32, (TILE // 8, 8, TILE), 2)
    sublane = lax.broadcasted_iota(jnp.int32, (TILE // 8, 8, TILE), 1)

    def add(index, total):
        place, scan = index // 2, index % 2
        across, along = place // 3, place % 3
        across = 1 + (across - 1) * (1 - 2 * parity_ref[0])
        along = 1 + (along - 1) * (1 - 2 * parity_ref[1])
        row, column = near_ref[place, 2 * scan], near_ref[place, 2 * scan + 1]
        column = jnp.where(row == 0, 0, 2 * TILE - along * TILE - (column - SHIFT))
        row = jnp.where(row == 0, WIDE, 2 * TILE - across * TILE - (row - SHIFT))
        inner = lax.rem(row, 8)
        base = pl.multiple_of(row - inner, 8)
        offset = lax.rem(column, TILE)
        block = pl.multiple_of(column - offset, TILE)
        turned = []
        for b in range(2):
            rows = padded[pl.ds(base, TILE + 8), pl.ds(block + b * TILE, TILE)]
            rows = pltpu.roll(rows.reshape(TILE // 8 + 1, 8, TILE), lax.rem(8 - inner, 8), 1)
            rows = jnp.where(sublane < 8 - inner, rows[:-1], rows[1:])
            turned.append(pltpu.roll(rows, lax.rem(TILE - offset, TILE), 2))
        return total + jnp.where(lane < TILE - offset, turned[0], turned[1])

    total = lax.fori_loop(0, 18, add, jnp.zeros((TILE // 8, 8, TILE), F32))
    out_ref[...] = total.reshape(TILE, TILE)


def spread_kernel(pieces_ref, out_ref):
    total = pieces_ref[0]
    for piece in range(1, GROUPS):
        total = total + pieces_ref[piece]
    for copy in range(DEPTH):
        out_ref[copy] = total


def update_kernel(pieces_ref, old_ref, out_ref, new_ref):
    total = pieces_ref[0]
    for piece in range(1, DEPTH):
        total = total + pieces_ref[piece]
    new = old_ref[...] + PROBE_STEP * total[:4] / (total[4:] + PROBE_REG)
    new_ref[...] = new
    for copy in range(GROUPS):
        out_ref[copy] = new


VMEM_SPEC = pl.BlockSpec(memory_space=pltpu.VMEM)
SMEM_SPEC = pl.BlockSpec(memory_space=pltpu.SMEM)
ANY_SPEC = pl.BlockSpec(memory_space=pl.ANY)


def in_hbm(value):
    return pltpu.with_memory_space_constraint(value, pltpu.HBM)


def params(mebibytes):
    return pltpu.CompilerParams(vmem_limit_bytes=mebibytes * 2**20)


def sort_measured(measured):
    return pl.pallas_call(
        sort_kernel,
        out_shape=jax.ShapeDtypeStruct((2, 2, HALF, SIDE), F32),
        in_specs=[VMEM_SPEC],
        out_specs=VMEM_SPEC,
        compiler_params=params(8),
        name="sort_measured",
    )(measured)


def step(offsets, parity, table, probe, measured, around):
    halves = len(probe) - 1
    band = jax.ShapeDtypeStruct((3, 2, TILE, TILE), F32)
    half = jax.ShapeDtypeStruct((GROUPS, 5, 8, SIDE), F32)
    return pl.pallas_call(
        functools.partial(step_kernel, halves),
        out_shape=[half, half, band, band, band, jax.ShapeDtypeStruct((SIDE, SIDE), F32)],
        in_specs=[SMEM_SPEC, SMEM_SPEC] + [ANY_SPEC] * (12 + halves),
        out_specs=[ANY_SPEC] * 5 + [VMEM_SPEC],
        scratch_shapes=[
            pltpu.VMEM(table.shape, BF16),
            pltpu.VMEM((4, 2 * GROUPS, 8, SIDE), F32),
            pltpu.VMEM(measured.shape, F32),
            pltpu.VMEM((2, WIDE + 8, WIDE), F32),
            pltpu.VMEM((2, 2, SIDE, SIDE), F32),
            pltpu.VMEM((2, 2, SIDE, SIDE), BF16),
            pltpu.VMEM((2, 2, SIDE, SIDE), BF16),
            pltpu.VMEM((4, 2, SIDE, SIDE), F32),
            pltpu.VMEM((2, SIDE, SIDE), F32),
            pltpu.VMEM((2, 2, SIDE, SIDE), F32),
            pltpu.VMEM((2, WIDE + 8, WIDE), F32),
            pltpu.VMEM((2 * GROUPS, 5, 8, SIDE), F32),
            pltpu.SemaphoreType.DMA((32,)),
        ],
        compiler_params=params(20),
        name="step",
    )(offsets, parity, table, *probe, measured, *around)


def pairs(first):
    both = [(i, i + 1) for i in range(first, 15, 2)]
    return both + [(j, i) for i, j in both]


def neighbourhood(tile):
    outer, inner = lax.ppermute(tile, "col", pairs(1)), lax.ppermute(tile, "col", pairs(0))
    second, first = lax.ppermute(tile, "row", pairs(1)), lax.ppermute(tile, "row", pairs(0))
    return (
        lax.ppermute(outer, "row", pairs(1)),
        second,
        lax.ppermute(second, "col", pairs(0)),
        outer,
        tile,
        inner,
        lax.ppermute(outer, "row", pairs(0)),
        first,
        lax.ppermute(first, "col", pairs(0)),
    )


def after(value, other):
    return lax.optimization_barrier((value, other))[0]


def places(device):
    row, column = divmod(device, 16)
    return (column // 8) * 4 + row // 4, row % 4, column // 2 % 4, column % 2


def grouped(key):
    groups = {}
    for device in range(256):
        groups.setdefault(key(*places(device)), []).append(device)
    return list(groups.values())


PLANES = grouped(lambda z, y, x, core: (z, core))
LINES = grouped(lambda z, y, x, core: (y, x, core))
BOTH = ("row", "col")
SWAP = [(i, i ^ 1) for i in range(16)]


def exchange(value, groups):
    return lax.all_to_all(value, BOTH, 0, 0, axis_index_groups=groups, tiled=True)


def weigh(parity, near, power):
    return pl.pallas_call(
        weigh_kernel,
        out_shape=jax.ShapeDtypeStruct((TILE, TILE), F32),
        in_specs=[SMEM_SPEC, SMEM_SPEC, VMEM_SPEC],
        out_specs=VMEM_SPEC,
        scratch_shapes=[pltpu.VMEM((4 * TILE + 8, 5 * TILE), F32)],
        compiler_params=params(8),
        name="weigh",
    )(parity, near, power)


def offsets_near(around):
    return jnp.stack([piece[0, TILE, :4] for piece in around]).astype(jnp.int32)


def spread(pieces):
    return pl.pallas_call(
        spread_kernel,
        out_shape=jax.ShapeDtypeStruct((DEPTH, 5, 8, SIDE), F32),
        compiler_params=params(8),
        name="spread",
    )(pieces)


def update(pieces, old):
    return pl.pallas_call(
        update_kernel,
        out_shape=[
            jax.ShapeDtypeStruct((GROUPS, 4, 8, SIDE), F32),
            jax.ShapeDtypeStruct((4, 8, SIDE), F32),
        ],
        compiler_params=params(8),
        name="update",
    )(pieces, old)


def local(object_field, probe, amplitudes, offsets):
    table = in_hbm(jnp.asarray(tables()))
    row, column = lax.axis_index("row"), lax.axis_index("col")
    core = column & 1
    group = core * GROUPS + (row & 3) * 4 + (lax.shift_right_logical(column, 1) & 3)
    probe = probe.reshape(4, 2 * GROUPS, 8, SIDE)
    old = lax.dynamic_index_in_dim(probe, group, 1, False)
    parity = jnp.stack([row & 1, core])
    measured = sort_measured(amplitudes[0, 0])
    parts = (in_hbm(probe),)
    tile = object_field
    marks = jnp.pad((offsets + SHIFT).astype(F32).reshape(1, 1, 4), ((0, 1), (0, 7), (0, TILE - 4)))
    around = neighbourhood(jnp.concatenate([tile, marks], axis=1))
    near = offsets_near(around)
    for iteration in range(ITERS):
        mine, other, second, middle, first, power = step(
            offsets, parity, table, parts, measured, around
        )
        mine = mine + lax.ppermute(other, "col", SWAP)
        first = lax.ppermute(after(first, mine), "row", pairs(0))
        second = lax.ppermute(after(second, mine), "row", pairs(1))
        weight = weigh(parity, near, after(power, mine))
        pieces = spread(after(exchange(mine, PLANES), weight))
        middle = after(middle, pieces)
        outer, own, inner = (middle[i] + first[i] + second[i] for i in range(3))
        folds = (outer, own, inner)
        inner = lax.ppermute(inner, "col", pairs(0))
        outer = lax.ppermute(outer, "col", pairs(1))
        pieces = after(exchange(pieces, LINES), folds)
        pieces, old = update(pieces, old)
        totals = after(own, old) + inner + outer
        tile = tile + OBJECT_STEP * totals / (weight + OBJECT_REG)
        if iteration + 1 < ITERS:
            around = neighbourhood(tile)
        mine = exchange(pieces, PLANES)
        mine = after(mine, around[1::2] if iteration + 1 < ITERS else (inner, outer))
        parts = (mine, lax.ppermute(mine, "col", SWAP))
    probe = pl.pallas_call(
        lay_out_kernel,
        out_shape=jax.ShapeDtypeStruct((4, 2 * GROUPS, 8, SIDE), F32),
        in_specs=[SMEM_SPEC, VMEM_SPEC, VMEM_SPEC],
        out_specs=VMEM_SPEC,
        compiler_params=params(8),
        name="lay_out",
    )(parity, *parts)
    return (tile, probe.reshape(2, 2, SIDE, SIDE))


def solution(mesh):
    return jax.shard_map(
        local,
        mesh=mesh,
        in_specs=(
            P(None, "row", "col"),
            P(),
            P("row", "col", None, None, None),
            P("row", "col", None, None),
        ),
        out_specs=(P(None, "row", "col"), P()),
        check_vma=False,
    )
```

```python
import functools
import math

import jax
import jax.numpy as jnp
import ml_dtypes
import numpy as np
from jax import lax
from jax.experimental import pallas as pl
from jax.experimental.pallas import tpu as pltpu
from jax.sharding import PartitionSpec as P

ITERS = 2
FLOOR = 0.5
OBJECT_STEP = 0.5
OBJECT_REG = 0.5
PROBE_STEP = 1.0
PROBE_REG = 1.0
TILE = 128
SIDE = 256
HALF = SIDE // 2
WIDE = 3 * TILE
CHUNK = 64
GROUPS = 16
DEPTH = 8
SHIFT = TILE + 1
F32 = jnp.float32
BF16 = jnp.bfloat16


def split_np(table):
    high = table.astype(np.float32).astype(ml_dtypes.bfloat16)
    low = (table - high.astype(np.float64)).astype(np.float32).astype(ml_dtypes.bfloat16)
    return np.stack([high, low])


def tables():
    out = []
    for parity in range(2):
        u = 2 * np.arange(HALF)[:, None] + parity
        angle = 2.0 * math.pi * ((u * np.arange(HALF)[None, :]) % SIDE) / SIDE
        cos, sin = np.cos(angle) / 16.0, np.sin(angle) / 16.0
        forward = np.block([[cos, sin], [-sin, cos]])
        out.append(np.stack([split_np(forward), split_np(forward.T)]))
    return np.stack(out)


def split(x):
    high = x.astype(BF16)
    return high, (x - high.astype(F32)).astype(BF16)


def split_whole(x):
    high = x.astype(BF16)
    rest = x - high.astype(F32)
    middle = rest.astype(BF16)
    return high, middle, (rest - middle.astype(F32)).astype(BF16)


def dot(a, b):
    return jnp.dot(a, b, preferred_element_type=F32)


def sort_kernel(measured_ref, out_ref):
    source = lax.broadcasted_iota(jnp.int32, (SIDE, SIDE), 0)
    place = lax.broadcasted_iota(jnp.int32, (SIDE, SIDE), 1)
    wanted = jnp.where(place < HALF, 2 * place, 2 * place - (SIDE - 1))
    select = jnp.where(source == wanted, 1.0, 0.0).astype(BF16)
    wanted = jnp.where(source < HALF, 2 * source, 2 * source - (SIDE - 1))
    select_rows = jnp.where(place == wanted, 1.0, 0.0).astype(BF16)
    for scan in range(2):
        high, middle, low = split_whole(measured_ref[scan])
        turned = (dot(low, select) + dot(middle, select)) + dot(high, select)
        high, middle, low = split_whole(turned)
        turned = (dot(select_rows, low) + dot(select_rows, middle)) + dot(select_rows, high)
        out_ref[scan, 0] = turned[:HALF]
        out_ref[scan, 1] = turned[HALF:]


def lay_out_kernel(parity_ref, mine_ref, other_ref, out_ref):
    for half, ref in enumerate((mine_ref, other_ref)):
        place = parity_ref[1] if half == 0 else 1 - parity_ref[1]
        for part in range(4):
            out_ref[part, pl.ds(place * GROUPS, GROUPS)] = ref[:, part]


def step_kernel(halves, offsets_ref, parity_ref, table_in, *refs):
    probe_in, refs = refs[: 1 + halves], refs[1 + halves :]
    (
        measured_in,
        *around_in,
        mine_out,
        other_out,
        grad_second,
        grad_middle,
        grad_first,
        power_out,
        table_ref,
        probe,
        measured_ref,
        padded,
        windows,
        folded,
        stacked,
        far,
        back,
        contrib,
        total,
        sums,
        semaphores,
    ) = refs
    row_parity, core = parity_ref[0], parity_ref[1]
    across = (row_parity * 2, 1, 2 - row_parity * 2)
    along = (core * 2, 1, 2 - core * 2)
    copies = []

    def start(source, target):
        copy = pltpu.make_async_copy(source, target, semaphores.at[len(copies)])
        copy.start()
        copies.append(copy)

    def third(block):
        return pl.ds(block * TILE if isinstance(block, int) else pl.multiple_of(block * TILE, TILE), TILE)

    if len(around_in) == 5:
        bands = around_in[3:4], around_in[:3], around_in[4:]
    else:
        bands = around_in[:3], around_in[3:6], around_in[6:]
    for row, band in enumerate(bands):
        for column in range(3):
            piece = band[0].at[column] if len(band) == 1 else band[column]
            place = padded.at[:, third(across[row]), third(along[column])]
            start(piece.at[:, third(0)], place)
    near = len(copies)
    if halves:
        for half, ref in enumerate(probe_in):
            place = core if half == 0 else 1 - core
            for part in range(4):
                start(ref.at[:, part], probe.at[part, pl.ds(place * GROUPS, GROUPS)])
    else:
        start(probe_in[0], probe)
    start(table_in, table_ref)
    operands = len(copies)
    start(measured_in, measured_ref)

    def probe_rows(part, mode, piece, columns=slice(None)):
        groups = pl.ds(piece * (CHUNK // 8), CHUNK // 8)
        value = probe[2 * part + mode, groups, :, columns]
        return value.reshape(CHUNK, value.shape[-1])

    lane = lax.broadcasted_iota(jnp.int32, (CHUNK // 8, 8, TILE), 2)
    sublane = lax.broadcasted_iota(jnp.int32, (CHUNK // 8, 8, TILE), 1)
    for channel in range(2):
        total[channel] = jnp.zeros((WIDE + 8, WIDE), F32)
    for copy in copies[:near]:
        copy.wait()

    def cut(scan, carry):
        row, column = offsets_ref[0, 0, scan, 0] + HALF, offsets_ref[0, 0, scan, 1] + HALF
        inner = lax.rem(row, 8)
        base = pl.multiple_of(row - inner, 8)
        turn, keep = lax.rem(TILE - column, TILE), lane < TILE - column
        lift, stay = lax.rem(8 - inner, 8), sublane < 8 - inner
        for channel in range(2):
            for piece in range(SIDE // CHUNK):
                turned = []
                for b in range(3):
                    rows = padded[channel, pl.ds(base + piece * CHUNK, CHUNK + 8), pl.ds(b * TILE, TILE)]
                    rows = pltpu.roll(rows.reshape(CHUNK // 8 + 1, 8, TILE), lift, 1)
                    rows = jnp.where(stay, rows[:-1], rows[1:])
                    turned.append(pltpu.roll(rows, turn, 2))
                for b in range(2):
                    windows[scan, channel, pl.ds(piece * CHUNK, CHUNK), pl.ds(b * TILE, TILE)] = (
                        jnp.where(keep, turned[b], turned[b + 1]).reshape(CHUNK, TILE)
                    )
        return carry

    lax.fori_loop(0, 2, cut, 0)
    for copy in copies[near:operands]:
        copy.wait()

    def forward(image, carry):
        scan, mode = image // 2, image % 2
        for piece in range(SIDE // CHUNK):
            rows = pl.ds(piece * CHUNK, CHUNK)
            p_re, p_im = probe_rows(0, mode, piece), probe_rows(1, mode, piece)
            w_re, w_im = windows[scan, 0, rows, :], windows[scan, 1, rows, :]
            e_re = p_re * w_re - p_im * w_im
            e_im = p_re * w_im + p_im * w_re
            for parity in range(2):
                sign = 1.0 if parity == 0 else -1.0
                for part, value in enumerate((e_re, e_im)):
                    half = value[:, :HALF] + sign * value[:, HALF:]
                    high, low = split(half)
                    folded[parity, 0, rows, part * HALF : (part + 1) * HALF] = high
                    folded[parity, 1, rows, part * HALF : (part + 1) * HALF] = low
        for parity in range(2):
            out = (
                dot(folded[parity, 1], table_ref[parity, 1, 0])
                + dot(folded[parity, 0], table_ref[parity, 1, 1])
                + dot(folded[parity, 0], table_ref[parity, 1, 0])
            )
            for other in range(2):
                sign = 1.0 if other == 0 else -1.0
                half = out[:HALF] + sign * out[HALF:]
                high, low = split(half)
                place = pl.ds(parity * HALF, HALF)
                stacked[other, 0, 0:HALF, place] = high[:, :HALF]
                stacked[other, 0, HALF:, place] = high[:, HALF:]
                stacked[other, 1, 0:HALF, place] = low[:, :HALF]
                stacked[other, 1, HALF:, place] = low[:, HALF:]
        for other in range(2):
            far[image, other] = (
                dot(table_ref[other, 0, 0], stacked[other, 1])
                + dot(table_ref[other, 0, 1], stacked[other, 0])
                + dot(table_ref[other, 0, 0], stacked[other, 0])
            )
        return carry

    lax.fori_loop(0, 4, forward, 0, unroll=4)

    def scale(index, carry):
        scan, other = index // 2, index % 2
        for piece in range(HALF // 32):
            upper, lower = pl.ds(piece * 32, 32), pl.ds(HALF + piece * 32, 32)
            parts = [
                far[2 * scan + mode, other, rows, :] for mode in range(2) for rows in (upper, lower)
            ]
            intensity = (parts[0] * parts[0] + parts[1] * parts[1]) + (
                parts[2] * parts[2] + parts[3] * parts[3]
            )
            measured = measured_ref[scan, other, upper, :]
            factor = measured / jnp.maximum(jnp.sqrt(intensity), FLOOR) - 1.0
            for mode in range(2):
                far[2 * scan + mode, other, upper, :] = parts[2 * mode] * factor
                far[2 * scan + mode, other, lower, :] = parts[2 * mode + 1] * factor
        return carry

    copies[operands].wait()
    lax.fori_loop(0, 4, scale, 0)

    def backward(image, carry):
        scan, mode = image // 2, image % 2
        halves = []
        for other in range(2):
            high, low = split(far[image, other])
            halves.append(
                dot(table_ref[other, 1, 0], low)
                + dot(table_ref[other, 1, 1], high)
                + dot(table_ref[other, 1, 0], high)
            )
        for place, value in ((0, halves[0] + halves[1]), (HALF, halves[0] - halves[1])):
            high, low = split(value)
            for parity in range(2):
                columns = slice(parity * HALF, (parity + 1) * HALF)
                for part in range(2):
                    rows = slice(part * HALF, (part + 1) * HALF)
                    target = pl.ds(part * HALF, HALF)
                    folded[parity, 0, pl.ds(place, HALF), target] = high[rows, columns]
                    folded[parity, 1, pl.ds(place, HALF), target] = low[rows, columns]
        for parity in range(2):
            back[parity] = (
                dot(folded[parity, 1], table_ref[parity, 0, 0])
                + dot(folded[parity, 0], table_ref[parity, 0, 1])
                + dot(folded[parity, 0], table_ref[parity, 0, 0])
            )
        first_scan, first_mode = scan == 0, mode == 0
        for piece in range(SIDE // CHUNK):
            rows = pl.ds(piece * CHUNK, CHUNK)
            even, odd = back[0, rows, :], back[1, rows, :]
            for b in range(2):
                columns = pl.ds(b * HALF, HALF)
                sign = 1.0 if b == 0 else -1.0
                b_re = even[:, :HALF] + sign * odd[:, :HALF]
                b_im = even[:, HALF:] + sign * odd[:, HALF:]
                p_re = probe_rows(0, mode, piece, columns)
                p_im = probe_rows(1, mode, piece, columns)
                w_re, w_im = windows[scan, 0, rows, columns], windows[scan, 1, rows, columns]
                o_re = p_re * b_re + p_im * b_im
                o_im = p_re * b_im - p_im * b_re
                zero = jnp.zeros_like(o_re)
                contrib[scan, 0, rows, columns] = o_re + jnp.where(
                    first_mode, zero, contrib[scan, 0, rows, columns]
                )
                contrib[scan, 1, rows, columns] = o_im + jnp.where(
                    first_mode, zero, contrib[scan, 1, rows, columns]
                )
                g_re = w_re * b_re + w_im * b_im
                g_im = w_re * b_im - w_im * b_re
                for slot in range(CHUNK // 8):
                    group = piece * (CHUNK // 8) + slot
                    inner = slice(slot * 8, slot * 8 + 8)
                    for part, value in enumerate((g_re, g_im)):
                        place = 2 * part + mode
                        old = sums[group, place, :, columns]
                        sums[group, place, :, columns] = value[inner] + jnp.where(
                            first_scan, jnp.zeros_like(old), old
                        )

        return carry

    for piece in range(SIDE // CHUNK):
        rows = pl.ds(piece * CHUNK, CHUNK)
        power = None
        for mode in range(2):
            for part in range(2):
                value = probe_rows(part, mode, piece)
                power = value * value if power is None else power + value * value
        power_out[rows, :] = power
        weight = None
        for scan in range(2):
            for part in range(2):
                value = windows[scan, part, rows, :]
                weight = value * value if weight is None else weight + value * value
        for slot in range(CHUNK // 8):
            sums[piece * (CHUNK // 8) + slot, 4] = weight[slot * 8 : slot * 8 + 8]

    lax.fori_loop(0, 4, backward, 0, unroll=4)

    def scatter(scan, carry):
        row, column = offsets_ref[0, 0, scan, 0] + HALF, offsets_ref[0, 0, scan, 1] + HALF
        inner = lax.rem(row, 8)
        base = pl.multiple_of(row - inner, 8)
        turn, keep = lax.rem(column, TILE), lane >= column
        zero = jnp.zeros((CHUNK // 8, 8, TILE), F32)
        edge = jnp.zeros((1, 8, TILE), F32)
        stay = lax.broadcasted_iota(jnp.int32, (CHUNK // 8 + 1, 8, TILE), 1) >= inner
        for channel in range(2):
            for piece in range(SIDE // CHUNK):
                halves = []
                for b in range(2):
                    value = contrib[scan, channel, pl.ds(piece * CHUNK, CHUNK), pl.ds(b * TILE, TILE)]
                    halves.append(pltpu.roll(value.reshape(CHUNK // 8, 8, TILE), turn, 2))
                thirds = (
                    jnp.where(keep, halves[0], zero),
                    jnp.where(keep, halves[1], halves[0]),
                    jnp.where(keep, zero, halves[1]),
                )
                place = pl.ds(base + piece * CHUNK, CHUNK + 8)
                for b in range(3):
                    value = pltpu.roll(thirds[b], inner, 1)
                    value = jnp.where(
                        stay,
                        jnp.concatenate([value, edge]),
                        jnp.concatenate([edge, value]),
                    )
                    total[channel, place, pl.ds(b * TILE, TILE)] += value.reshape(CHUNK + 8, TILE)
        return carry

    done = len(copies)
    start(sums.at[pl.ds(core * GROUPS, GROUPS)], mine_out)
    start(sums.at[pl.ds((1 - core) * GROUPS, GROUPS)], other_out)
    lax.fori_loop(0, 2, scatter, 0)
    for block, ref in enumerate((grad_second, grad_middle, grad_first)):
        for column in range(3):
            start(total.at[:, third(across[block]), third(along[column])], ref.at[column])
    for copy in copies[done:]:
        copy.wait()


def weigh_kernel(parity_ref, near_ref, power_ref, out_ref, padded):
    padded[...] = jnp.zeros_like(padded)
    padded[pl.ds(TILE, SIDE), pl.ds(TILE, SIDE)] = power_ref[...]
    lane = lax.broadcasted_iota(jnp.int32, (TILE // 8, 8, TILE), 2)
    sublane = lax.broadcasted_iota(jnp.int32, (TILE // 8, 8, TILE), 1)

    def add(index, total):
        place, scan = index // 2, index % 2
        across, along = place // 3, place % 3
        across = 1 + (across - 1) * (1 - 2 * parity_ref[0])
        along = 1 + (along - 1) * (1 - 2 * parity_ref[1])
        row, column = near_ref[place, 2 * scan], near_ref[place, 2 * scan + 1]
        column = jnp.where(row == 0, 0, 2 * TILE - along * TILE - (column - SHIFT))
        row = jnp.where(row == 0, WIDE, 2 * TILE - across * TILE - (row - SHIFT))
        inner = lax.rem(row, 8)
        base = pl.multiple_of(row - inner, 8)
        offset = lax.rem(column, TILE)
        block = pl.multiple_of(column - offset, TILE)
        turned = []
        for b in range(2):
            rows = padded[pl.ds(base, TILE + 8), pl.ds(block + b * TILE, TILE)]
            rows = pltpu.roll(rows.reshape(TILE // 8 + 1, 8, TILE), lax.rem(8 - inner, 8), 1)
            rows = jnp.where(sublane < 8 - inner, rows[:-1], rows[1:])
            turned.append(pltpu.roll(rows, lax.rem(TILE - offset, TILE), 2))
        return total + jnp.where(lane < TILE - offset, turned[0], turned[1])

    total = lax.fori_loop(0, 18, add, jnp.zeros((TILE // 8, 8, TILE), F32))
    out_ref[...] = total.reshape(TILE, TILE)


def spread_kernel(pieces_ref, out_ref):
    total = pieces_ref[0]
    for piece in range(1, GROUPS):
        total = total + pieces_ref[piece]
    for copy in range(DEPTH):
        out_ref[copy] = total


def update_kernel(pieces_ref, old_ref, out_ref, new_ref):
    total = pieces_ref[0]
    for piece in range(1, DEPTH):
        total = total + pieces_ref[piece]
    new = old_ref[...] + PROBE_STEP * total[:4] / (total[4:] + PROBE_REG)
    new_ref[...] = new
    for copy in range(GROUPS):
        out_ref[copy] = new


VMEM_SPEC = pl.BlockSpec(memory_space=pltpu.VMEM)
SMEM_SPEC = pl.BlockSpec(memory_space=pltpu.SMEM)
ANY_SPEC = pl.BlockSpec(memory_space=pl.ANY)


def in_hbm(value):
    return pltpu.with_memory_space_constraint(value, pltpu.HBM)


def params(mebibytes):
    return pltpu.CompilerParams(vmem_limit_bytes=mebibytes * 2**20)


def sort_measured(measured):
    return pl.pallas_call(
        sort_kernel,
        out_shape=jax.ShapeDtypeStruct((2, 2, HALF, SIDE), F32),
        in_specs=[VMEM_SPEC],
        out_specs=VMEM_SPEC,
        compiler_params=params(8),
        name="sort_measured",
    )(measured)


def step(offsets, parity, table, probe, measured, around):
    halves = len(probe) - 1
    band = jax.ShapeDtypeStruct((3, 2, TILE, TILE), F32)
    half = jax.ShapeDtypeStruct((GROUPS, 5, 8, SIDE), F32)
    return pl.pallas_call(
        functools.partial(step_kernel, halves),
        out_shape=[half, half, band, band, band, jax.ShapeDtypeStruct((SIDE, SIDE), F32)],
        in_specs=[SMEM_SPEC, SMEM_SPEC] + [ANY_SPEC] * (3 + halves + len(around)),
        out_specs=[ANY_SPEC] * 5 + [VMEM_SPEC],
        scratch_shapes=[
            pltpu.VMEM(table.shape, BF16),
            pltpu.VMEM((4, 2 * GROUPS, 8, SIDE), F32),
            pltpu.VMEM(measured.shape, F32),
            pltpu.VMEM((2, WIDE + 8, WIDE), F32),
            pltpu.VMEM((2, 2, SIDE, SIDE), F32),
            pltpu.VMEM((2, 2, SIDE, SIDE), BF16),
            pltpu.VMEM((2, 2, SIDE, SIDE), BF16),
            pltpu.VMEM((4, 2, SIDE, SIDE), F32),
            pltpu.VMEM((2, SIDE, SIDE), F32),
            pltpu.VMEM((2, 2, SIDE, SIDE), F32),
            pltpu.VMEM((2, WIDE + 8, WIDE), F32),
            pltpu.VMEM((2 * GROUPS, 5, 8, SIDE), F32),
            pltpu.SemaphoreType.DMA((32,)),
        ],
        compiler_params=params(20),
        name="step",
    )(offsets, parity, table, *probe, measured, *around)


def pairs(first):
    both = [(i, i + 1) for i in range(first, 15, 2)]
    return both + [(j, i) for i, j in both]


def neighbourhood(tile):
    outer, inner = lax.ppermute(tile, "col", pairs(1)), lax.ppermute(tile, "col", pairs(0))
    second, first = lax.ppermute(tile, "row", pairs(1)), lax.ppermute(tile, "row", pairs(0))
    return (
        lax.ppermute(outer, "row", pairs(1)),
        second,
        lax.ppermute(second, "col", pairs(0)),
        outer,
        tile,
        inner,
        lax.ppermute(outer, "row", pairs(0)),
        first,
        lax.ppermute(first, "col", pairs(0)),
    )


def band_neighbourhood(tile):
    outer, inner = lax.ppermute(tile, "col", pairs(1)), lax.ppermute(tile, "col", pairs(0))
    band = jnp.stack([outer, tile, inner])
    second, first = lax.ppermute(band, "row", pairs(1)), lax.ppermute(band, "row", pairs(0))
    return outer, tile, inner, second, first


def after(value, other):
    return lax.optimization_barrier((value, other))[0]


def places(device):
    row, column = divmod(device, 16)
    return (column // 8) * 4 + row // 4, row % 4, column // 2 % 4, column % 2


def grouped(key):
    groups = {}
    for device in range(256):
        groups.setdefault(key(*places(device)), []).append(device)
    return list(groups.values())


PLANES = grouped(lambda z, y, x, core: (z, core))
LINES = grouped(lambda z, y, x, core: (y, x, core))
BOTH = ("row", "col")
SWAP = [(i, i ^ 1) for i in range(16)]


def exchange(value, groups):
    return lax.all_to_all(value, BOTH, 0, 0, axis_index_groups=groups, tiled=True)


def weigh(parity, near, power):
    return pl.pallas_call(
        weigh_kernel,
        out_shape=jax.ShapeDtypeStruct((TILE, TILE), F32),
        in_specs=[SMEM_SPEC, SMEM_SPEC, VMEM_SPEC],
        out_specs=VMEM_SPEC,
        scratch_shapes=[pltpu.VMEM((4 * TILE + 8, 5 * TILE), F32)],
        compiler_params=params(8),
        name="weigh",
    )(parity, near, power)


def offsets_near(around):
    return jnp.stack([piece[0, TILE, :4] for piece in around]).astype(jnp.int32)


def spread(pieces):
    return pl.pallas_call(
        spread_kernel,
        out_shape=jax.ShapeDtypeStruct((DEPTH, 5, 8, SIDE), F32),
        compiler_params=params(8),
        name="spread",
    )(pieces)


def update(pieces, old):
    return pl.pallas_call(
        update_kernel,
        out_shape=[
            jax.ShapeDtypeStruct((GROUPS, 4, 8, SIDE), F32),
            jax.ShapeDtypeStruct((4, 8, SIDE), F32),
        ],
        compiler_params=params(8),
        name="update",
    )(pieces, old)


def local(object_field, probe, amplitudes, offsets):
    table = in_hbm(jnp.asarray(tables()))
    row, column = lax.axis_index("row"), lax.axis_index("col")
    core = column & 1
    group = core * GROUPS + (row & 3) * 4 + (lax.shift_right_logical(column, 1) & 3)
    probe = probe.reshape(4, 2 * GROUPS, 8, SIDE)
    old = lax.dynamic_index_in_dim(probe, group, 1, False)
    parity = jnp.stack([row & 1, core])
    measured = sort_measured(amplitudes[0, 0])
    parts = (in_hbm(probe),)
    tile = object_field
    marks = jnp.pad((offsets + SHIFT).astype(F32).reshape(1, 1, 4), ((0, 1), (0, 7), (0, TILE - 4)))
    around = neighbourhood(jnp.concatenate([tile, marks], axis=1))
    near = offsets_near(around)
    for iteration in range(ITERS):
        mine, other, second, middle, first, power = step(
            offsets, parity, table, parts, measured, around
        )
        mine = mine + lax.ppermute(other, "col", SWAP)
        first = lax.ppermute(after(first, mine), "row", pairs(0))
        second = lax.ppermute(after(second, mine), "row", pairs(1))
        weight = weigh(parity, near, after(power, mine))
        pieces = spread(after(exchange(mine, PLANES), weight))
        middle = after(middle, pieces)
        outer, own, inner = (middle[i] + first[i] + second[i] for i in range(3))
        folds = (outer, own, inner)
        inner = lax.ppermute(inner, "col", pairs(0))
        outer = lax.ppermute(outer, "col", pairs(1))
        pieces = after(exchange(pieces, LINES), folds)
        pieces, old = update(pieces, old)
        totals = after(own, old) + inner + outer
        tile = tile + OBJECT_STEP * totals / (weight + OBJECT_REG)
        if iteration + 1 < ITERS:
            around = band_neighbourhood(tile)
        mine = exchange(pieces, PLANES)
        if iteration + 1 == ITERS:
            mine = after(mine, (inner, outer))
        parts = (mine, lax.ppermute(mine, "col", SWAP))
    probe = pl.pallas_call(
        lay_out_kernel,
        out_shape=jax.ShapeDtypeStruct((4, 2 * GROUPS, 8, SIDE), F32),
        in_specs=[SMEM_SPEC, VMEM_SPEC, VMEM_SPEC],
        out_specs=VMEM_SPEC,
        compiler_params=params(8),
        name="lay_out",
    )(parity, *parts)
    return (tile, probe.reshape(2, 2, SIDE, SIDE))


def solution(mesh):
    return jax.shard_map(
        local,
        mesh=mesh,
        in_specs=(
            P(None, "row", "col"),
            P(),
            P("row", "col", None, None, None),
            P("row", "col", None, None),
        ),
        out_specs=(P(None, "row", "col"), P()),
        check_vma=False,
    )
```

```python
import functools
import math

import jax
import jax.numpy as jnp
import ml_dtypes
import numpy as np
from jax import lax
from jax.experimental import pallas as pl
from jax.experimental.pallas import tpu as pltpu
from jax.sharding import PartitionSpec as P

ITERS = 2
FLOOR = 0.5
OBJECT_STEP = 0.5
OBJECT_REG = 0.5
PROBE_STEP = 1.0
PROBE_REG = 1.0
TILE = 128
SIDE = 256
HALF = SIDE // 2
WIDE = 3 * TILE
CHUNK = 64
GROUPS = 16
DEPTH = 8
SHIFT = TILE + 1
F32 = jnp.float32
BF16 = jnp.bfloat16


def split_np(table):
    high = table.astype(np.float32).astype(ml_dtypes.bfloat16)
    low = (table - high.astype(np.float64)).astype(np.float32).astype(ml_dtypes.bfloat16)
    return np.stack([high, low])


def tables():
    out = []
    for parity in range(2):
        u = 2 * np.arange(HALF)[:, None] + parity
        angle = 2.0 * math.pi * ((u * np.arange(HALF)[None, :]) % SIDE) / SIDE
        cos, sin = np.cos(angle) / 16.0, np.sin(angle) / 16.0
        forward = np.block([[cos, sin], [-sin, cos]])
        out.append(np.stack([split_np(forward), split_np(forward.T)]))
    return np.stack(out)


def split(x):
    high = x.astype(BF16)
    return high, (x - high.astype(F32)).astype(BF16)


def split_whole(x):
    high = x.astype(BF16)
    rest = x - high.astype(F32)
    middle = rest.astype(BF16)
    return high, middle, (rest - middle.astype(F32)).astype(BF16)


def dot(a, b):
    return jnp.dot(a, b, preferred_element_type=F32)


def sort_kernel(measured_ref, out_ref):
    source = lax.broadcasted_iota(jnp.int32, (SIDE, SIDE), 0)
    place = lax.broadcasted_iota(jnp.int32, (SIDE, SIDE), 1)
    wanted = jnp.where(place < HALF, 2 * place, 2 * place - (SIDE - 1))
    select = jnp.where(source == wanted, 1.0, 0.0).astype(BF16)
    wanted = jnp.where(source < HALF, 2 * source, 2 * source - (SIDE - 1))
    select_rows = jnp.where(place == wanted, 1.0, 0.0).astype(BF16)
    for scan in range(2):
        high, middle, low = split_whole(measured_ref[scan])
        turned = (dot(low, select) + dot(middle, select)) + dot(high, select)
        high, middle, low = split_whole(turned)
        turned = (dot(select_rows, low) + dot(select_rows, middle)) + dot(select_rows, high)
        out_ref[scan, 0] = turned[:HALF]
        out_ref[scan, 1] = turned[HALF:]


def lay_out_kernel(parity_ref, mine_ref, other_ref, out_ref):
    for half, ref in enumerate((mine_ref, other_ref)):
        place = parity_ref[1] if half == 0 else 1 - parity_ref[1]
        for part in range(4):
            out_ref[part, pl.ds(place * GROUPS, GROUPS)] = ref[:, part]


def step_kernel(halves, offsets_ref, parity_ref, table_in, *refs):
    probe_in, refs = refs[: 1 + halves], refs[1 + halves :]
    (
        measured_in,
        *around_in,
        mine_out,
        other_out,
        grad_second,
        grad_middle,
        grad_first,
        power_out,
        table_ref,
        probe,
        measured_ref,
        padded,
        windows,
        folded,
        stacked,
        far,
        back,
        contrib,
        total,
        sums,
        semaphores,
    ) = refs
    row_parity, core = parity_ref[0], parity_ref[1]
    across = (row_parity * 2, 1, 2 - row_parity * 2)
    along = (core * 2, 1, 2 - core * 2)
    copies = []

    def start(source, target):
        copy = pltpu.make_async_copy(source, target, semaphores.at[len(copies)])
        copy.start()
        copies.append(copy)

    def third(block):
        return pl.ds(block * TILE if isinstance(block, int) else pl.multiple_of(block * TILE, TILE), TILE)

    if len(around_in) == 5:
        bands = around_in[3:4], around_in[:3], around_in[4:]
    else:
        bands = around_in[:3], around_in[3:6], around_in[6:]
    for row, band in enumerate(bands):
        for column in range(3):
            piece = band[0].at[column] if len(band) == 1 else band[column]
            place = padded.at[:, third(across[row]), third(along[column])]
            start(piece.at[:, third(0)], place)
    near = len(copies)
    if halves:
        for half, ref in enumerate(probe_in):
            place = core if half == 0 else 1 - core
            for part in range(4):
                start(ref.at[:, part], probe.at[part, pl.ds(place * GROUPS, GROUPS)])
    else:
        start(probe_in[0], probe)
    start(table_in, table_ref)
    operands = len(copies)
    start(measured_in, measured_ref)

    def probe_rows(part, mode, piece, columns=slice(None)):
        groups = pl.ds(piece * (CHUNK // 8), CHUNK // 8)
        value = probe[2 * part + mode, groups, :, columns]
        return value.reshape(CHUNK, value.shape[-1])

    lane = lax.broadcasted_iota(jnp.int32, (CHUNK // 8, 8, TILE), 2)
    sublane = lax.broadcasted_iota(jnp.int32, (CHUNK // 8, 8, TILE), 1)
    for channel in range(2):
        total[channel] = jnp.zeros((WIDE + 8, WIDE), F32)
    for copy in copies[:near]:
        copy.wait()

    def cut(scan, carry):
        row, column = offsets_ref[0, 0, scan, 0] + HALF, offsets_ref[0, 0, scan, 1] + HALF
        inner = lax.rem(row, 8)
        base = pl.multiple_of(row - inner, 8)
        turn, keep = lax.rem(TILE - column, TILE), lane < TILE - column
        lift, stay = lax.rem(8 - inner, 8), sublane < 8 - inner
        for channel in range(2):
            for piece in range(SIDE // CHUNK):
                turned = []
                for b in range(3):
                    rows = padded[channel, pl.ds(base + piece * CHUNK, CHUNK + 8), pl.ds(b * TILE, TILE)]
                    rows = pltpu.roll(rows.reshape(CHUNK // 8 + 1, 8, TILE), lift, 1)
                    rows = jnp.where(stay, rows[:-1], rows[1:])
                    turned.append(pltpu.roll(rows, turn, 2))
                for b in range(2):
                    windows[scan, channel, pl.ds(piece * CHUNK, CHUNK), pl.ds(b * TILE, TILE)] = (
                        jnp.where(keep, turned[b], turned[b + 1]).reshape(CHUNK, TILE)
                    )
        return carry

    lax.fori_loop(0, 2, cut, 0, unroll=2)
    for copy in copies[near:operands]:
        copy.wait()

    def forward(image, carry):
        scan, mode = image // 2, image % 2
        for piece in range(SIDE // CHUNK):
            rows = pl.ds(piece * CHUNK, CHUNK)
            p_re, p_im = probe_rows(0, mode, piece), probe_rows(1, mode, piece)
            w_re, w_im = windows[scan, 0, rows, :], windows[scan, 1, rows, :]
            e_re = p_re * w_re - p_im * w_im
            e_im = p_re * w_im + p_im * w_re
            for parity in range(2):
                sign = 1.0 if parity == 0 else -1.0
                for part, value in enumerate((e_re, e_im)):
                    half = value[:, :HALF] + sign * value[:, HALF:]
                    high, low = split(half)
                    folded[parity, 0, rows, part * HALF : (part + 1) * HALF] = high
                    folded[parity, 1, rows, part * HALF : (part + 1) * HALF] = low
        for parity in range(2):
            out = (
                dot(folded[parity, 1], table_ref[parity, 1, 0])
                + dot(folded[parity, 0], table_ref[parity, 1, 1])
                + dot(folded[parity, 0], table_ref[parity, 1, 0])
            )
            for other in range(2):
                sign = 1.0 if other == 0 else -1.0
                half = out[:HALF] + sign * out[HALF:]
                high, low = split(half)
                place = pl.ds(parity * HALF, HALF)
                stacked[other, 0, 0:HALF, place] = high[:, :HALF]
                stacked[other, 0, HALF:, place] = high[:, HALF:]
                stacked[other, 1, 0:HALF, place] = low[:, :HALF]
                stacked[other, 1, HALF:, place] = low[:, HALF:]
        for other in range(2):
            far[image, other] = (
                dot(table_ref[other, 0, 0], stacked[other, 1])
                + dot(table_ref[other, 0, 1], stacked[other, 0])
                + dot(table_ref[other, 0, 0], stacked[other, 0])
            )
        return carry

    lax.fori_loop(0, 4, forward, 0, unroll=4)

    def scale(index, carry):
        scan, other = index // 2, index % 2
        for piece in range(HALF // 32):
            upper, lower = pl.ds(piece * 32, 32), pl.ds(HALF + piece * 32, 32)
            parts = [
                far[2 * scan + mode, other, rows, :] for mode in range(2) for rows in (upper, lower)
            ]
            intensity = (parts[0] * parts[0] + parts[1] * parts[1]) + (
                parts[2] * parts[2] + parts[3] * parts[3]
            )
            measured = measured_ref[scan, other, upper, :]
            factor = measured / jnp.maximum(jnp.sqrt(intensity), FLOOR) - 1.0
            for mode in range(2):
                far[2 * scan + mode, other, upper, :] = parts[2 * mode] * factor
                far[2 * scan + mode, other, lower, :] = parts[2 * mode + 1] * factor
        return carry

    copies[operands].wait()
    lax.fori_loop(0, 4, scale, 0, unroll=4)

    def backward(image, carry):
        scan, mode = image // 2, image % 2
        halves = []
        for other in range(2):
            high, low = split(far[image, other])
            halves.append(
                dot(table_ref[other, 1, 0], low)
                + dot(table_ref[other, 1, 1], high)
                + dot(table_ref[other, 1, 0], high)
            )
        for place, value in ((0, halves[0] + halves[1]), (HALF, halves[0] - halves[1])):
            high, low = split(value)
            for parity in range(2):
                columns = slice(parity * HALF, (parity + 1) * HALF)
                for part in range(2):
                    rows = slice(part * HALF, (part + 1) * HALF)
                    target = pl.ds(part * HALF, HALF)
                    folded[parity, 0, pl.ds(place, HALF), target] = high[rows, columns]
                    folded[parity, 1, pl.ds(place, HALF), target] = low[rows, columns]
        for parity in range(2):
            back[parity] = (
                dot(folded[parity, 1], table_ref[parity, 0, 0])
                + dot(folded[parity, 0], table_ref[parity, 0, 1])
                + dot(folded[parity, 0], table_ref[parity, 0, 0])
            )
        first_scan, first_mode = scan == 0, mode == 0
        for piece in range(SIDE // CHUNK):
            rows = pl.ds(piece * CHUNK, CHUNK)
            even, odd = back[0, rows, :], back[1, rows, :]
            for b in range(2):
                columns = pl.ds(b * HALF, HALF)
                sign = 1.0 if b == 0 else -1.0
                b_re = even[:, :HALF] + sign * odd[:, :HALF]
                b_im = even[:, HALF:] + sign * odd[:, HALF:]
                p_re = probe_rows(0, mode, piece, columns)
                p_im = probe_rows(1, mode, piece, columns)
                w_re, w_im = windows[scan, 0, rows, columns], windows[scan, 1, rows, columns]
                o_re = p_re * b_re + p_im * b_im
                o_im = p_re * b_im - p_im * b_re
                zero = jnp.zeros_like(o_re)
                contrib[scan, 0, rows, columns] = o_re + jnp.where(
                    first_mode, zero, contrib[scan, 0, rows, columns]
                )
                contrib[scan, 1, rows, columns] = o_im + jnp.where(
                    first_mode, zero, contrib[scan, 1, rows, columns]
                )
                g_re = w_re * b_re + w_im * b_im
                g_im = w_re * b_im - w_im * b_re
                for slot in range(CHUNK // 8):
                    group = piece * (CHUNK // 8) + slot
                    inner = slice(slot * 8, slot * 8 + 8)
                    for part, value in enumerate((g_re, g_im)):
                        place = 2 * part + mode
                        old = sums[group, place, :, columns]
                        sums[group, place, :, columns] = value[inner] + jnp.where(
                            first_scan, jnp.zeros_like(old), old
                        )

        return carry

    for piece in range(SIDE // CHUNK):
        rows = pl.ds(piece * CHUNK, CHUNK)
        power = None
        for mode in range(2):
            for part in range(2):
                value = probe_rows(part, mode, piece)
                power = value * value if power is None else power + value * value
        power_out[rows, :] = power
        weight = None
        for scan in range(2):
            for part in range(2):
                value = windows[scan, part, rows, :]
                weight = value * value if weight is None else weight + value * value
        for slot in range(CHUNK // 8):
            sums[piece * (CHUNK // 8) + slot, 4] = weight[slot * 8 : slot * 8 + 8]

    lax.fori_loop(0, 4, backward, 0, unroll=4)

    def scatter(scan, carry):
        row, column = offsets_ref[0, 0, scan, 0] + HALF, offsets_ref[0, 0, scan, 1] + HALF
        inner = lax.rem(row, 8)
        base = pl.multiple_of(row - inner, 8)
        turn, keep = lax.rem(column, TILE), lane >= column
        zero = jnp.zeros((CHUNK // 8, 8, TILE), F32)
        edge = jnp.zeros((1, 8, TILE), F32)
        stay = lax.broadcasted_iota(jnp.int32, (CHUNK // 8 + 1, 8, TILE), 1) >= inner
        for channel in range(2):
            for piece in range(SIDE // CHUNK):
                halves = []
                for b in range(2):
                    value = contrib[scan, channel, pl.ds(piece * CHUNK, CHUNK), pl.ds(b * TILE, TILE)]
                    halves.append(pltpu.roll(value.reshape(CHUNK // 8, 8, TILE), turn, 2))
                thirds = (
                    jnp.where(keep, halves[0], zero),
                    jnp.where(keep, halves[1], halves[0]),
                    jnp.where(keep, zero, halves[1]),
                )
                place = pl.ds(base + piece * CHUNK, CHUNK + 8)
                for b in range(3):
                    value = pltpu.roll(thirds[b], inner, 1)
                    value = jnp.where(
                        stay,
                        jnp.concatenate([value, edge]),
                        jnp.concatenate([edge, value]),
                    )
                    total[channel, place, pl.ds(b * TILE, TILE)] += value.reshape(CHUNK + 8, TILE)
        return carry

    done = len(copies)
    start(sums.at[pl.ds(core * GROUPS, GROUPS)], mine_out)
    start(sums.at[pl.ds((1 - core) * GROUPS, GROUPS)], other_out)
    lax.fori_loop(0, 2, scatter, 0)
    for block, ref in enumerate((grad_second, grad_middle, grad_first)):
        for column in range(3):
            start(total.at[:, third(across[block]), third(along[column])], ref.at[column])
    for copy in copies[done:]:
        copy.wait()


def weigh_kernel(parity_ref, near_ref, power_ref, out_ref, padded):
    padded[...] = jnp.zeros_like(padded)
    padded[pl.ds(TILE, SIDE), pl.ds(TILE, SIDE)] = power_ref[...]
    lane = lax.broadcasted_iota(jnp.int32, (TILE // 8, 8, TILE), 2)
    sublane = lax.broadcasted_iota(jnp.int32, (TILE // 8, 8, TILE), 1)

    def add(index, total):
        place, scan = index // 2, index % 2
        across, along = place // 3, place % 3
        across = 1 + (across - 1) * (1 - 2 * parity_ref[0])
        along = 1 + (along - 1) * (1 - 2 * parity_ref[1])
        row, column = near_ref[place, 2 * scan], near_ref[place, 2 * scan + 1]
        column = jnp.where(row == 0, 0, 2 * TILE - along * TILE - (column - SHIFT))
        row = jnp.where(row == 0, WIDE, 2 * TILE - across * TILE - (row - SHIFT))
        inner = lax.rem(row, 8)
        base = pl.multiple_of(row - inner, 8)
        offset = lax.rem(column, TILE)
        block = pl.multiple_of(column - offset, TILE)
        turned = []
        for b in range(2):
            rows = padded[pl.ds(base, TILE + 8), pl.ds(block + b * TILE, TILE)]
            rows = pltpu.roll(rows.reshape(TILE // 8 + 1, 8, TILE), lax.rem(8 - inner, 8), 1)
            rows = jnp.where(sublane < 8 - inner, rows[:-1], rows[1:])
            turned.append(pltpu.roll(rows, lax.rem(TILE - offset, TILE), 2))
        return total + jnp.where(lane < TILE - offset, turned[0], turned[1])

    total = lax.fori_loop(0, 18, add, jnp.zeros((TILE // 8, 8, TILE), F32))
    out_ref[...] = total.reshape(TILE, TILE)


def spread_kernel(pieces_ref, out_ref):
    total = pieces_ref[0]
    for piece in range(1, GROUPS):
        total = total + pieces_ref[piece]
    for copy in range(DEPTH):
        out_ref[copy] = total


def update_kernel(pieces_ref, old_ref, out_ref, new_ref):
    total = pieces_ref[0]
    for piece in range(1, DEPTH):
        total = total + pieces_ref[piece]
    new = old_ref[...] + PROBE_STEP * total[:4] / (total[4:] + PROBE_REG)
    new_ref[...] = new
    for copy in range(GROUPS):
        out_ref[copy] = new


VMEM_SPEC = pl.BlockSpec(memory_space=pltpu.VMEM)
SMEM_SPEC = pl.BlockSpec(memory_space=pltpu.SMEM)
ANY_SPEC = pl.BlockSpec(memory_space=pl.ANY)


def in_hbm(value):
    return pltpu.with_memory_space_constraint(value, pltpu.HBM)


def params(mebibytes):
    return pltpu.CompilerParams(vmem_limit_bytes=mebibytes * 2**20)


def sort_measured(measured):
    return pl.pallas_call(
        sort_kernel,
        out_shape=jax.ShapeDtypeStruct((2, 2, HALF, SIDE), F32),
        in_specs=[VMEM_SPEC],
        out_specs=VMEM_SPEC,
        compiler_params=params(8),
        name="sort_measured",
    )(measured)


def step(offsets, parity, table, probe, measured, around):
    halves = len(probe) - 1
    band = jax.ShapeDtypeStruct((3, 2, TILE, TILE), F32)
    half = jax.ShapeDtypeStruct((GROUPS, 5, 8, SIDE), F32)
    return pl.pallas_call(
        functools.partial(step_kernel, halves),
        out_shape=[half, half, band, band, band, jax.ShapeDtypeStruct((SIDE, SIDE), F32)],
        in_specs=[SMEM_SPEC, SMEM_SPEC] + [ANY_SPEC] * (3 + halves + len(around)),
        out_specs=[ANY_SPEC] * 5 + [VMEM_SPEC],
        scratch_shapes=[
            pltpu.VMEM(table.shape, BF16),
            pltpu.VMEM((4, 2 * GROUPS, 8, SIDE), F32),
            pltpu.VMEM(measured.shape, F32),
            pltpu.VMEM((2, WIDE + 8, WIDE), F32),
            pltpu.VMEM((2, 2, SIDE, SIDE), F32),
            pltpu.VMEM((2, 2, SIDE, SIDE), BF16),
            pltpu.VMEM((2, 2, SIDE, SIDE), BF16),
            pltpu.VMEM((4, 2, SIDE, SIDE), F32),
            pltpu.VMEM((2, SIDE, SIDE), F32),
            pltpu.VMEM((2, 2, SIDE, SIDE), F32),
            pltpu.VMEM((2, WIDE + 8, WIDE), F32),
            pltpu.VMEM((2 * GROUPS, 5, 8, SIDE), F32),
            pltpu.SemaphoreType.DMA((32,)),
        ],
        compiler_params=params(20),
        name="step",
    )(offsets, parity, table, *probe, measured, *around)


def pairs(first):
    both = [(i, i + 1) for i in range(first, 15, 2)]
    return both + [(j, i) for i, j in both]


def neighbourhood(tile):
    outer, inner = lax.ppermute(tile, "col", pairs(1)), lax.ppermute(tile, "col", pairs(0))
    second, first = lax.ppermute(tile, "row", pairs(1)), lax.ppermute(tile, "row", pairs(0))
    return (
        lax.ppermute(outer, "row", pairs(1)),
        second,
        lax.ppermute(second, "col", pairs(0)),
        outer,
        tile,
        inner,
        lax.ppermute(outer, "row", pairs(0)),
        first,
        lax.ppermute(first, "col", pairs(0)),
    )


def band_neighbourhood(tile):
    outer, inner = lax.ppermute(tile, "col", pairs(1)), lax.ppermute(tile, "col", pairs(0))
    band = jnp.stack([outer, tile, inner])
    second, first = lax.ppermute(band, "row", pairs(1)), lax.ppermute(band, "row", pairs(0))
    return outer, tile, inner, second, first


def after(value, other):
    return lax.optimization_barrier((value, other))[0]


def places(device):
    row, column = divmod(device, 16)
    return (column // 8) * 4 + row // 4, row % 4, column // 2 % 4, column % 2


def grouped(key):
    groups = {}
    for device in range(256):
        groups.setdefault(key(*places(device)), []).append(device)
    return list(groups.values())


PLANES = grouped(lambda z, y, x, core: (z, core))
LINES = grouped(lambda z, y, x, core: (y, x, core))
BOTH = ("row", "col")
SWAP = [(i, i ^ 1) for i in range(16)]


def exchange(value, groups):
    return lax.all_to_all(value, BOTH, 0, 0, axis_index_groups=groups, tiled=True)


def weigh(parity, near, power):
    return pl.pallas_call(
        weigh_kernel,
        out_shape=jax.ShapeDtypeStruct((TILE, TILE), F32),
        in_specs=[SMEM_SPEC, SMEM_SPEC, VMEM_SPEC],
        out_specs=VMEM_SPEC,
        scratch_shapes=[pltpu.VMEM((4 * TILE + 8, 5 * TILE), F32)],
        compiler_params=params(8),
        name="weigh",
    )(parity, near, power)


def offsets_near(around):
    return jnp.stack([piece[0, TILE, :4] for piece in around]).astype(jnp.int32)


def spread(pieces):
    return pl.pallas_call(
        spread_kernel,
        out_shape=jax.ShapeDtypeStruct((DEPTH, 5, 8, SIDE), F32),
        compiler_params=params(8),
        name="spread",
    )(pieces)


def update(pieces, old):
    return pl.pallas_call(
        update_kernel,
        out_shape=[
            jax.ShapeDtypeStruct((GROUPS, 4, 8, SIDE), F32),
            jax.ShapeDtypeStruct((4, 8, SIDE), F32),
        ],
        compiler_params=params(8),
        name="update",
    )(pieces, old)


def local(object_field, probe, amplitudes, offsets):
    table = in_hbm(jnp.asarray(tables()))
    row, column = lax.axis_index("row"), lax.axis_index("col")
    core = column & 1
    group = core * GROUPS + (row & 3) * 4 + (lax.shift_right_logical(column, 1) & 3)
    probe = probe.reshape(4, 2 * GROUPS, 8, SIDE)
    old = lax.dynamic_index_in_dim(probe, group, 1, False)
    parity = jnp.stack([row & 1, core])
    measured = sort_measured(amplitudes[0, 0])
    parts = (in_hbm(probe),)
    tile = object_field
    marks = jnp.pad((offsets + SHIFT).astype(F32).reshape(1, 1, 4), ((0, 1), (0, 7), (0, TILE - 4)))
    around = neighbourhood(jnp.concatenate([tile, marks], axis=1))
    near = offsets_near(around)
    for iteration in range(ITERS):
        mine, other, second, middle, first, power = step(
            offsets, parity, table, parts, measured, around
        )
        mine = mine + lax.ppermute(other, "col", SWAP)
        first = lax.ppermute(after(first, mine), "row", pairs(0))
        second = lax.ppermute(after(second, mine), "row", pairs(1))
        weight = weigh(parity, near, after(power, mine))
        pieces = spread(after(exchange(mine, PLANES), weight))
        middle = after(middle, pieces)
        outer, own, inner = (middle[i] + first[i] + second[i] for i in range(3))
        folds = (outer, own, inner)
        inner = lax.ppermute(inner, "col", pairs(0))
        outer = lax.ppermute(outer, "col", pairs(1))
        pieces = after(exchange(pieces, LINES), folds)
        pieces, old = update(pieces, old)
        totals = after(own, old) + inner + outer
        tile = tile + OBJECT_STEP * totals / (weight + OBJECT_REG)
        if iteration + 1 < ITERS:
            around = band_neighbourhood(tile)
        mine = exchange(pieces, PLANES)
        if iteration + 1 == ITERS:
            mine = after(mine, (inner, outer))
        parts = (mine, lax.ppermute(mine, "col", SWAP))
    probe = pl.pallas_call(
        lay_out_kernel,
        out_shape=jax.ShapeDtypeStruct((4, 2 * GROUPS, 8, SIDE), F32),
        in_specs=[SMEM_SPEC, VMEM_SPEC, VMEM_SPEC],
        out_specs=VMEM_SPEC,
        compiler_params=params(8),
        name="lay_out",
    )(parity, *parts)
    return (tile, probe.reshape(2, 2, SIDE, SIDE))


def solution(mesh):
    return jax.shard_map(
        local,
        mesh=mesh,
        in_specs=(
            P(None, "row", "col"),
            P(),
            P("row", "col", None, None, None),
            P("row", "col", None, None),
        ),
        out_specs=(P(None, "row", "col"), P()),
        check_vma=False,
    )
```
